128 devices in a mesh: src: 8 (over y, z_lo), tgt: 16 (over x, z_hi, core).
Axes of the slice: x: 4, y: 4, z: 4 (z_hi: 2, z_lo: 2; z = z_hi * 2 + z_lo), core: 2. Of those that a mesh axis runs over, the one named last changes fastest.
Arguments:
- positions: float32 [3, 524288], P(None, ('src', 'tgt')), may hold values from -2.7 to 2.7
- velocities: float32 [3, 524288], P(None, ('src', 'tgt')), may hold values from -2.4 to 2.4
- accelerations: float32 [3, 524288], P(None, ('src', 'tgt')), may hold values from -6 to 6
- jerk_terms: float32 [3, 524288], P(None, ('src', 'tgt')), may hold values from -6 to 6
- masses: float32 [524288], P(('src', 'tgt')), may hold values from 5.722046e-07 to 5.722046e-06
- elapsed: float32 [524288], P(('src', 'tgt')), may hold values from 0.02 to 0.1
- active_idx: int32 [512], P(('src', 'tgt')), may hold values from 0 to 524287, as said below
- owners: int32 [512], P(('src', 'tgt')), may hold values from 0 to 7, as said below
- counts: int32 [512], P(('src', 'tgt')), may hold values from 1 to 16
- block_lists: int32 [512, 16], P(('src', 'tgt')), may hold values from 0 to 39, as said below
Outputs:
- new_states: float32 [6, 512], P(None, ('src', 'tgt'))
- fields: float32 [12, 512], P(None, ('src', 'tgt'))
- taylor: float32 [6, 512], P(None, ('src', 'tgt'))
The draws below stay inside these ranges and needn't reach their ends.
Inputs may be any that keep to these rules, and one draw needn't show every extreme that they name: Entry i is a star of owner block owners[i] of its own group: with t = (i // 4) mod 16, (owners[i] 16 + t) * 4096 <= active_idx[i] < (owners[i] 16 + t + 1) * 4096. Entries are distinct. `owners`: among the 4 entries of one device at most 2 name the same owner; in each group some owner is named 2 times by every device of the group. `block_lists`: each row holds 16 distinct numbers; only the first counts[i] of row i are read.
All inputs are finite; a program needn't handle non-finite values.
Results may differ from the reference program's by a relative error of at most 0.0003.
Values sent between devices are 32-bit elements; how exact they have to be, the bound alone decides.
A program may use at most 64 MiB of HBM per device.

```python
import math
import jax
import jax.numpy as jnp
from jax import lax

STAR_DEV = 4096
ACT_DEV = 4
BLOCK = 128
MAXB = 16
HALO_BLK = 4
SUBS = 2
OWNERS = 8
GROUPS = 16
STARS = 524288
ACTIVE = 512
CAP = 2
WIN = 40


def draw_positions(key, part):
    shard_id = jnp.arange(STARS, dtype=jnp.int32) // STAR_DEV
    owner_row = (shard_id // GROUPS).astype(jnp.float32)
    group_col = (shard_id % GROUPS).astype(jnp.float32)
    centre = jnp.stack([0.3 * (owner_row - (OWNERS - 1) / 2.0), 0.3 * (group_col - (GROUPS - 1) / 2.0), jnp.zeros_like(owner_row)], 0)
    reach = 0.15 * max(OWNERS, GROUPS) + 0.3
    key_core, key_wide, key_pick = jax.random.split(key, 3)
    spread = jnp.clip(0.05 * jax.random.normal(key_core, (3, STARS), jnp.float32), -0.3, 0.3)
    wide = jnp.clip(0.5 * reach * jax.random.normal(key_wide, (3, STARS), jnp.float32), -reach, reach)
    far_flag = jax.random.randint(key_pick, (STARS,), 0, 4) == 0
    spot = jnp.where(far_flag[None, :], wide, centre + spread)
    return jnp.clip(spot, -reach, reach)


def routing(key):
    base_key = jax.random.fold_in(key, 7)
    key_busy, key_order, key_other, key_place = jax.random.split(base_key, 4)
    shards = ACTIVE // ACT_DEV
    busy_owner = jax.random.randint(key_busy, (GROUPS,), 0, OWNERS)
    shard_id = jnp.arange(shards, dtype=jnp.int32)
    group_col = shard_id % GROUPS
    sender = shard_id // GROUPS
    slots = jnp.arange(ACT_DEV, dtype=jnp.int32)
    scores = jax.random.randint(key_order, (shards, ACT_DEV), 0, 1 << 20) * ACT_DEV + slots[None, :]
    ordering = jnp.argsort(scores, axis=1)
    slot_rank = jnp.argsort(ordering, axis=1)
    busy_here = busy_owner[group_col][:, None]
    other_owner = (busy_here + 1 + jax.random.randint(key_other, (shards, ACT_DEV), 0, OWNERS - 1)) % OWNERS
    home_owner = jnp.where(slot_rank < CAP, busy_here, other_owner)
    stride = STAR_DEV // (OWNERS * ACT_DEV)
    offset = (sender[:, None] * ACT_DEV + slots[None, :]) * stride + jax.random.randint(key_place, (shards, ACT_DEV), 0, stride)
    star_index = (home_owner * GROUPS + group_col[:, None]) * STAR_DEV + offset
    return (home_owner.reshape(-1).astype(jnp.int32), star_index.reshape(-1).astype(jnp.int32))


def draw_owners(key, part):
    home_owner, star_index = routing(key)
    return home_owner


def draw_active_idx(key, part):
    home_owner, star_index = routing(key)
    return star_index


def draw_counts(key, part):
    key_base, key_full = jax.random.split(jax.random.fold_in(key, 11))
    base_count = jax.random.randint(key_base, (ACTIVE,), 1, MAXB + 1)
    chosen = jax.random.randint(key_full, (ACTIVE // ACT_DEV,), 0, ACT_DEV)
    full_row = jnp.arange(ACTIVE, dtype=jnp.int32) % ACT_DEV == jnp.repeat(chosen, ACT_DEV)
    return jnp.where(full_row, MAXB, base_count).astype(jnp.int32)


def draw_block_lists(key, part):
    scores = jax.random.randint(jax.random.fold_in(key, 13), (ACTIVE, WIN), 0, 1 << 16) * WIN + jnp.arange(WIN, dtype=jnp.int32)[None, :]
    values, chosen = lax.top_k(scores, MAXB)
    return chosen.astype(jnp.int32)


def levels(key, dims, cuts, low, high):
    factor_of, own = 1.0, jax.random.fold_in(key, 6)
    for axis_at, parts in cuts:
        steps = jnp.exp(jax.random.uniform(jax.random.fold_in(own, axis_at), (parts,), jnp.float32, low / len(cuts), high / len(cuts)))
        factor_of = factor_of * jnp.repeat(steps, dims[axis_at] // parts).reshape([-1 if axis == axis_at else 1 for axis in range(len(dims))])
    return factor_of


def gaussian(rng, dims, scale, most, pieces=(), kind=jnp.bfloat16):
    array = scale * jax.random.normal(rng, dims, jnp.float32)
    if pieces:
        array = array * levels(rng, dims, pieces, -0.22, 0.18)
    return jnp.clip(array, -most, most).astype(kind)


def setup_inputs(seed: int = 0) -> dict:
    keys = jax.random.split(jax.random.key(seed), 11)
    positions = draw_positions(jax.random.fold_in(keys[10], 71), 0)
    velocities = gaussian(keys[1], (3, STARS), 0.3, 2.4, ((1, 128),), jnp.float32)
    accelerations = gaussian(keys[2], (3, STARS), 1.0, 6.0, ((1, 128),), jnp.float32)
    jerk_terms = gaussian(keys[3], (3, STARS), 1.0, 6.0, ((1, 128),), jnp.float32)
    masses = jnp.clip(jnp.exp(math.log(5.7220458984375e-06) - 2.3025851 * jax.random.uniform(keys[4], (STARS,), jnp.float32) ** levels(keys[4], (STARS,), ((0, 128),), -0.2, 0.2)), 5.722046125811175e-07, 5.7220458984375e-06)
    elapsed = jnp.clip(jnp.exp(math.log(0.1) - 1.609438 * jax.random.uniform(keys[5], (STARS,), jnp.float32) ** levels(keys[5], (STARS,), ((0, 128),), -0.2, 0.2)), 0.02, 0.1)
    active_idx = draw_active_idx(jax.random.fold_in(keys[10], 71), 0)
    owners = draw_owners(jax.random.fold_in(keys[10], 71), 0)
    counts = draw_counts(jax.random.fold_in(keys[10], 71), 0)
    block_lists = draw_block_lists(jax.random.fold_in(keys[10], 71), 0)
    return {"positions": positions, "velocities": velocities, "accelerations": accelerations, "jerk_terms": jerk_terms, "masses": masses, "elapsed": elapsed, "active_idx": active_idx, "owners": owners, "counts": counts, "block_lists": block_lists}


SOFTENING = 0.0001

def predict(position, velocity, acceleration, jerk_now, interval):
    new_position = position + interval * (velocity + interval * (0.5 * acceleration + interval * jerk_now / 6.0))
    new_velocity = velocity + interval * (acceleration + 0.5 * interval * jerk_now)
    return (new_position, new_velocity)

def pair_terms(targets, sources):
    offset = sources[0:3] - targets[0:3, :, None]
    relative = sources[3:6] - targets[3:6, :, None]
    distance = offset[0] * offset[0] + offset[1] * offset[1] + offset[2] * offset[2] + SOFTENING
    inverse = lax.rsqrt(distance)
    weight = sources[6] * inverse * inverse * inverse
    radial = 3.0 * (offset[0] * relative[0] + offset[1] * relative[1] + offset[2] * relative[2]) / distance
    pull_sum = lax.optimization_barrier(jnp.sum(weight * offset, axis=-1))
    change = lax.optimization_barrier(jnp.sum(weight * (relative - radial * offset), axis=-1))
    return jnp.concatenate([pull_sum, change], 0)

def correct(position, velocity, old_pull, old_change, new_pull, new_change, interval):
    jump = old_pull - new_pull
    snap_term = -6.0 * jump - interval * (4.0 * old_change + 2.0 * new_change)
    crackle = 12.0 * jump + 6.0 * interval * (old_change + new_change)
    new_position = position + interval * interval * (snap_term / 24.0 + crackle / 120.0)
    new_velocity = velocity + interval * (snap_term / 6.0 + crackle / 24.0)
    return (new_position, new_velocity, snap_term, crackle)

def neighbour_field(targets, nearby, usable, advance):
    moved_pos, moved_vel = predict(nearby[0:3], nearby[3:6], nearby[6:9], nearby[9:12], nearby[13] + advance[:, None])
    sources = jnp.concatenate([moved_pos, moved_vel, (nearby[12] * usable)[None]], 0)
    return pair_terms(targets, sources)

def home_steps(nearby, usable, own_state, totals):
    interval = own_state[13]
    start_pos, start_vel = predict(own_state[0:3], own_state[3:6], own_state[6:9], own_state[9:12], interval)
    inner_field = neighbour_field(jnp.concatenate([start_pos, start_vel], 0), nearby, usable, jnp.zeros_like(interval))
    regular = totals - inner_field
    position, velocity, snap_term, crackle = correct(start_pos, start_vel, own_state[6:9], own_state[9:12], totals[0:3], totals[3:6], interval)
    pull_now, change = (totals[0:3], totals[3:6])
    substep = 0.25 * interval
    for number in range(SUBS):
        advance = substep * (number + 1)
        guess_pos, guess_vel = predict(position, velocity, pull_now, change, substep)
        inner_field = neighbour_field(jnp.concatenate([guess_pos, guess_vel], 0), nearby, usable, advance)
        new_pull = regular[0:3] + advance * regular[3:6] + inner_field[0:3]
        new_change = regular[3:6] + inner_field[3:6]
        position, velocity, unused, ignored = correct(guess_pos, guess_vel, pull_now, change, new_pull, new_change, substep)
        pull_now, change = (new_pull, new_change)
    return jnp.concatenate([position, velocity, regular, inner_field, snap_term, crackle], 0)

def usable_mask(near_lists, near_counts, star_offset):
    lane_index = jnp.arange(BLOCK, dtype=jnp.int32)
    within = near_lists[:, :, None] * BLOCK + lane_index[None, None, :]
    listed = jnp.arange(near_lists.shape[1], dtype=jnp.int32)[None, :, None] < near_counts[:, None, None]
    itself = (star_offset + HALO_BLK * BLOCK)[:, None, None]
    return (listed & (within != itself)).reshape(near_lists.shape[0], -1).astype(jnp.float32)

def reference(positions, velocities, accelerations, jerk_terms, masses, elapsed, active_idx, owners, counts, block_lists):
    raw_state = jnp.concatenate([positions, velocities, accelerations, jerk_terms, masses[None], elapsed[None]], 0)
    pred_pos, pred_vel = predict(positions, velocities, accelerations, jerk_terms, elapsed)
    moving = jnp.concatenate([pred_pos, pred_vel], 0)
    sources = jnp.concatenate([moving, masses[None]], 0)[:, None, :]
    targets = jnp.take(moving, active_idx, axis=1)
    target_blocks = targets.reshape(6, ACTIVE // 4, 4).transpose(1, 0, 2)
    block_totals = lax.map(lambda target_block: pair_terms(target_block, sources), target_blocks)
    totals = block_totals.transpose(1, 0, 2).reshape(6, ACTIVE)
    margin = HALO_BLK * BLOCK
    star_grid = raw_state.reshape(14, OWNERS, GROUPS, STAR_DEV)
    zero_slab = jnp.zeros((14, 1, GROUPS, STAR_DEV), jnp.float32)
    padded = jnp.concatenate([zero_slab, star_grid, zero_slab], 1)
    windows = jnp.concatenate([padded[:, :-2, :, STAR_DEV - margin:], star_grid, padded[:, 2:, :, :margin]], 3)
    block_cells = windows.reshape(14, OWNERS * GROUPS * WIN, BLOCK)
    column = jnp.arange(ACTIVE, dtype=jnp.int32) // ACT_DEV % GROUPS
    window_base = (owners * GROUPS + column) * WIN
    block_picks = (window_base[:, None] + block_lists).reshape(-1)
    nearby = jnp.take(block_cells, block_picks, axis=1).reshape(14, ACTIVE, MAXB * BLOCK)
    usable = usable_mask(block_lists, counts, active_idx % STAR_DEV)
    own_state = jnp.take(raw_state, active_idx, axis=1)
    result = home_steps(nearby, usable, own_state, totals)
    return (result[0:6], result[6:18], result[18:24])
```

```python
import jax
import jax.numpy as jnp
from jax import lax
from jax.experimental import pallas as pl
from jax.experimental.pallas import tpu as pltpu
from jax.sharding import PartitionSpec as P

LANES = 128
ROWS = 8
BLOCK = 128
HALO = 4 * BLOCK
SUBS = 2
CAP = 2
ACT = 4
SRC = 8
TGT = 16
SOFTENING = 0.0001
MESH = pl.DeviceIdType.MESH
PAIRS = ((1, 0), (2, 0), (1, 1), (2, 1), (3, 1), (0, 1), (3, 0), (0, 0))
DX_TABLE = sum(dx * 4**at for at, (dx, dz) in enumerate(PAIRS))
DZ_TABLE = sum(dz * 2**at for at, (dx, dz) in enumerate(PAIRS))


def predict(position, velocity, acceleration, jerk_now, interval):
    new_position = [
        x + interval * (v + interval * (0.5 * a + interval * j / 6.0))
        for x, v, a, j in zip(position, velocity, acceleration, jerk_now)
    ]
    new_velocity = [
        v + interval * (a + 0.5 * interval * j)
        for v, a, j in zip(velocity, acceleration, jerk_now)
    ]
    return new_position, new_velocity


def correct(position, velocity, old_pull, old_change, new_pull, new_change, interval):
    new_position, new_velocity, snaps, crackles = [], [], [], []
    for x, v, a0, j0, a1, j1 in zip(
        position, velocity, old_pull, old_change, new_pull, new_change
    ):
        jump = a0 - a1
        snap = -6.0 * jump - interval * (4.0 * j0 + 2.0 * j1)
        crackle = 12.0 * jump + 6.0 * interval * (j0 + j1)
        new_position.append(x + interval * interval * (snap / 24.0 + crackle / 120.0))
        new_velocity.append(v + interval * (snap / 6.0 + crackle / 24.0))
        snaps.append(snap)
        crackles.append(crackle)
    return new_position, new_velocity, snaps, crackles


def pair_sums(sums, target, source, mass):
    u = [source[k] - target[k] for k in range(3)]
    e = [source[3 + k] - target[3 + k] for k in range(3)]
    distance = u[0] * u[0] + u[1] * u[1] + (u[2] * u[2] + SOFTENING)
    inverse = lax.rsqrt(distance)
    square = inverse * inverse
    weight = (mass * inverse) * square
    along = u[0] * e[0] + u[1] * e[1] + u[2] * e[2]
    radial = weight * (along * square)
    return (
        [sums[k] + weight * u[k] for k in range(3)]
        + [sums[3 + k] + weight * e[k] for k in range(3)]
        + [sums[6 + k] + radial * u[k] for k in range(3)]
    )


def total_of(sums):
    six = sums[0:3] + [sums[3 + k] - 3.0 * sums[6 + k] for k in range(3)]
    return [
        jnp.broadcast_to(jnp.sum(part, axis=1, keepdims=True), (ROWS, LANES)) for part in six
    ]


def lane_of(tile, lane):
    return jnp.broadcast_to(tile[:, lane : lane + 1], (ROWS, LANES))


def row_of(ref, row, block):
    lanes = pl.ds(pl.multiple_of(block * LANES, LANES), LANES)
    return jnp.broadcast_to(ref[row : row + 1, lanes], (ROWS, LANES))


def kernel(
    pos, vel, acc, jrk, mas, ela, idx, own, cnt, lists,
    o_state, o_fields, o_taylor,
    wpos, wvel, wacc, wjrk, wmas, wela, ppos, pvel, mw,
    s1b, s1r, s2b, s2r, s3b, s3r, s4b, s4r, s5b, s5r, s6b, s6r,
    load_sem, halo_send, halo_recv, src_send, src_recv, tgt_send, tgt_recv, sum_send, sum_recv,
):
    stars = pos.shape[1]
    blocks = stars // BLOCK
    window_blocks = wpos.shape[1] // BLOCK
    me = lax.axis_index("src")
    my_group = lax.axis_index("tgt")
    my_x, my_z, my_core = my_group // 4, (my_group // 2) % 2, my_group % 2

    def src_peer(step):
        return {"src": lax.rem(me + step, SRC)}

    def tgt_peer(dx, dz, dc):
        x, z, core = lax.rem(my_x + dx, 4), lax.rem(my_z + dz, 2), lax.rem(my_core + dc, 2)
        return {"tgt": x * 4 + z * 2 + core}

    def tile_rows(at):
        return pl.ds(pl.multiple_of(at * ROWS, ROWS), ROWS)

    lane = lax.broadcasted_iota(jnp.int32, (ROWS, LANES), 1)
    sub = lax.broadcasted_iota(jnp.int32, (ROWS, LANES), 0)
    zero = jnp.zeros((ROWS, LANES), jnp.float32)

    arrays = ((pos, wpos), (vel, wvel), (acc, wacc), (jrk, wjrk), (mas, wmas), (ela, wela))
    loads = [
        pltpu.make_async_copy(hbm, win.at[:, HALO : HALO + stars], load_sem.at[at])
        for at, (hbm, win) in enumerate(arrays)
    ]
    for load in loads:
        load.start()

    barrier = pltpu.get_barrier_semaphore()
    for step in range(1, SRC):
        pl.semaphore_signal(barrier, inc=1, device_id=src_peer(step), device_id_type=MESH)
    for at in range(1, TGT):
        pl.semaphore_signal(
            barrier,
            inc=1,
            device_id=tgt_peer(at // 4, (at // 2) % 2, at % 2),
            device_id_type=MESH,
        )

    tile = jnp.zeros((ROWS, LANES), jnp.int32)
    for place in range(ACT):
        for at, ref in enumerate((idx, own, cnt)):
            tile = jnp.where((sub == place) & (lane == 16 + at), ref[place], tile)
    s1b[...] = tile
    s1b[0:ACT, 0:16] = lists[...]

    pl.semaphore_wait(barrier, SRC + TGT - 2)

    def share(stage, sent, landed):
        copies = []
        for step in range(1, SRC):
            copies.append(
                pltpu.make_async_remote_copy(
                    src_ref=sent,
                    dst_ref=landed.at[tile_rows(me), :],
                    send_sem=src_send.at[stage, step],
                    recv_sem=src_recv.at[stage, step],
                    device_id=src_peer(step),
                    device_id_type=MESH,
                )
            )
        for copy in copies:
            copy.start()
        return copies

    first = share(0, s1b, s1r)
    s1r[tile_rows(me), :] = s1b[...]

    up = [
        pltpu.make_async_remote_copy(
            src_ref=hbm.at[:, stars - HALO : stars],
            dst_ref=win.at[:, 0:HALO],
            send_sem=halo_send.at[0, at],
            recv_sem=halo_recv.at[0, at],
            device_id={"src": lax.rem(me + 1, SRC)},
            device_id_type=MESH,
        )
        for at, (hbm, win) in enumerate(arrays)
    ]
    down = [
        pltpu.make_async_remote_copy(
            src_ref=hbm.at[:, 0:HALO],
            dst_ref=win.at[:, HALO + stars : 2 * HALO + stars],
            send_sem=halo_send.at[1, at],
            recv_sem=halo_recv.at[1, at],
            device_id={"src": lax.rem(me + SRC - 1, SRC)},
            device_id_type=MESH,
        )
        for at, (hbm, win) in enumerate(arrays)
    ]

    @pl.when(me < SRC - 1)
    def _():
        for copy in up:
            copy.start()

    @pl.when(me > 0)
    def _():
        for copy in down:
            copy.start()

    @pl.when(me == 0)
    def _():
        for hbm, win in arrays:
            win[:, 0:HALO] = jnp.zeros((win.shape[0], HALO), jnp.float32)

    @pl.when(me == SRC - 1)
    def _():
        for hbm, win in arrays:
            win[:, HALO + stars :] = jnp.zeros((win.shape[0], HALO), jnp.float32)

    for load in loads:
        load.wait()

    chunk = 4 * LANES

    def predict_chunk(at, carry):
        here = pl.ds(pl.multiple_of(at * chunk, LANES), chunk)
        there = pl.ds(pl.multiple_of(HALO + at * chunk, LANES), chunk)
        (moved,), (speed,) = predict(
            [wpos[:, there]], [wvel[:, there]], [wacc[:, there]], [wjrk[:, there]], wela[:, there]
        )
        ppos[:, here] = moved
        pvel[:, here] = speed
        return carry

    lax.fori_loop(0, stars // chunk, predict_chunk, 0)

    for copy in first:
        copy.wait_recv()

    numbers = [s1r[pl.ds(place, SRC, stride=ROWS), :] for place in range(ACT)]
    chosen = [[], []]
    before = jnp.zeros((ROWS, LANES), jnp.int32)
    for place in range(ACT):
        mine = lane_of(numbers[place], 17) == me
        for c in range(CAP):
            chosen[c].append(mine & (before == c))
        before = before + jnp.where(mine, 1, 0)

    def pick(c, values, empty):
        result = empty
        for place in range(ACT):
            result = jnp.where(chosen[c][place], values[place], result)
        return result

    izero = jnp.zeros((ROWS, LANES), jnp.int32)
    detail = [pick(c, numbers, izero) for c in range(CAP)]
    first_star = (me * TGT + my_group) * stars
    offset = [lane_of(detail[c], 16) - first_star for c in range(CAP)]
    count = [lane_of(detail[c], 18) for c in range(CAP)]

    def extract(refs, base):
        wide = sum(ref.shape[0] for ref in refs)

        def step(block, found):
            rows = [
                row_of(ref, row, block + base) for ref in refs for row in range(ref.shape[0])
            ]
            out = []
            for c in range(CAP):
                here = lane + block * BLOCK == offset[c]
                out.append([jnp.where(here, row, old) for row, old in zip(rows, found[c])])
            return out

        found = lax.fori_loop(0, blocks, step, [[zero] * wide for _ in range(CAP)], unroll=2)
        return [
            [
                jnp.broadcast_to(jnp.sum(part, axis=1, keepdims=True), (ROWS, LANES))
                for part in found[c]
            ]
            for c in range(CAP)
        ]

    start = extract((ppos, pvel), 0)

    def spread(values, width):
        slots = []
        for c in range(CAP):
            slot = zero
            for k, value in enumerate(values[c]):
                slot = jnp.where(lax.rem(lane, width) == k, value, slot)
            slots.append(slot)
        result = zero
        for place in range(ACT):
            there = lane // width == place
            for c in range(CAP):
                result = jnp.where(there & chosen[c][place], slots[c], result)
        return result

    s2b[...] = spread(start, 8)
    second = share(1, s2b, s2r)
    s2r[tile_rows(me), :] = s2b[...]

    raw = extract((wpos, wvel, wacc, wjrk, wela), HALO // BLOCK)

    def mask_block(block, carry):
        mass = row_of(wmas, 0, block)
        for c in range(CAP):
            listed = jnp.where((detail[c] == block) & (lane < count[c]), 1.0, 0.0)
            member = jnp.broadcast_to(jnp.sum(listed, axis=1, keepdims=True), (ROWS, LANES))
            itself = lane + block * BLOCK == offset[c] + HALO
            mw[block, c] = jnp.where(itself, 0.0, member * mass)
        return carry

    @pl.when(me > 0)
    def _():
        for copy in up:
            copy.wait_recv()

    @pl.when(me < SRC - 1)
    def _():
        for copy in down:
            copy.wait_recv()

    lax.fori_loop(0, window_blocks, mask_block, 0, unroll=4)

    for copy in second:
        copy.wait_recv()

    def gathered(ref):
        total = ref[0:ROWS, :]
        for at in range(1, SRC):
            total = total + ref[at * ROWS : (at + 1) * ROWS, :]
        return total

    group_targets = gathered(s2r)
    s3b[...] = group_targets
    s3r[0] = group_targets
    third = []
    for dx, dz in PAIRS:
        for dc in (1, 0):
            if (dx, dz, dc) == (0, 0, 0):
                continue
            there = ((4 - dx) % 4) * 4 + dz * 2 + dc
            third.append(
                pltpu.make_async_remote_copy(
                    src_ref=s3b,
                    dst_ref=s3r.at[there],
                    send_sem=tgt_send.at[there],
                    recv_sem=tgt_recv.at[there],
                    device_id=tgt_peer(dx, dz, dc),
                    device_id_type=MESH,
                )
            )
    for copy in third:
        copy.start()

    def near_field(targets, advance):
        def step(block, sums):
            x = [row_of(wpos, k, block) for k in range(3)]
            v = [row_of(wvel, k, block) for k in range(3)]
            a = [row_of(wacc, k, block) for k in range(3)]
            j = [row_of(wjrk, k, block) for k in range(3)]
            since = row_of(wela, 0, block)
            out = []
            for c in range(CAP):
                moved, speed = predict(x, v, a, j, since + advance[c])
                out.append(pair_sums(sums[c], targets[c], moved + speed, mw[block, c]))
            return out

        sums = lax.fori_loop(0, window_blocks, step, [[zero] * 9 for _ in range(CAP)], unroll=2)
        return [total_of(sums[c]) for c in range(CAP)]

    inner = near_field(start, [zero] * CAP)

    def field(targets):
        result = zero
        for half in range(2):
            places = (2 * half, 2 * half + 1)
            aims = [[lane_of(targets, place * 8 + k) for k in range(6)] for place in places]

            def step(block, sums):
                source = [row_of(ppos, k, block) for k in range(3)]
                source += [row_of(pvel, k, block) for k in range(3)]
                mass = row_of(wmas, 0, block + HALO // BLOCK)
                return [pair_sums(sums[at], aims[at], source, mass) for at in range(2)]

            sums = lax.fori_loop(0, blocks, step, [[zero] * 9 for _ in range(2)], unroll=2)
            for at, place in enumerate(places):
                for k, value in enumerate(total_of(sums[at])):
                    result = jnp.where(lane == place * 8 + k, value, result)
        return result

    def sum_copy(at, dx, dz, dc):
        there = lax.rem(4 - dx, 4) * 4 + dz * 2 + dc
        return pltpu.make_async_remote_copy(
            src_ref=s4b.at[at],
            dst_ref=s4r.at[there],
            send_sem=sum_send.at[at],
            recv_sem=sum_recv.at[there],
            device_id=tgt_peer(dx, dz, dc),
            device_id_type=MESH,
        )

    def group_pair(pair, tables):
        dx, dz = lax.rem(tables[0], 4), lax.rem(tables[1], 2)
        for dc in (1, 0):
            at = dx * 4 + dz * 2 + dc

            def wait():
                pltpu.make_async_remote_copy(
                    src_ref=s3b,
                    dst_ref=s3r.at[at],
                    send_sem=tgt_send.at[at],
                    recv_sem=tgt_recv.at[at],
                    device_id=tgt_peer(dx, dz, dc),
                    device_id_type=MESH,
                ).wait_recv()

            if dc:
                wait()
            else:
                pl.when(pair < len(PAIRS) - 1)(wait)
            result = field(s3r[at])

            def send():
                s4b[at] = result
                sum_copy(at, dx, dz, dc).start()

            if dc:
                send()
            else:
                pl.when(pair < len(PAIRS) - 1)(send)

                @pl.when(pair == len(PAIRS) - 1)
                def _():
                    s4r[0] = result

        return tables[0] // 4, tables[1] // 2

    lax.fori_loop(0, len(PAIRS), group_pair, (jnp.int32(DX_TABLE), jnp.int32(DZ_TABLE)))

    for at in range(1, TGT):
        sum_copy(at, at // 4, (at // 2) % 2, at % 2).wait_send()
        pltpu.make_async_remote_copy(
            src_ref=s4b.at[at],
            dst_ref=s4r.at[at],
            send_sem=sum_send.at[at],
            recv_sem=sum_recv.at[at],
            device_id=tgt_peer(at // 4, (at // 2) % 2, at % 2),
            device_id_type=MESH,
        ).wait_recv()
    group_sum = s4r[0]
    for at in range(1, TGT):
        group_sum = group_sum + s4r[at]

    s5b[...] = group_sum
    fifth = share(2, s5b, s5r)
    s5r[tile_rows(me), :] = group_sum
    for copy in fifth:
        copy.wait_recv()
    summed = gathered(s5r)
    lanes_of = [[lane_of(summed, place * 8 + k) for place in range(ACT)] for k in range(6)]

    totals = [[pick(c, lanes_of[k], zero) for k in range(6)] for c in range(CAP)]
    states = []
    for c in range(CAP):
        interval = raw[c][12]
        old_pull, old_change = raw[c][6:9], raw[c][9:12]
        regular = [totals[c][k] - inner[c][k] for k in range(6)]
        x, v, snap, crackle = correct(
            start[c][0:3],
            start[c][3:6],
            old_pull,
            old_change,
            totals[c][0:3],
            totals[c][3:6],
            interval,
        )
        states.append((x, v, totals[c][0:3], totals[c][3:6], 0.25 * interval, regular, snap + crackle))
    for number in range(SUBS):
        advance = [states[c][4] * (number + 1) for c in range(CAP)]
        guesses = [predict(*states[c][0:5]) for c in range(CAP)]
        inner = near_field([x + v for x, v in guesses], advance)
        after = []
        for c in range(CAP):
            x, v, pull, change, substep, regular, rest = states[c]
            new_pull = [
                regular[k] + advance[c] * regular[3 + k] + inner[c][k] for k in range(3)
            ]
            new_change = [regular[3 + k] + inner[c][3 + k] for k in range(3)]
            x, v, unused, ignored = correct(
                guesses[c][0], guesses[c][1], pull, change, new_pull, new_change, substep
            )
            after.append((x, v, new_pull, new_change, substep, regular, rest))
        states = after

    results = [
        states[c][0] + states[c][1] + states[c][5] + inner[c] + states[c][6] for c in range(CAP)
    ]
    s6b[...] = spread(results, 32)
    sixth = share(3, s6b, s6r)
    s6r[tile_rows(me), :] = s6b[...]
    for copy in sixth:
        copy.wait_recv()
    mine = jnp.sum(s6r[pl.ds(me, SRC, stride=ROWS), :], axis=0, keepdims=True)
    mine = jnp.broadcast_to(mine, (ROWS, LANES))
    shifted = mine
    for place in range(1, ACT):
        shifted = jnp.where(sub == place, pltpu.roll(mine, LANES - 32 * place, 1), shifted)
    columns = jnp.transpose(shifted)
    o_state[...] = columns[0:6, 0:ACT]
    o_fields[...] = columns[6:18, 0:ACT]
    o_taylor[...] = columns[18:24, 0:ACT]

    for copy in first + second + third + fifth + sixth:
        copy.wait_send()

    @pl.when(me < SRC - 1)
    def _():
        for copy in up:
            copy.wait_send()

    @pl.when(me > 0)
    def _():
        for copy in down:
            copy.wait_send()


def shards(
    positions,
    velocities,
    accelerations,
    jerk_terms,
    masses,
    elapsed,
    active_idx,
    owners,
    counts,
    block_lists,
):
    stars = positions.shape[1]
    window = stars + 2 * HALO
    hbm = pl.BlockSpec(memory_space=pl.ANY)
    smem = pl.BlockSpec(memory_space=pltpu.SMEM)
    vmem = pl.BlockSpec(memory_space=pltpu.VMEM)
    tile = pltpu.VMEM((ROWS, LANES), jnp.float32)
    landed = pltpu.VMEM((SRC * ROWS, LANES), jnp.float32)
    groups = pltpu.VMEM((TGT, ROWS, LANES), jnp.float32)
    itile = pltpu.VMEM((ROWS, LANES), jnp.int32)
    ilanded = pltpu.VMEM((SRC * ROWS, LANES), jnp.int32)
    three = pltpu.VMEM((3, window), jnp.float32)
    one = pltpu.VMEM((1, window), jnp.float32)
    predicted = pltpu.VMEM((3, stars), jnp.float32)
    dma = pltpu.SemaphoreType.DMA
    return pl.pallas_call(
        kernel,
        out_shape=(
            jax.ShapeDtypeStruct((6, ACT), jnp.float32),
            jax.ShapeDtypeStruct((12, ACT), jnp.float32),
            jax.ShapeDtypeStruct((6, ACT), jnp.float32),
        ),
        in_specs=[hbm] * 6 + [smem] * 3 + [vmem],
        out_specs=(vmem, vmem, vmem),
        scratch_shapes=[
            three, three, three, three, one, one, predicted, predicted,
            pltpu.VMEM((window // BLOCK, CAP, ROWS, LANES), jnp.float32),
            itile, ilanded, tile, landed, tile, groups, groups, groups, tile, landed, tile, landed,
            dma((6,)), dma((2, 6)), dma((2, 6)), dma((4, SRC)), dma((4, SRC)),
            dma((TGT,)), dma((TGT,)), dma((TGT,)), dma((TGT,)),
        ],
        compiler_params=pltpu.CompilerParams(collective_id=0, has_side_effects=True),
    )(
        positions,
        velocities,
        accelerations,
        jerk_terms,
        masses[None],
        elapsed[None],
        active_idx,
        owners,
        counts,
        block_lists,
    )


def solution(mesh):
    in_specs = (
        P(None, ("src", "tgt")),
        P(None, ("src", "tgt")),
        P(None, ("src", "tgt")),
        P(None, ("src", "tgt")),
        P(("src", "tgt")),
        P(("src", "tgt")),
        P(("src", "tgt")),
        P(("src", "tgt")),
        P(("src", "tgt")),
        P(("src", "tgt"), None),
    )
    out_specs = (P(None, ("src", "tgt")), P(None, ("src", "tgt")), P(None, ("src", "tgt")))
    return jax.shard_map(shards, mesh=mesh, in_specs=in_specs, out_specs=out_specs, check_vma=False)
```

```python
import jax
import jax.numpy as jnp
from jax import lax
from jax.experimental import pallas as pl
from jax.experimental.pallas import tpu as pltpu
from jax.sharding import PartitionSpec as P

LANES = 128
ROWS = 8
BLOCK = 128
HALO = 4 * BLOCK
SUBS = 2
CAP = 2
ACT = 4
SRC = 8
TGT = 16
SOFTENING = 0.0001
MESH = pl.DeviceIdType.MESH
PAIRS = ((1, 0), (2, 0), (1, 1), (2, 1), (3, 1), (0, 1), (3, 0), (0, 0))
DX_TABLE = sum(dx * 4**at for at, (dx, dz) in enumerate(PAIRS))
DZ_TABLE = sum(dz * 2**at for at, (dx, dz) in enumerate(PAIRS))


def predict(position, velocity, acceleration, jerk_now, interval):
    new_position = [
        x + interval * (v + interval * (0.5 * a + interval * j / 6.0))
        for x, v, a, j in zip(position, velocity, acceleration, jerk_now)
    ]
    new_velocity = [
        v + interval * (a + 0.5 * interval * j)
        for v, a, j in zip(velocity, acceleration, jerk_now)
    ]
    return new_position, new_velocity


def correct(position, velocity, old_pull, old_change, new_pull, new_change, interval):
    new_position, new_velocity, snaps, crackles = [], [], [], []
    for x, v, a0, j0, a1, j1 in zip(
        position, velocity, old_pull, old_change, new_pull, new_change
    ):
        jump = a0 - a1
        snap = -6.0 * jump - interval * (4.0 * j0 + 2.0 * j1)
        crackle = 12.0 * jump + 6.0 * interval * (j0 + j1)
        new_position.append(x + interval * interval * (snap / 24.0 + crackle / 120.0))
        new_velocity.append(v + interval * (snap / 6.0 + crackle / 24.0))
        snaps.append(snap)
        crackles.append(crackle)
    return new_position, new_velocity, snaps, crackles


def pair_sums(sums, target, source, mass):
    u = [source[k] - target[k] for k in range(3)]
    e = [source[3 + k] - target[3 + k] for k in range(3)]
    distance = u[0] * u[0] + u[1] * u[1] + (u[2] * u[2] + SOFTENING)
    inverse = lax.rsqrt(distance)
    square = inverse * inverse
    weight = (mass * inverse) * square
    radial = (u[0] * e[0] + u[1] * e[1] + u[2] * e[2]) * square
    pull = [weight * u[k] for k in range(3)]
    return (
        [sums[k] + pull[k] for k in range(3)]
        + [sums[3 + k] + weight * e[k] for k in range(3)]
        + [sums[6 + k] + radial * pull[k] for k in range(3)]
    )


def total_of(sums):
    six = sums[0:3] + [sums[3 + k] - 3.0 * sums[6 + k] for k in range(3)]
    return [
        jnp.broadcast_to(jnp.sum(part, axis=1, keepdims=True), (ROWS, LANES)) for part in six
    ]


def lane_of(tile, lane):
    return jnp.broadcast_to(tile[:, lane : lane + 1], (ROWS, LANES))


def row_of(ref, row, block):
    lanes = pl.ds(pl.multiple_of(block * LANES, LANES), LANES)
    return jnp.broadcast_to(ref[row : row + 1, lanes], (ROWS, LANES))


def kernel(
    pos, vel, acc, jrk, mas, ela, idx, own, cnt, lists,
    o_all,
    wpos, wvel, wacc, wjrk, wmas, wela, ppos, pvel, mw, moved,
    s1b, s1r, s2b, s2r, s3b, s3r, s4b, s4r, s5b, s5r, s6b, s6r,
    load_sem, halo_send, halo_recv, src_send, src_recv, tgt_send, tgt_recv, sum_send, sum_recv,
):
    stars = pos.shape[1]
    blocks = stars // BLOCK
    window_blocks = wpos.shape[1] // BLOCK
    me = lax.axis_index("src")
    my_group = lax.axis_index("tgt")
    my_x, my_z, my_core = my_group // 4, (my_group // 2) % 2, my_group % 2

    def src_peer(step):
        return {"src": lax.rem(me + step, SRC)}

    def tgt_peer(dx, dz, dc):
        x, z, core = lax.rem(my_x + dx, 4), lax.rem(my_z + dz, 2), lax.rem(my_core + dc, 2)
        return {"tgt": x * 4 + z * 2 + core}

    def tile_rows(at):
        return pl.ds(pl.multiple_of(at * ROWS, ROWS), ROWS)

    lane = lax.broadcasted_iota(jnp.int32, (ROWS, LANES), 1)
    sub = lax.broadcasted_iota(jnp.int32, (ROWS, LANES), 0)
    zero = jnp.zeros((ROWS, LANES), jnp.float32)

    arrays = ((pos, wpos), (vel, wvel), (acc, wacc), (jrk, wjrk), (mas, wmas), (ela, wela))
    loads = [
        pltpu.make_async_copy(hbm, win.at[:, HALO : HALO + stars], load_sem.at[at])
        for at, (hbm, win) in enumerate(arrays)
    ]
    for load in loads:
        load.start()

    barrier = pltpu.get_barrier_semaphore()
    for step in range(1, SRC):
        pl.semaphore_signal(barrier, inc=1, device_id=src_peer(step), device_id_type=MESH)
    for at in range(1, TGT):
        pl.semaphore_signal(
            barrier,
            inc=1,
            device_id=tgt_peer(at // 4, (at // 2) % 2, at % 2),
            device_id_type=MESH,
        )

    tile = jnp.zeros((ROWS, LANES), jnp.int32)
    for place in range(ACT):
        for at, ref in enumerate((idx, own, cnt)):
            tile = jnp.where((sub == place) & (lane == 16 + at), ref[place], tile)
    s1b[...] = tile
    s1b[0:ACT, 0:16] = lists[...]

    pl.semaphore_wait(barrier, SRC + TGT - 2)

    def share(stage, sent, landed):
        copies = []
        for step in range(1, SRC):
            copies.append(
                pltpu.make_async_remote_copy(
                    src_ref=sent,
                    dst_ref=landed.at[tile_rows(me), :],
                    send_sem=src_send.at[stage, step],
                    recv_sem=src_recv.at[stage, step],
                    device_id=src_peer(step),
                    device_id_type=MESH,
                )
            )
        for copy in copies:
            copy.start()
        return copies

    first = share(0, s1b, s1r)
    s1r[tile_rows(me), :] = s1b[...]

    up = [
        pltpu.make_async_remote_copy(
            src_ref=hbm.at[:, stars - HALO : stars],
            dst_ref=win.at[:, 0:HALO],
            send_sem=halo_send.at[0, at],
            recv_sem=halo_recv.at[0, at],
            device_id={"src": lax.rem(me + 1, SRC)},
            device_id_type=MESH,
        )
        for at, (hbm, win) in enumerate(arrays)
    ]
    down = [
        pltpu.make_async_remote_copy(
            src_ref=hbm.at[:, 0:HALO],
            dst_ref=win.at[:, HALO + stars : 2 * HALO + stars],
            send_sem=halo_send.at[1, at],
            recv_sem=halo_recv.at[1, at],
            device_id={"src": lax.rem(me + SRC - 1, SRC)},
            device_id_type=MESH,
        )
        for at, (hbm, win) in enumerate(arrays)
    ]

    @pl.when(me < SRC - 1)
    def _():
        for copy in up:
            copy.start()

    @pl.when(me > 0)
    def _():
        for copy in down:
            copy.start()

    @pl.when(me == 0)
    def _():
        for hbm, win in arrays:
            win[:, 0:HALO] = jnp.zeros((win.shape[0], HALO), jnp.float32)

    @pl.when(me == SRC - 1)
    def _():
        for hbm, win in arrays:
            win[:, HALO + stars :] = jnp.zeros((win.shape[0], HALO), jnp.float32)

    for load in loads:
        load.wait()

    chunk = 4 * LANES

    def predict_chunk(at, carry):
        there = pl.ds(pl.multiple_of(at * chunk, LANES), chunk)
        (place,), (speed,) = predict(
            [wpos[:, there]], [wvel[:, there]], [wacc[:, there]], [wjrk[:, there]], wela[:, there]
        )
        ppos[:, there] = place
        pvel[:, there] = speed
        return carry

    lax.fori_loop(1, 1 + stars // chunk, predict_chunk, 0)

    for copy in first:
        copy.wait_recv()

    numbers = [s1r[pl.ds(place, SRC, stride=ROWS), :] for place in range(ACT)]
    chosen = [[], []]
    before = jnp.zeros((ROWS, LANES), jnp.int32)
    for place in range(ACT):
        mine = lane_of(numbers[place], 17) == me
        for c in range(CAP):
            chosen[c].append(mine & (before == c))
        before = before + jnp.where(mine, 1, 0)

    def pick(c, values, empty):
        result = empty
        for place in range(ACT):
            result = jnp.where(chosen[c][place], values[place], result)
        return result

    izero = jnp.zeros((ROWS, LANES), jnp.int32)
    detail = [pick(c, numbers, izero) for c in range(CAP)]
    first_star = (me * TGT + my_group) * stars
    offset = [lane_of(detail[c], 16) - first_star for c in range(CAP)]
    count = [lane_of(detail[c], 18) for c in range(CAP)]

    def extract(refs):
        wide = sum(ref.shape[0] for ref in refs)

        def step(block, found):
            rows = [
                row_of(ref, row, block + HALO // BLOCK) for ref in refs for row in range(ref.shape[0])
            ]
            out = []
            for c in range(CAP):
                here = lane + block * BLOCK == offset[c]
                out.append([jnp.where(here, row, old) for row, old in zip(rows, found[c])])
            return out

        found = lax.fori_loop(0, blocks, step, [[zero] * wide for _ in range(CAP)], unroll=2)
        return [
            [
                jnp.broadcast_to(jnp.sum(part, axis=1, keepdims=True), (ROWS, LANES))
                for part in found[c]
            ]
            for c in range(CAP)
        ]

    start = extract((ppos, pvel))

    def spread(values, width):
        slots = []
        for c in range(CAP):
            slot = zero
            for k, value in enumerate(values[c]):
                slot = jnp.where(lax.rem(lane, width) == k, value, slot)
            slots.append(slot)
        result = zero
        for place in range(ACT):
            there = lane // width == place
            for c in range(CAP):
                result = jnp.where(there & chosen[c][place], slots[c], result)
        return result

    s2b[...] = spread(start, 8)
    second = share(1, s2b, s2r)
    s2r[tile_rows(me), :] = s2b[...]

    raw = extract((wpos, wvel, wacc, wjrk, wela))

    def mask_block(block, carry):
        mass = row_of(wmas, 0, block)
        for c in range(CAP):
            listed = jnp.where((detail[c] == block) & (lane < count[c]), 1.0, 0.0)
            member = jnp.broadcast_to(jnp.sum(listed, axis=1, keepdims=True), (ROWS, LANES))
            itself = lane + block * BLOCK == offset[c] + HALO
            mw[block, c] = jnp.where(itself, 0.0, member * mass)
        return carry

    @pl.when(me > 0)
    def _():
        for copy in up:
            copy.wait_recv()

    @pl.when(me < SRC - 1)
    def _():
        for copy in down:
            copy.wait_recv()

    lax.fori_loop(0, window_blocks, mask_block, 0, unroll=4)

    for copy in second:
        copy.wait_recv()

    def gathered(ref):
        total = ref[0:ROWS, :]
        for at in range(1, SRC):
            total = total + ref[at * ROWS : (at + 1) * ROWS, :]
        return total

    group_targets = gathered(s2r)
    s3b[...] = group_targets
    s3r[0] = group_targets
    third = []
    for dx, dz in PAIRS:
        for dc in (1, 0):
            if (dx, dz, dc) == (0, 0, 0):
                continue
            there = ((4 - dx) % 4) * 4 + dz * 2 + dc
            third.append(
                pltpu.make_async_remote_copy(
                    src_ref=s3b,
                    dst_ref=s3r.at[there],
                    send_sem=tgt_send.at[there],
                    recv_sem=tgt_recv.at[there],
                    device_id=tgt_peer(dx, dz, dc),
                    device_id_type=MESH,
                )
            )
    for copy in third:
        copy.start()

    def advance_block(block, carry):
        x = [row_of(wpos, k, block) for k in range(3)]
        v = [row_of(wvel, k, block) for k in range(3)]
        a = [row_of(wacc, k, block) for k in range(3)]
        half = [0.5 * row for row in a]
        j = [row_of(wjrk, k, block) for k in range(3)]
        sixth_j = [row / 6.0 for row in j]
        half_j = [0.5 * row for row in j]
        since = row_of(wela, 0, block)
        for number in range(SUBS):
            for c in range(CAP):
                d = since + (0.25 * (number + 1)) * raw[c][12]
                for k in range(3):
                    moved[number, block, c, k] = x[k] + d * (
                        v[k] + d * (half[k] + d * sixth_j[k])
                    )
                    moved[number, block, c, 3 + k] = v[k] + d * (a[k] + d * half_j[k])
        return carry

    lax.fori_loop(0, window_blocks, advance_block, 0)

    def near_field(targets, number):
        def step(block, sums):
            if number is None:
                source = [row_of(ref, k, block) for ref in (ppos, pvel) for k in range(3)]
                sources = [source] * CAP
            else:
                sources = [[moved[number, block, c, k] for k in range(6)] for c in range(CAP)]
            return [pair_sums(sums[c], targets[c], sources[c], mw[block, c]) for c in range(CAP)]

        sums = lax.fori_loop(0, window_blocks, step, [[zero] * 9 for _ in range(CAP)], unroll=8)
        return [total_of(sums[c]) for c in range(CAP)]

    predict_chunk(0, 0)
    predict_chunk(window_blocks * LANES // chunk - 1, 0)
    inner = near_field(start, None)

    def field(targets):
        result = zero
        for half in range(2):
            places = (2 * half, 2 * half + 1)
            aims = [[lane_of(targets, place * 8 + k) for k in range(6)] for place in places]

            def step(block, sums):
                source = [row_of(ppos, k, block) for k in range(3)]
                source += [row_of(pvel, k, block) for k in range(3)]
                mass = row_of(wmas, 0, block)
                return [pair_sums(sums[at], aims[at], source, mass) for at in range(2)]

            sums = lax.fori_loop(
                HALO // BLOCK,
                HALO // BLOCK + blocks,
                step,
                [[zero] * 9 for _ in range(2)],
                unroll=8,
            )
            for at, place in enumerate(places):
                for k, value in enumerate(total_of(sums[at])):
                    result = jnp.where(lane == place * 8 + k, value, result)
        return result

    def sum_copy(at, dx, dz, dc):
        there = lax.rem(4 - dx, 4) * 4 + dz * 2 + dc
        return pltpu.make_async_remote_copy(
            src_ref=s4b.at[at],
            dst_ref=s4r.at[there],
            send_sem=sum_send.at[at],
            recv_sem=sum_recv.at[there],
            device_id=tgt_peer(dx, dz, dc),
            device_id_type=MESH,
        )

    def group_pair(pair, tables):
        dx, dz = lax.rem(tables[0], 4), lax.rem(tables[1], 2)
        for dc in (1, 0):
            at = dx * 4 + dz * 2 + dc

            def wait():
                pltpu.make_async_remote_copy(
                    src_ref=s3b,
                    dst_ref=s3r.at[at],
                    send_sem=tgt_send.at[at],
                    recv_sem=tgt_recv.at[at],
                    device_id=tgt_peer(dx, dz, dc),
                    device_id_type=MESH,
                ).wait_recv()

            if dc:
                wait()
            else:
                pl.when(pair < len(PAIRS) - 1)(wait)
            result = field(s3r[at])

            def send():
                s4b[at] = result
                sum_copy(at, dx, dz, dc).start()

            if dc:
                send()
            else:
                pl.when(pair < len(PAIRS) - 1)(send)

                @pl.when(pair == len(PAIRS) - 1)
                def _():
                    s4r[0] = result

        return tables[0] // 4, tables[1] // 2

    lax.fori_loop(0, len(PAIRS), group_pair, (jnp.int32(DX_TABLE), jnp.int32(DZ_TABLE)))

    for at in range(1, TGT):
        sum_copy(at, at // 4, (at // 2) % 2, at % 2).wait_send()
        pltpu.make_async_remote_copy(
            src_ref=s4b.at[at],
            dst_ref=s4r.at[at],
            send_sem=sum_send.at[at],
            recv_sem=sum_recv.at[at],
            device_id=tgt_peer(at // 4, (at // 2) % 2, at % 2),
            device_id_type=MESH,
        ).wait_recv()
    group_sum = s4r[0]
    for at in range(1, TGT):
        group_sum = group_sum + s4r[at]

    s5b[...] = group_sum
    fifth = share(2, s5b, s5r)
    s5r[tile_rows(me), :] = group_sum
    for copy in fifth:
        copy.wait_recv()
    summed = gathered(s5r)
    lanes_of = [[lane_of(summed, place * 8 + k) for place in range(ACT)] for k in range(6)]

    totals = [[pick(c, lanes_of[k], zero) for k in range(6)] for c in range(CAP)]
    states = []
    for c in range(CAP):
        interval = raw[c][12]
        old_pull, old_change = raw[c][6:9], raw[c][9:12]
        regular = [totals[c][k] - inner[c][k] for k in range(6)]
        x, v, snap, crackle = correct(
            start[c][0:3],
            start[c][3:6],
            old_pull,
            old_change,
            totals[c][0:3],
            totals[c][3:6],
            interval,
        )
        states.append((x, v, totals[c][0:3], totals[c][3:6], 0.25 * interval, regular, snap + crackle))
    for number in range(SUBS):
        advance = [states[c][4] * (number + 1) for c in range(CAP)]
        guesses = [predict(*states[c][0:5]) for c in range(CAP)]
        inner = near_field([x + v for x, v in guesses], number)
        after = []
        for c in range(CAP):
            x, v, pull, change, substep, regular, rest = states[c]
            new_pull = [
                regular[k] + advance[c] * regular[3 + k] + inner[c][k] for k in range(3)
            ]
            new_change = [regular[3 + k] + inner[c][3 + k] for k in range(3)]
            x, v, unused, ignored = correct(
                guesses[c][0], guesses[c][1], pull, change, new_pull, new_change, substep
            )
            after.append((x, v, new_pull, new_change, substep, regular, rest))
        states = after

    results = [
        states[c][0] + states[c][1] + states[c][5] + inner[c] + states[c][6] for c in range(CAP)
    ]
    s6b[...] = spread(results, 32)
    sixth = share(3, s6b, s6r)
    s6r[tile_rows(me), :] = s6b[...]
    for copy in sixth:
        copy.wait_recv()
    mine = jnp.sum(s6r[pl.ds(me, SRC, stride=ROWS), :], axis=0, keepdims=True)
    mine = jnp.broadcast_to(mine, (ROWS, LANES))
    shifted = mine
    for place in range(1, ACT):
        shifted = jnp.where(sub == place, pltpu.roll(mine, LANES - 32 * place, 1), shifted)
    o_all[...] = shifted[0:ACT, :]

    for copy in first + second + third + fifth + sixth:
        copy.wait_send()

    @pl.when(me < SRC - 1)
    def _():
        for copy in up:
            copy.wait_send()

    @pl.when(me > 0)
    def _():
        for copy in down:
            copy.wait_send()


def cut(result, state, fields, taylor):
    state[...] = result[:, 0:6]
    fields[...] = result[:, 6:18]
    taylor[...] = result[:, 18:24]


def shards(
    positions,
    velocities,
    accelerations,
    jerk_terms,
    masses,
    elapsed,
    active_idx,
    owners,
    counts,
    block_lists,
):
    stars = positions.shape[1]
    window = stars + 2 * HALO
    hbm = pl.BlockSpec(memory_space=pl.ANY)
    smem = pl.BlockSpec(memory_space=pltpu.SMEM)
    vmem = pl.BlockSpec(memory_space=pltpu.VMEM)
    tile = pltpu.VMEM((ROWS, LANES), jnp.float32)
    landed = pltpu.VMEM((SRC * ROWS, LANES), jnp.float32)
    groups = pltpu.VMEM((TGT, ROWS, LANES), jnp.float32)
    itile = pltpu.VMEM((ROWS, LANES), jnp.int32)
    ilanded = pltpu.VMEM((SRC * ROWS, LANES), jnp.int32)
    three = pltpu.VMEM((3, window), jnp.float32)
    one = pltpu.VMEM((1, window), jnp.float32)
    dma = pltpu.SemaphoreType.DMA
    result = pl.pallas_call(
        kernel,
        out_shape=jax.ShapeDtypeStruct((ACT, LANES), jnp.float32),
        in_specs=[hbm] * 6 + [smem] * 3 + [vmem],
        out_specs=vmem,
        scratch_shapes=[
            three, three, three, three, one, one, three, three,
            pltpu.VMEM((window // BLOCK, CAP, ROWS, LANES), jnp.float32),
            pltpu.VMEM((SUBS, window // BLOCK, CAP, 6, ROWS, LANES), jnp.float32),
            itile, ilanded, tile, landed, tile, groups, groups, groups, tile, landed, tile, landed,
            dma((6,)), dma((2, 6)), dma((2, 6)), dma((4, SRC)), dma((4, SRC)),
            dma((TGT,)), dma((TGT,)), dma((TGT,)), dma((TGT,)),
        ],
        compiler_params=pltpu.CompilerParams(collective_id=0, has_side_effects=True),
    )(
        positions,
        velocities,
        accelerations,
        jerk_terms,
        masses[None],
        elapsed[None],
        active_idx,
        owners,
        counts,
        block_lists,
    )
    state, fields, taylor = pl.pallas_call(
        cut,
        out_shape=(
            jax.ShapeDtypeStruct((ACT, 6), jnp.float32),
            jax.ShapeDtypeStruct((ACT, 12), jnp.float32),
            jax.ShapeDtypeStruct((ACT, 6), jnp.float32),
        ),
        in_specs=[vmem],
        out_specs=(vmem, vmem, vmem),
    )(result)
    return state.T, fields.T, taylor.T


def solution(mesh):
    in_specs = (
        P(None, ("src", "tgt")),
        P(None, ("src", "tgt")),
        P(None, ("src", "tgt")),
        P(None, ("src", "tgt")),
        P(("src", "tgt")),
        P(("src", "tgt")),
        P(("src", "tgt")),
        P(("src", "tgt")),
        P(("src", "tgt")),
        P(("src", "tgt"), None),
    )
    out_specs = (P(None, ("src", "tgt")), P(None, ("src", "tgt")), P(None, ("src", "tgt")))
    return jax.shard_map(shards, mesh=mesh, in_specs=in_specs, out_specs=out_specs, check_vma=False)
```

```python
import jax
import jax.numpy as jnp
from jax import lax
from jax.experimental import pallas as pl
from jax.experimental.pallas import tpu as pltpu
from jax.sharding import PartitionSpec as P

LANES = 128
ROWS = 8
BLOCK = 128
HALO = 4 * BLOCK
SUBS = 2
CAP = 2
ACT = 4
SRC = 8
TGT = 16
SOFTENING = 0.0001
PIECES = 4
UNROLL = 8
MESH = pl.DeviceIdType.MESH
PAIRS = ((0, 1), (1, 1), (2, 0), (3, 0), (2, 1), (3, 1), (1, 0), (0, 0))
CODE_TABLE = sum(code * 4**at for at, (code, dz) in enumerate(PAIRS))
DZ_TABLE = sum(dz * 2**at for at, (code, dz) in enumerate(PAIRS))


def predict(position, velocity, acceleration, jerk_now, interval):
    new_position = [
        x + interval * (v + interval * (0.5 * a + interval * j / 6.0))
        for x, v, a, j in zip(position, velocity, acceleration, jerk_now)
    ]
    new_velocity = [
        v + interval * (a + 0.5 * interval * j)
        for v, a, j in zip(velocity, acceleration, jerk_now)
    ]
    return new_position, new_velocity


def correct(position, velocity, old_pull, old_change, new_pull, new_change, interval):
    new_position, new_velocity, snaps, crackles = [], [], [], []
    for x, v, a0, j0, a1, j1 in zip(
        position, velocity, old_pull, old_change, new_pull, new_change
    ):
        jump = a0 - a1
        snap = -6.0 * jump - interval * (4.0 * j0 + 2.0 * j1)
        crackle = 12.0 * jump + 6.0 * interval * (j0 + j1)
        new_position.append(x + interval * interval * (snap / 24.0 + crackle / 120.0))
        new_velocity.append(v + interval * (snap / 6.0 + crackle / 24.0))
        snaps.append(snap)
        crackles.append(crackle)
    return new_position, new_velocity, snaps, crackles


def pair_sums(sums, target, source, mass):
    u = [source[k] - target[k] for k in range(3)]
    e = [source[3 + k] - target[3 + k] for k in range(3)]
    distance = u[0] * u[0] + u[1] * u[1] + (u[2] * u[2] + SOFTENING)
    inverse = lax.rsqrt(distance)
    square = inverse * inverse
    weight = (mass * inverse) * square
    radial = (u[0] * e[0] + u[1] * e[1] + u[2] * e[2]) * square
    pull = [weight * u[k] for k in range(3)]
    return (
        [sums[k] + pull[k] for k in range(3)]
        + [sums[3 + k] + weight * e[k] for k in range(3)]
        + [sums[6 + k] + radial * pull[k] for k in range(3)]
    )


def total_of(sums):
    six = sums[0:3] + [sums[3 + k] - 3.0 * sums[6 + k] for k in range(3)]
    return [
        jnp.broadcast_to(jnp.sum(part, axis=1, keepdims=True), (ROWS, LANES)) for part in six
    ]


def lane_of(tile, lane):
    return jnp.broadcast_to(tile[:, lane : lane + 1], (ROWS, LANES))


def wide_row(ref, row, block, many):
    lanes = pl.ds(pl.multiple_of(block * LANES, LANES), LANES)
    return jnp.broadcast_to(ref[row : row + 1, lanes], (many * ACT * ROWS, LANES))


def row_of(ref, row, block):
    lanes = pl.ds(pl.multiple_of(block * LANES, LANES), LANES)
    return jnp.broadcast_to(ref[row : row + 1, lanes], (ROWS, LANES))


def kernel(
    pos, vel, acc, jrk, mas, ela, idx, own, cnt, lists,
    o_all,
    wpos, wvel, wacc, wjrk, wmas, wela, ppos, pvel, feat, mw, moved,
    s1b, s1r, s2b, s2r, s3b, s3r, s4b, s4r, s5b, s5r, s6b, s6r,
    hsend, hland, idx_here, own_here, cnt_here, lists_here,
    load_sem, number_sem, halo_send, halo_recv, src_send, src_recv, tgt_send, tgt_recv, sum_send, sum_recv,
):
    stars = pos.shape[1]
    blocks = stars // BLOCK
    window_blocks = wpos.shape[1] // BLOCK
    me = lax.axis_index("src")
    my_group = lax.axis_index("tgt")
    my_x, my_z, my_core = my_group // 4, (my_group // 2) % 2, my_group % 2

    def src_peer(step):
        return {"src": lax.rem(me + step, SRC)}

    def tgt_peer(code, dz, dc):
        x = lax.rem(my_x + code * (1 + 2 * lax.rem(my_x, 2)), 4)
        z, core = lax.rem(my_z + dz, 2), lax.rem(my_core + dc, 2)
        return {"tgt": x * 4 + z * 2 + core}

    def tile_rows(at):
        return pl.ds(pl.multiple_of(at * ROWS, ROWS), ROWS)

    lane = lax.broadcasted_iota(jnp.int32, (ROWS, LANES), 1)
    sub = lax.broadcasted_iota(jnp.int32, (ROWS, LANES), 0)
    zero = jnp.zeros((ROWS, LANES), jnp.float32)

    barrier = pltpu.get_barrier_semaphore()
    for step in (4, 3, 5, 2, 6, 1, 7):
        pl.semaphore_signal(barrier, inc=1, device_id=src_peer(step), device_id_type=MESH)
    for code, dz in PAIRS:
        for dc in (1, 0):
            if code or dz or dc:
                pl.semaphore_signal(
                    barrier, inc=1, device_id=tgt_peer(code, dz, dc), device_id_type=MESH
                )

    numbered = ((idx, idx_here), (own, own_here), (cnt, cnt_here), (lists, lists_here))
    number_loads = [
        pltpu.make_async_copy(hbm, here, number_sem.at[at])
        for at, (hbm, here) in enumerate(numbered)
    ]
    for load in number_loads:
        load.start()

    arrays = ((pos, wpos), (vel, wvel), (acc, wacc), (jrk, wjrk), (mas, wmas), (ela, wela))
    loads = [
        pltpu.make_async_copy(hbm, win.at[:, HALO : HALO + stars], load_sem.at[at])
        for at, (hbm, win) in enumerate(arrays)
    ]
    for load in loads:
        load.start()
    for load in number_loads:
        load.wait()

    tile = jnp.zeros((ROWS, LANES), jnp.int32)
    for place in range(ACT):
        for at, ref in enumerate((idx_here, own_here, cnt_here)):
            tile = jnp.where((sub == place) & (lane == 16 + at), ref[place], tile)
    s1b[...] = tile
    s1b[0:ACT, 0:16] = lists_here[...]

    pl.semaphore_wait(barrier, SRC + TGT - 2)

    def share(stage, sent, landed):
        for step in (4, 3, 5, 2, 6, 1, 7):
            pltpu.make_async_remote_copy(
                src_ref=sent,
                dst_ref=landed.at[tile_rows(me), :],
                send_sem=src_send.at[stage],
                recv_sem=src_recv.at[stage],
                device_id=src_peer(step),
                device_id_type=MESH,
            ).start()
        return stage, landed

    def wait_bytes(ref, semaphore):
        pltpu.make_async_copy(ref, ref, semaphore).wait()

    def wait_sent(shared):
        stage, landed = shared
        wait_bytes(landed.at[0 : (SRC - 1) * ROWS], src_send.at[stage])

    def wait_landed(shared):
        stage, landed = shared
        wait_bytes(landed.at[0 : (SRC - 1) * ROWS], src_recv.at[stage])

    first = share(0, s1b, s1r)
    s1r[tile_rows(me), :] = s1b[...]

    for load in loads:
        load.wait()

    up = pltpu.make_async_remote_copy(
        src_ref=hsend.at[0],
        dst_ref=hland.at[0],
        send_sem=halo_send.at[0],
        recv_sem=halo_recv.at[0],
        device_id={"src": lax.rem(me + 1, SRC)},
        device_id_type=MESH,
    )
    down = pltpu.make_async_remote_copy(
        src_ref=hsend.at[1],
        dst_ref=hland.at[1],
        send_sem=halo_send.at[1],
        recv_sem=halo_recv.at[1],
        device_id={"src": lax.rem(me + SRC - 1, SRC)},
        device_id_type=MESH,
    )
    row = 0
    for hbm, win in arrays:
        height = win.shape[0]
        hsend[0, row : row + height] = win[:, stars : stars + HALO]
        hsend[1, row : row + height] = win[:, HALO : 2 * HALO]
        row += height

    @pl.when(me < SRC - 1)
    def _():
        up.start()

    @pl.when(me > 0)
    def _():
        down.start()

    @pl.when(me == 0)
    def _():
        hland[0] = jnp.zeros(hland.shape[1:], jnp.float32)

    @pl.when(me == SRC - 1)
    def _():
        hland[1] = jnp.zeros(hland.shape[1:], jnp.float32)

    chunk = 4 * LANES

    def predict_chunk(at, carry):
        there = pl.ds(pl.multiple_of(at * chunk, LANES), chunk)
        (place,), (speed,) = predict(
            [wpos[:, there]], [wvel[:, there]], [wacc[:, there]], [wjrk[:, there]], wela[:, there]
        )
        ppos[:, there] = place
        pvel[:, there] = speed
        return carry

    lax.fori_loop(1, 1 + stars // chunk, predict_chunk, 0)

    def feature_chunk(at, carry):
        there = pl.ds(pl.multiple_of(HALO + at * chunk, LANES), chunk)
        wide = lax.broadcasted_iota(jnp.int32, (ROWS, chunk), 0)
        rest = jnp.where(wide == 6, 1.0, 0.0)
        for k in range(3):
            rest = jnp.where(wide == k, jnp.broadcast_to(ppos[k : k + 1, there], (ROWS, chunk)), rest)
            rest = jnp.where(
                wide == 3 + k, jnp.broadcast_to(pvel[k : k + 1, there], (ROWS, chunk)), rest
            )
        parts = []
        for part in range(3):
            parts.append(rest.astype(jnp.bfloat16).astype(jnp.float32))
            rest = rest - parts[-1]
        parts.append(jnp.zeros((ROWS, chunk), jnp.float32))
        here = pl.ds(pl.multiple_of(at * chunk, LANES), chunk)
        feat[:, here] = jnp.concatenate(parts, 0).astype(jnp.bfloat16)
        return carry

    lax.fori_loop(0, stars // chunk, feature_chunk, 0)

    wait_landed(first)

    numbers = [s1r[pl.ds(place, SRC, stride=ROWS), :] for place in range(ACT)]
    chosen = [[], []]
    before = jnp.zeros((ROWS, LANES), jnp.int32)
    for place in range(ACT):
        mine = lane_of(numbers[place], 17) == me
        for c in range(CAP):
            chosen[c].append(mine & (before == c))
        before = before + jnp.where(mine, 1, 0)

    def pick(c, values, empty):
        result = empty
        for place in range(ACT):
            result = jnp.where(chosen[c][place], values[place], result)
        return result

    izero = jnp.zeros((ROWS, LANES), jnp.int32)
    detail = [pick(c, numbers, izero) for c in range(CAP)]
    first_star = (me * TGT + my_group) * stars
    offset = [lane_of(detail[c], 16) - first_star for c in range(CAP)]
    count = [lane_of(detail[c], 18) for c in range(CAP)]

    def extract(refs):
        wide = sum(ref.shape[0] for ref in refs)

        def step(block, found):
            rows = [
                row_of(ref, row, block + HALO // BLOCK) for ref in refs for row in range(ref.shape[0])
            ]
            out = []
            for c in range(CAP):
                here = lane + block * BLOCK == offset[c]
                out.append([jnp.where(here, row, old) for row, old in zip(rows, found[c])])
            return out

        found = lax.fori_loop(0, blocks, step, [[zero] * wide for _ in range(CAP)], unroll=2)
        return [
            [
                jnp.broadcast_to(jnp.sum(part, axis=1, keepdims=True), (ROWS, LANES))
                for part in found[c]
            ]
            for c in range(CAP)
        ]

    start = extract((ppos, pvel))

    def spread(values, width):
        slots = []
        for c in range(CAP):
            slot = zero
            for k, value in enumerate(values[c]):
                slot = jnp.where(lax.rem(lane, width) == k, value, slot)
            slots.append(slot)
        result = zero
        for place in range(ACT):
            there = lane // width == place
            for c in range(CAP):
                result = jnp.where(there & chosen[c][place], slots[c], result)
        return result

    s2b[...] = spread(start, 8)
    second = share(1, s2b, s2r)
    s2r[tile_rows(me), :] = s2b[...]

    wait_sent(first)
    raw = extract((wpos, wvel, wacc, wjrk, wela))

    def mask_block(block, carry):
        mass = row_of(wmas, 0, block)
        for c in range(CAP):
            listed = jnp.where((detail[c] == block) & (lane < count[c]), 1.0, 0.0)
            member = jnp.broadcast_to(jnp.sum(listed, axis=1, keepdims=True), (ROWS, LANES))
            itself = lane + block * BLOCK == offset[c] + HALO
            mw[block, c] = jnp.where(itself, 0.0, member * mass)
        return carry

    @pl.when(me > 0)
    def _():
        up.wait_recv()

    @pl.when(me < SRC - 1)
    def _():
        down.wait_recv()

    row = 0
    for hbm, win in arrays:
        height = win.shape[0]
        win[:, 0:HALO] = hland[0, row : row + height]
        win[:, HALO + stars :] = hland[1, row : row + height]
        row += height

    lax.fori_loop(0, window_blocks, mask_block, 0, unroll=4)

    wait_landed(second)

    def gathered(ref):
        total = ref[0:ROWS, :]
        for at in range(1, SRC):
            total = total + ref[at * ROWS : (at + 1) * ROWS, :]
        return total

    group_targets = gathered(s2r)
    s3b[...] = group_targets
    s3r[0] = group_targets
    for code, dz in PAIRS:
        for dc in (1, 0):
            if code or dz or dc:
                pltpu.make_async_remote_copy(
                    src_ref=s3b,
                    dst_ref=s3r.at[code * 4 + dz * 2 + dc],
                    send_sem=tgt_send,
                    recv_sem=tgt_recv.at[code * 2 + dz],
                    device_id=tgt_peer(code, dz, dc),
                    device_id_type=MESH,
                ).start()

    def advance_block(block, carry):
        x = [row_of(wpos, k, block) for k in range(3)]
        v = [row_of(wvel, k, block) for k in range(3)]
        a = [row_of(wacc, k, block) for k in range(3)]
        half = [0.5 * row for row in a]
        j = [row_of(wjrk, k, block) for k in range(3)]
        sixth_j = [row / 6.0 for row in j]
        half_j = [0.5 * row for row in j]
        since = row_of(wela, 0, block)
        for number in range(SUBS):
            for c in range(CAP):
                d = since + (0.25 * (number + 1)) * raw[c][12]
                for k in range(3):
                    moved[number, block, c, k] = x[k] + d * (
                        v[k] + d * (half[k] + d * sixth_j[k])
                    )
                    moved[number, block, c, 3 + k] = v[k] + d * (a[k] + d * half_j[k])
        return carry

    lax.fori_loop(0, window_blocks, advance_block, 0)

    def near_field(targets, number):
        def step(block, sums):
            if number is None:
                source = [row_of(ref, k, block) for ref in (ppos, pvel) for k in range(3)]
                sources = [source] * CAP
            else:
                sources = [[moved[number, block, c, k] for k in range(6)] for c in range(CAP)]
            return [pair_sums(sums[c], targets[c], sources[c], mw[block, c]) for c in range(CAP)]

        sums = lax.fori_loop(0, window_blocks, step, [[zero] * 9 for _ in range(CAP)], unroll=8)
        return [total_of(sums[c]) for c in range(CAP)]

    predict_chunk(0, 0)
    predict_chunk(window_blocks * LANES // chunk - 1, 0)
    inner = near_field(start, None)

    def field(tiles):
        many = len(tiles)
        aims = [
            jnp.concatenate(
                [lane_of(tile, place * 8 + k) for tile in tiles for place in range(ACT)], 0
            )
            for k in range(6)
        ]

        def halves(value):
            high = value.astype(jnp.bfloat16)
            return high, (value - high.astype(jnp.float32)).astype(jnp.bfloat16)

        def step(at, sums):
            columns = []
            for piece in range(PIECES):
                block = at * PIECES + piece
                rows = [wide_row(ppos, k, block + HALO // BLOCK, many) for k in range(3)]
                rows += [wide_row(pvel, k, block + HALO // BLOCK, many) for k in range(3)]
                mass = wide_row(wmas, 0, block + HALO // BLOCK, many)
                u = [rows[k] - aims[k] for k in range(3)]
                e = [rows[3 + k] - aims[3 + k] for k in range(3)]
                inverse = lax.rsqrt(u[0] * u[0] + u[1] * u[1] + (u[2] * u[2] + SOFTENING))
                square = inverse * inverse
                weight = (mass * inverse) * square
                radial = weight * ((u[0] * e[0] + u[1] * e[1] + u[2] * e[2]) * square)
                columns.append(jnp.concatenate(halves(weight) + halves(radial), 0))
            left = jnp.concatenate(columns, 1)
            right = feat[:, pl.ds(pl.multiple_of(at * PIECES * LANES, LANES), PIECES * LANES)]
            return sums + lax.dot_general(
                left, right, (((1,), (1,)), ((), ())), preferred_element_type=jnp.float32
            )

        sums = lax.fori_loop(
            0,
            blocks // PIECES,
            step,
            jnp.zeros((4 * many * ACT * ROWS, 4 * ROWS), jnp.float32),
            unroll=UNROLL,
        )
        blank = jnp.zeros((4 * many * ACT * ROWS, LANES - 4 * ROWS), jnp.float32)
        sums = jnp.concatenate([sums, blank], 1)
        results = []
        for at, targets in enumerate(tiles):
            result = zero
            for place in range(ACT):
                sides = []
                for array in range(2):
                    row = (2 * array * ACT * many + at * ACT + place) * ROWS
                    both = sums[row : row + ROWS] + sums[row + many * ACT * ROWS : row + (many * ACT + 1) * ROWS]
                    sides.append(
                        both + pltpu.roll(both, LANES - 8, 1) + pltpu.roll(both, LANES - 16, 1)
                    )
                aim = pltpu.roll(targets, (LANES - 8 * place) % LANES, 1) if place else targets
                plain = sides[0] - aim * lane_of(sides[0], 6)
                along = sides[1] - aim * lane_of(sides[1], 6)
                change = plain - 3.0 * pltpu.roll(along, 3, 1)
                six = jnp.where(lane < 3, plain, change)
                if place:
                    six = pltpu.roll(six, 8 * place, 1)
                result = jnp.where(lane // 8 == place, six, result)
            results.append(result)
        return results

    def send_sum(at, code, dz, dc):
        pltpu.make_async_remote_copy(
            src_ref=s4b.at[at],
            dst_ref=s4r.at[at],
            send_sem=sum_send,
            recv_sem=sum_recv,
            device_id=tgt_peer(code, dz, dc),
            device_id_type=MESH,
        ).start()

    def group_pair(pair, tables):
        code, dz = lax.rem(tables[0], 4), lax.rem(tables[1], 2)
        other = pair < len(PAIRS) - 1
        places = [code * 4 + dz * 2 + dc for dc in (0, 1)]

        @pl.when(other)
        def _():
            wait_bytes(s3r.at[pl.ds(0, 2)], tgt_recv.at[code * 2 + dz])

        @pl.when(jnp.logical_not(other))
        def _():
            wait_bytes(s3r.at[0], tgt_recv.at[code * 2 + dz])

        results = field([s3r[place] for place in places])
        for dc in (1, 0):
            s4b[places[dc]] = results[dc]
        send_sum(places[1], code, dz, 1)

        @pl.when(other)
        def _():
            send_sum(places[0], code, dz, 0)

        @pl.when(jnp.logical_not(other))
        def _():
            s4r[0] = results[0]

        return tables[0] // 4, tables[1] // 2

    lax.fori_loop(0, len(PAIRS), group_pair, (jnp.int32(CODE_TABLE), jnp.int32(DZ_TABLE)))

    wait_bytes(s4r.at[pl.ds(0, TGT - 1)], sum_recv)
    group_sum = s4r[0]
    for at in range(1, TGT):
        group_sum = group_sum + s4r[at]

    s5b[...] = group_sum
    fifth = share(2, s5b, s5r)
    s5r[tile_rows(me), :] = group_sum
    wait_sent(second)
    wait_bytes(s3r.at[pl.ds(0, TGT - 1)], tgt_send)
    wait_bytes(s4r.at[pl.ds(0, TGT - 1)], sum_send)

    @pl.when(me < SRC - 1)
    def _():
        up.wait_send()

    @pl.when(me > 0)
    def _():
        down.wait_send()

    wait_sent(fifth)
    wait_landed(fifth)
    summed = gathered(s5r)
    lanes_of = [[lane_of(summed, place * 8 + k) for place in range(ACT)] for k in range(6)]

    totals = [[pick(c, lanes_of[k], zero) for k in range(6)] for c in range(CAP)]
    states = []
    for c in range(CAP):
        interval = raw[c][12]
        old_pull, old_change = raw[c][6:9], raw[c][9:12]
        regular = [totals[c][k] - inner[c][k] for k in range(6)]
        x, v, snap, crackle = correct(
            start[c][0:3],
            start[c][3:6],
            old_pull,
            old_change,
            totals[c][0:3],
            totals[c][3:6],
            interval,
        )
        states.append((x, v, totals[c][0:3], totals[c][3:6], 0.25 * interval, regular, snap + crackle))
    for number in range(SUBS):
        advance = [states[c][4] * (number + 1) for c in range(CAP)]
        guesses = [predict(*states[c][0:5]) for c in range(CAP)]
        inner = near_field([x + v for x, v in guesses], number)
        after = []
        for c in range(CAP):
            x, v, pull, change, substep, regular, rest = states[c]
            new_pull = [
                regular[k] + advance[c] * regular[3 + k] + inner[c][k] for k in range(3)
            ]
            new_change = [regular[3 + k] + inner[c][3 + k] for k in range(3)]
            x, v, unused, ignored = correct(
                guesses[c][0], guesses[c][1], pull, change, new_pull, new_change, substep
            )
            after.append((x, v, new_pull, new_change, substep, regular, rest))
        states = after

    results = [
        states[c][0] + states[c][1] + states[c][5] + inner[c] + states[c][6] for c in range(CAP)
    ]
    s6b[...] = spread(results, 32)
    sixth = share(3, s6b, s6r)
    s6r[tile_rows(me), :] = s6b[...]
    wait_landed(sixth)
    mine = jnp.sum(s6r[pl.ds(me, SRC, stride=ROWS), :], axis=0, keepdims=True)
    mine = jnp.broadcast_to(mine, (ROWS, LANES))
    shifted = mine
    for place in range(1, ACT):
        shifted = jnp.where(sub == place, pltpu.roll(mine, LANES - 32 * place, 1), shifted)
    o_all[...] = shifted[0:ACT, :]

    wait_sent(sixth)


def cut(result, state, fields, taylor):
    state[...] = result[:, 0:6]
    fields[...] = result[:, 6:18]
    taylor[...] = result[:, 18:24]


def shards(
    positions,
    velocities,
    accelerations,
    jerk_terms,
    masses,
    elapsed,
    active_idx,
    owners,
    counts,
    block_lists,
):
    stars = positions.shape[1]
    window = stars + 2 * HALO
    hbm = pl.BlockSpec(memory_space=pl.ANY)
    vmem = pl.BlockSpec(memory_space=pltpu.VMEM)
    tile = pltpu.VMEM((ROWS, LANES), jnp.float32)
    landed = pltpu.VMEM((SRC * ROWS, LANES), jnp.float32)
    groups = pltpu.VMEM((TGT, ROWS, LANES), jnp.float32)
    itile = pltpu.VMEM((ROWS, LANES), jnp.int32)
    ilanded = pltpu.VMEM((SRC * ROWS, LANES), jnp.int32)
    three = pltpu.VMEM((3, window), jnp.float32)
    one = pltpu.VMEM((1, window), jnp.float32)
    dma = pltpu.SemaphoreType.DMA
    result = pl.pallas_call(
        kernel,
        out_shape=jax.ShapeDtypeStruct((ACT, LANES), jnp.float32),
        in_specs=[hbm] * 10,
        out_specs=vmem,
        scratch_shapes=[
            three, three, three, three, one, one, three, three,
            pltpu.VMEM((4 * ROWS, stars), jnp.bfloat16),
            pltpu.VMEM((window // BLOCK, CAP, ROWS, LANES), jnp.float32),
            pltpu.VMEM((SUBS, window // BLOCK, CAP, 6, ROWS, LANES), jnp.float32),
            itile, ilanded, tile, landed, tile, groups, groups, groups, tile, landed, tile, landed,
            pltpu.VMEM((2, 14, HALO), jnp.float32), pltpu.VMEM((2, 14, HALO), jnp.float32),
            pltpu.SMEM((ACT,), jnp.int32), pltpu.SMEM((ACT,), jnp.int32), pltpu.SMEM((ACT,), jnp.int32),
            pltpu.VMEM((ACT, 16), jnp.int32),
            dma((6,)), dma((4,)), dma((2,)), dma((2,)), dma((4,)), dma((4,)),
            dma, dma((len(PAIRS),)), dma, dma,
        ],
        compiler_params=pltpu.CompilerParams(collective_id=0, has_side_effects=True),
    )(
        positions,
        velocities,
        accelerations,
        jerk_terms,
        masses[None],
        elapsed[None],
        active_idx,
        owners,
        counts,
        block_lists,
    )
    state, fields, taylor = pl.pallas_call(
        cut,
        out_shape=(
            jax.ShapeDtypeStruct((ACT, 6), jnp.float32),
            jax.ShapeDtypeStruct((ACT, 12), jnp.float32),
            jax.ShapeDtypeStruct((ACT, 6), jnp.float32),
        ),
        in_specs=[vmem],
        out_specs=(vmem, vmem, vmem),
    )(result)
    return state.T, fields.T, taylor.T


def solution(mesh):
    in_specs = (
        P(None, ("src", "tgt")),
        P(None, ("src", "tgt")),
        P(None, ("src", "tgt")),
        P(None, ("src", "tgt")),
        P(("src", "tgt")),
        P(("src", "tgt")),
        P(("src", "tgt")),
        P(("src", "tgt")),
        P(("src", "tgt")),
        P(("src", "tgt"), None),
    )
    out_specs = (P(None, ("src", "tgt")), P(None, ("src", "tgt")), P(None, ("src", "tgt")))
    return jax.shard_map(shards, mesh=mesh, in_specs=in_specs, out_specs=out_specs, check_vma=False)
```

```python
import jax
import jax.numpy as jnp
from jax import lax
from jax.experimental import pallas as pl
from jax.experimental.pallas import tpu as pltpu
from jax.sharding import PartitionSpec as P

LANES = 128
ROWS = 8
BLOCK = 128
HALO = 4 * BLOCK
SUBS = 2
CAP = 2
ACT = 4
SRC = 8
TGT = 16
SOFTENING = 0.0001
PIECES = 4
UNROLL = 8
MESH = pl.DeviceIdType.MESH
PAIRS = ((0, 1), (1, 1), (2, 0), (3, 0), (2, 1), (3, 1), (1, 0), (0, 0))
CODE_TABLE = sum(code * 4**at for at, (code, dz) in enumerate(PAIRS))
DZ_TABLE = sum(dz * 2**at for at, (code, dz) in enumerate(PAIRS))


def predict(position, velocity, acceleration, jerk_now, interval):
    new_position = [
        x + interval * (v + interval * (0.5 * a + interval * j / 6.0))
        for x, v, a, j in zip(position, velocity, acceleration, jerk_now)
    ]
    new_velocity = [
        v + interval * (a + 0.5 * interval * j)
        for v, a, j in zip(velocity, acceleration, jerk_now)
    ]
    return new_position, new_velocity


def correct(position, velocity, old_pull, old_change, new_pull, new_change, interval):
    new_position, new_velocity, snaps, crackles = [], [], [], []
    for x, v, a0, j0, a1, j1 in zip(
        position, velocity, old_pull, old_change, new_pull, new_change
    ):
        jump = a0 - a1
        snap = -6.0 * jump - interval * (4.0 * j0 + 2.0 * j1)
        crackle = 12.0 * jump + 6.0 * interval * (j0 + j1)
        new_position.append(x + interval * interval * (snap / 24.0 + crackle / 120.0))
        new_velocity.append(v + interval * (snap / 6.0 + crackle / 24.0))
        snaps.append(snap)
        crackles.append(crackle)
    return new_position, new_velocity, snaps, crackles


def pair_sums(sums, target, source, mass):
    u = [source[k] - target[k] for k in range(3)]
    e = [source[3 + k] - target[3 + k] for k in range(3)]
    distance = u[0] * u[0] + u[1] * u[1] + (u[2] * u[2] + SOFTENING)
    inverse = lax.rsqrt(distance)
    square = inverse * inverse
    weight = (mass * inverse) * square
    radial = (u[0] * e[0] + u[1] * e[1] + u[2] * e[2]) * square
    pull = [weight * u[k] for k in range(3)]
    return (
        [sums[k] + pull[k] for k in range(3)]
        + [sums[3 + k] + weight * e[k] for k in range(3)]
        + [sums[6 + k] + radial * pull[k] for k in range(3)]
    )


def total_of(sums):
    six = sums[0:3] + [sums[3 + k] - 3.0 * sums[6 + k] for k in range(3)]
    return [
        jnp.broadcast_to(jnp.sum(part, axis=1, keepdims=True), (ROWS, LANES)) for part in six
    ]


def lane_of(tile, lane):
    return jnp.broadcast_to(tile[:, lane : lane + 1], (ROWS, LANES))


def wide_row(ref, row, block, many):
    lanes = pl.ds(pl.multiple_of(block * LANES, LANES), LANES)
    return jnp.broadcast_to(ref[row : row + 1, lanes], (many * ACT * ROWS, LANES))


def row_of(ref, row, block):
    lanes = pl.ds(pl.multiple_of(block * LANES, LANES), LANES)
    return jnp.broadcast_to(ref[row : row + 1, lanes], (ROWS, LANES))


def kernel(
    pos, vel, acc, jrk, mas, ela, idx, own, cnt, lists,
    o_all,
    wpos, wvel, wacc, wjrk, wmas, wela, ppos, pvel, feat, mw, moved,
    s1b, s1r, s2b, s2r, s3b, s3r, s4b, s4r, s5b, s5r, s6b, s6r,
    hsend, hland, idx_here, own_here, cnt_here, lists_here,
    load_sem, number_sem, halo_send, halo_recv, src_send, src_recv, tgt_send, tgt_recv, sum_send, sum_recv,
):
    stars = pos.shape[1]
    blocks = stars // BLOCK
    window_blocks = wpos.shape[1] // BLOCK
    me = lax.axis_index("src")
    my_group = lax.axis_index("tgt")
    my_x, my_z, my_core = my_group // 4, (my_group // 2) % 2, my_group % 2

    def src_peer(step):
        return {"src": lax.rem(me + step, SRC)}

    def tgt_peer(code, dz, dc):
        x = lax.rem(my_x + code * (1 + 2 * lax.rem(my_x, 2)), 4)
        z, core = lax.rem(my_z + dz, 2), lax.rem(my_core + dc, 2)
        return {"tgt": x * 4 + z * 2 + core}

    def tile_rows(at):
        return pl.ds(pl.multiple_of(at * ROWS, ROWS), ROWS)

    lane = lax.broadcasted_iota(jnp.int32, (ROWS, LANES), 1)
    sub = lax.broadcasted_iota(jnp.int32, (ROWS, LANES), 0)
    zero = jnp.zeros((ROWS, LANES), jnp.float32)

    barrier = pltpu.get_barrier_semaphore()
    for step in (4, 3, 5, 2, 6, 1, 7):
        pl.semaphore_signal(barrier, inc=1, device_id=src_peer(step), device_id_type=MESH)
    for code, dz in PAIRS:
        for dc in (1, 0):
            if code or dz or dc:
                pl.semaphore_signal(
                    barrier, inc=1, device_id=tgt_peer(code, dz, dc), device_id_type=MESH
                )

    numbered = ((idx, idx_here), (own, own_here), (cnt, cnt_here), (lists, lists_here))
    number_loads = [
        pltpu.make_async_copy(hbm, here, number_sem.at[at])
        for at, (hbm, here) in enumerate(numbered)
    ]
    for load in number_loads:
        load.start()

    arrays = ((pos, wpos), (vel, wvel), (acc, wacc), (jrk, wjrk), (mas, wmas), (ela, wela))
    loads = [
        pltpu.make_async_copy(hbm, win.at[:, HALO : HALO + stars], load_sem.at[at])
        for at, (hbm, win) in enumerate(arrays)
    ]
    for load in loads:
        load.start()
    for load in number_loads:
        load.wait()

    tile = jnp.zeros((ROWS, LANES), jnp.int32)
    for place in range(ACT):
        for at, ref in enumerate((idx_here, own_here, cnt_here)):
            tile = jnp.where((sub == place) & (lane == 16 + at), ref[place], tile)
    s1b[...] = tile
    s1b[0:ACT, 0:16] = lists_here[...]

    pl.semaphore_wait(barrier, SRC + TGT - 2)

    def share(stage, sent, landed):
        for step in (4, 3, 5, 2, 6, 1, 7):
            pltpu.make_async_remote_copy(
                src_ref=sent,
                dst_ref=landed.at[tile_rows(me), :],
                send_sem=src_send.at[stage],
                recv_sem=src_recv.at[stage],
                device_id=src_peer(step),
                device_id_type=MESH,
            ).start()
        return stage, landed

    def wait_bytes(ref, semaphore):
        pltpu.make_async_copy(ref, ref, semaphore).wait()

    def wait_sent(shared):
        stage, landed = shared
        wait_bytes(landed.at[0 : (SRC - 1) * ROWS], src_send.at[stage])

    def wait_landed(shared):
        stage, landed = shared
        wait_bytes(landed.at[0 : (SRC - 1) * ROWS], src_recv.at[stage])

    first = share(0, s1b, s1r)
    s1r[tile_rows(me), :] = s1b[...]

    for load in loads:
        load.wait()

    up = pltpu.make_async_remote_copy(
        src_ref=hsend.at[0],
        dst_ref=hland.at[0],
        send_sem=halo_send.at[0],
        recv_sem=halo_recv.at[0],
        device_id={"src": lax.rem(me + 1, SRC)},
        device_id_type=MESH,
    )
    down = pltpu.make_async_remote_copy(
        src_ref=hsend.at[1],
        dst_ref=hland.at[1],
        send_sem=halo_send.at[1],
        recv_sem=halo_recv.at[1],
        device_id={"src": lax.rem(me + SRC - 1, SRC)},
        device_id_type=MESH,
    )
    row = 0
    for hbm, win in arrays:
        height = win.shape[0]
        hsend[0, row : row + height] = win[:, stars : stars + HALO]
        hsend[1, row : row + height] = win[:, HALO : 2 * HALO]
        row += height

    @pl.when(me < SRC - 1)
    def _():
        up.start()

    @pl.when(me > 0)
    def _():
        down.start()

    @pl.when(me == 0)
    def _():
        hland[0] = jnp.zeros(hland.shape[1:], jnp.float32)

    @pl.when(me == SRC - 1)
    def _():
        hland[1] = jnp.zeros(hland.shape[1:], jnp.float32)

    chunk = 4 * LANES

    def predict_chunk(at, carry):
        there = pl.ds(pl.multiple_of(at * chunk, LANES), chunk)
        (place,), (speed,) = predict(
            [wpos[:, there]], [wvel[:, there]], [wacc[:, there]], [wjrk[:, there]], wela[:, there]
        )
        ppos[:, there] = place
        pvel[:, there] = speed
        return carry

    lax.fori_loop(1, 1 + stars // chunk, predict_chunk, 0)

    def feature_chunk(at, carry):
        there = pl.ds(pl.multiple_of(HALO + at * chunk, LANES), chunk)
        wide = lax.broadcasted_iota(jnp.int32, (ROWS, chunk), 0)
        rest = jnp.where(wide == 6, 1.0, 0.0)
        for k in range(3):
            rest = jnp.where(wide == k, jnp.broadcast_to(ppos[k : k + 1, there], (ROWS, chunk)), rest)
            rest = jnp.where(
                wide == 3 + k, jnp.broadcast_to(pvel[k : k + 1, there], (ROWS, chunk)), rest
            )
        parts = []
        for part in range(3):
            parts.append(rest.astype(jnp.bfloat16).astype(jnp.float32))
            rest = rest - parts[-1]
        parts.append(jnp.zeros((ROWS, chunk), jnp.float32))
        here = pl.ds(pl.multiple_of(at * chunk, LANES), chunk)
        feat[:, here] = jnp.concatenate(parts, 0).astype(jnp.bfloat16)
        return carry

    lax.fori_loop(0, stars // chunk, feature_chunk, 0)

    wait_landed(first)

    numbers = [s1r[pl.ds(place, SRC, stride=ROWS), :] for place in range(ACT)]
    chosen = [[], []]
    before = jnp.zeros((ROWS, LANES), jnp.int32)
    for place in range(ACT):
        mine = lane_of(numbers[place], 17) == me
        for c in range(CAP):
            chosen[c].append(mine & (before == c))
        before = before + jnp.where(mine, 1, 0)

    def pick(c, values, empty):
        result = empty
        for place in range(ACT):
            result = jnp.where(chosen[c][place], values[place], result)
        return result

    izero = jnp.zeros((ROWS, LANES), jnp.int32)
    detail = [pick(c, numbers, izero) for c in range(CAP)]
    first_star = (me * TGT + my_group) * stars
    offset = [lane_of(detail[c], 16) - first_star for c in range(CAP)]
    count = [lane_of(detail[c], 18) for c in range(CAP)]

    def extract(refs):
        wide = sum(ref.shape[0] for ref in refs)

        def step(block, found):
            rows = [
                row_of(ref, row, block + HALO // BLOCK) for ref in refs for row in range(ref.shape[0])
            ]
            out = []
            for c in range(CAP):
                here = lane + block * BLOCK == offset[c]
                out.append([jnp.where(here, row, old) for row, old in zip(rows, found[c])])
            return out

        found = lax.fori_loop(0, blocks, step, [[zero] * wide for _ in range(CAP)], unroll=2)
        return [
            [
                jnp.broadcast_to(jnp.sum(part, axis=1, keepdims=True), (ROWS, LANES))
                for part in found[c]
            ]
            for c in range(CAP)
        ]

    start = extract((ppos, pvel))

    def spread(values, width):
        slots = []
        for c in range(CAP):
            slot = zero
            for k, value in enumerate(values[c]):
                slot = jnp.where(lax.rem(lane, width) == k, value, slot)
            slots.append(slot)
        result = zero
        for place in range(ACT):
            there = lane // width == place
            for c in range(CAP):
                result = jnp.where(there & chosen[c][place], slots[c], result)
        return result

    s2b[...] = spread(start, 8)
    second = share(1, s2b, s2r)
    s2r[tile_rows(me), :] = s2b[...]

    wait_sent(first)
    raw = extract((wpos, wvel, wacc, wjrk, wela))

    def mask_block(block, carry):
        mass = row_of(wmas, 0, block)
        for c in range(CAP):
            listed = jnp.where((detail[c] == block) & (lane < count[c]), 1.0, 0.0)
            member = jnp.broadcast_to(jnp.sum(listed, axis=1, keepdims=True), (ROWS, LANES))
            itself = lane + block * BLOCK == offset[c] + HALO
            mw[block, c] = jnp.where(itself, 0.0, member * mass)
        return carry

    @pl.when(me > 0)
    def _():
        up.wait_recv()

    @pl.when(me < SRC - 1)
    def _():
        down.wait_recv()

    row = 0
    for hbm, win in arrays:
        height = win.shape[0]
        win[:, 0:HALO] = hland[0, row : row + height]
        win[:, HALO + stars :] = hland[1, row : row + height]
        row += height

    lax.fori_loop(0, window_blocks, mask_block, 0, unroll=4)

    wait_landed(second)

    def gathered(ref):
        total = ref[0:ROWS, :]
        for at in range(1, SRC):
            total = total + ref[at * ROWS : (at + 1) * ROWS, :]
        return total

    group_targets = gathered(s2r)
    s3b[...] = group_targets
    s3r[0] = group_targets
    for code, dz in PAIRS:
        for dc in (1, 0):
            if code or dz or dc:
                pltpu.make_async_remote_copy(
                    src_ref=s3b,
                    dst_ref=s3r.at[code * 4 + dz * 2 + dc],
                    send_sem=tgt_send,
                    recv_sem=tgt_recv.at[code * 2 + dz],
                    device_id=tgt_peer(code, dz, dc),
                    device_id_type=MESH,
                ).start()

    def advance_block(block, carry):
        x = [row_of(wpos, k, block) for k in range(3)]
        v = [row_of(wvel, k, block) for k in range(3)]
        a = [row_of(wacc, k, block) for k in range(3)]
        half = [0.5 * row for row in a]
        j = [row_of(wjrk, k, block) for k in range(3)]
        sixth_j = [row / 6.0 for row in j]
        half_j = [0.5 * row for row in j]
        since = row_of(wela, 0, block)
        for number in range(SUBS):
            for c in range(CAP):
                d = since + (0.25 * (number + 1)) * raw[c][12]
                for k in range(3):
                    moved[number, block, c, k] = x[k] + d * (
                        v[k] + d * (half[k] + d * sixth_j[k])
                    )
                    moved[number, block, c, 3 + k] = v[k] + d * (a[k] + d * half_j[k])
        return carry

    lax.fori_loop(0, window_blocks, advance_block, 0)

    def near_field(targets, number):
        def step(block, sums):
            if number is None:
                source = [row_of(ref, k, block) for ref in (ppos, pvel) for k in range(3)]
                sources = [source] * CAP
            else:
                sources = [[moved[number, block, c, k] for k in range(6)] for c in range(CAP)]
            return [pair_sums(sums[c], targets[c], sources[c], mw[block, c]) for c in range(CAP)]

        sums = lax.fori_loop(0, window_blocks, step, [[zero] * 9 for _ in range(CAP)], unroll=8)
        return [total_of(sums[c]) for c in range(CAP)]

    predict_chunk(0, 0)
    predict_chunk(window_blocks * LANES // chunk - 1, 0)
    inner = near_field(start, None)

    def field(tiles):
        many = len(tiles)
        aims = [
            jnp.concatenate(
                [lane_of(tile, place * 8 + k) for tile in tiles for place in range(ACT)], 0
            )
            for k in range(6)
        ]

        def halves(value):
            high = value.astype(jnp.bfloat16)
            return high, (value - high.astype(jnp.float32)).astype(jnp.bfloat16)

        def step(at, sums):
            columns = []
            for piece in range(PIECES):
                block = at * PIECES + piece
                rows = [wide_row(ppos, k, block + HALO // BLOCK, many) for k in range(3)]
                rows += [wide_row(pvel, k, block + HALO // BLOCK, many) for k in range(3)]
                mass = wide_row(wmas, 0, block + HALO // BLOCK, many)
                u = [rows[k] - aims[k] for k in range(3)]
                e = [rows[3 + k] - aims[3 + k] for k in range(3)]
                inverse = lax.rsqrt(u[0] * u[0] + u[1] * u[1] + (u[2] * u[2] + SOFTENING))
                square = inverse * inverse
                weight = (mass * inverse) * square
                radial = weight * ((u[0] * e[0] + u[1] * e[1] + u[2] * e[2]) * square)
                columns.append(jnp.concatenate(halves(weight) + halves(radial), 0))
            left = jnp.concatenate(columns, 1)
            right = feat[:, pl.ds(pl.multiple_of(at * PIECES * LANES, LANES), PIECES * LANES)]
            return sums + lax.dot_general(
                left, right, (((1,), (1,)), ((), ())), preferred_element_type=jnp.float32
            )

        sums = lax.fori_loop(
            0,
            blocks // PIECES,
            step,
            jnp.zeros((4 * many * ACT * ROWS, 4 * ROWS), jnp.float32),
            unroll=UNROLL,
        )
        blank = jnp.zeros((4 * many * ACT * ROWS, LANES - 4 * ROWS), jnp.float32)
        sums = jnp.concatenate([sums, blank], 1)
        results = []
        for at in range(many):
            for array in range(2):
                tile = zero
                for place in range(ACT):
                    row = ((2 * array * many + at) * ACT + place) * ROWS
                    both = sums[row : row + ROWS] + sums[row + many * ACT * ROWS :][0:ROWS]
                    tile = tile + (pltpu.roll(both, 32 * place, 1) if place else both)
                results.append(tile)
        return results

    def send_sum(at, code, dz, dc):
        pltpu.make_async_remote_copy(
            src_ref=s4b.at[at],
            dst_ref=s4r.at[at],
            send_sem=sum_send,
            recv_sem=sum_recv,
            device_id=tgt_peer(code, dz, dc),
            device_id_type=MESH,
        ).start()

    def group_pair(pair, tables):
        code, dz = lax.rem(tables[0], 4), lax.rem(tables[1], 2)
        other = pair < len(PAIRS) - 1
        places = [code * 4 + dz * 2 + dc for dc in (0, 1)]

        @pl.when(other)
        def _():
            wait_bytes(s3r.at[pl.ds(0, 2)], tgt_recv.at[code * 2 + dz])

        @pl.when(jnp.logical_not(other))
        def _():
            wait_bytes(s3r.at[0], tgt_recv.at[code * 2 + dz])

        results = field([s3r[place] for place in places])
        for dc in (1, 0):
            for array in range(2):
                s4b[places[dc], array] = results[2 * dc + array]
        send_sum(places[1], code, dz, 1)

        @pl.when(other)
        def _():
            send_sum(places[0], code, dz, 0)

        @pl.when(jnp.logical_not(other))
        def _():
            for array in range(2):
                s4r[0, array] = results[array]

        return tables[0] // 4, tables[1] // 2

    lax.fori_loop(0, len(PAIRS), group_pair, (jnp.int32(CODE_TABLE), jnp.int32(DZ_TABLE)))

    aim = group_targets
    for place in range(1, ACT):
        aim = jnp.where(lane // 32 == place, pltpu.roll(group_targets, 24 * place, 1), aim)
    wait_bytes(s4r.at[pl.ds(0, TGT - 1)], sum_recv)
    sides = []
    for array in range(2):
        both = s4r[0, array]
        for at in range(1, TGT):
            both = both + s4r[at, array]
        both = both + pltpu.roll(both, LANES - 8, 1) + pltpu.roll(both, LANES - 16, 1)
        ones = lane_of(both, 6)
        for place in range(1, ACT):
            ones = jnp.where(lane // 32 == place, lane_of(both, 32 * place + 6), ones)
        sides.append(both - aim * ones)
    group_sum = jnp.where(
        lax.rem(lane, 32) < 3, sides[0], sides[0] - 3.0 * pltpu.roll(sides[1], 3, 1)
    )

    s5b[...] = group_sum
    fifth = share(2, s5b, s5r)
    s5r[tile_rows(me), :] = group_sum
    wait_sent(second)
    wait_bytes(s3r.at[pl.ds(0, TGT - 1)], tgt_send)
    wait_bytes(s4r.at[pl.ds(0, TGT - 1)], sum_send)

    @pl.when(me < SRC - 1)
    def _():
        up.wait_send()

    @pl.when(me > 0)
    def _():
        down.wait_send()

    wait_sent(fifth)
    wait_landed(fifth)
    summed = gathered(s5r)
    lanes_of = [[lane_of(summed, place * 32 + k) for place in range(ACT)] for k in range(6)]

    totals = [[pick(c, lanes_of[k], zero) for k in range(6)] for c in range(CAP)]
    states = []
    for c in range(CAP):
        interval = raw[c][12]
        old_pull, old_change = raw[c][6:9], raw[c][9:12]
        regular = [totals[c][k] - inner[c][k] for k in range(6)]
        x, v, snap, crackle = correct(
            start[c][0:3],
            start[c][3:6],
            old_pull,
            old_change,
            totals[c][0:3],
            totals[c][3:6],
            interval,
        )
        states.append((x, v, totals[c][0:3], totals[c][3:6], 0.25 * interval, regular, snap + crackle))
    for number in range(SUBS):
        advance = [states[c][4] * (number + 1) for c in range(CAP)]
        guesses = [predict(*states[c][0:5]) for c in range(CAP)]
        inner = near_field([x + v for x, v in guesses], number)
        after = []
        for c in range(CAP):
            x, v, pull, change, substep, regular, rest = states[c]
            new_pull = [
                regular[k] + advance[c] * regular[3 + k] + inner[c][k] for k in range(3)
            ]
            new_change = [regular[3 + k] + inner[c][3 + k] for k in range(3)]
            x, v, unused, ignored = correct(
                guesses[c][0], guesses[c][1], pull, change, new_pull, new_change, substep
            )
            after.append((x, v, new_pull, new_change, substep, regular, rest))
        states = after

    results = [
        states[c][0] + states[c][1] + states[c][5] + inner[c] + states[c][6] for c in range(CAP)
    ]
    s6b[...] = spread(results, 32)
    sixth = share(3, s6b, s6r)
    s6r[tile_rows(me), :] = s6b[...]
    wait_landed(sixth)
    mine = jnp.sum(s6r[pl.ds(me, SRC, stride=ROWS), :], axis=0, keepdims=True)
    mine = jnp.broadcast_to(mine, (ROWS, LANES))
    shifted = mine
    for place in range(1, ACT):
        shifted = jnp.where(sub == place, pltpu.roll(mine, LANES - 32 * place, 1), shifted)
    o_all[...] = shifted[0:ACT, :]

    wait_sent(sixth)


def cut(result, state, fields, taylor):
    state[...] = result[:, 0:6]
    fields[...] = result[:, 6:18]
    taylor[...] = result[:, 18:24]


def shards(
    positions,
    velocities,
    accelerations,
    jerk_terms,
    masses,
    elapsed,
    active_idx,
    owners,
    counts,
    block_lists,
):
    stars = positions.shape[1]
    window = stars + 2 * HALO
    hbm = pl.BlockSpec(memory_space=pl.ANY)
    vmem = pl.BlockSpec(memory_space=pltpu.VMEM)
    tile = pltpu.VMEM((ROWS, LANES), jnp.float32)
    landed = pltpu.VMEM((SRC * ROWS, LANES), jnp.float32)
    groups = pltpu.VMEM((TGT, ROWS, LANES), jnp.float32)
    sums = pltpu.VMEM((TGT, 2, ROWS, LANES), jnp.float32)
    itile = pltpu.VMEM((ROWS, LANES), jnp.int32)
    ilanded = pltpu.VMEM((SRC * ROWS, LANES), jnp.int32)
    three = pltpu.VMEM((3, window), jnp.float32)
    one = pltpu.VMEM((1, window), jnp.float32)
    dma = pltpu.SemaphoreType.DMA
    result = pl.pallas_call(
        kernel,
        out_shape=pltpu.VMEM((ACT, LANES), jnp.float32),
        in_specs=[hbm] * 10,
        out_specs=vmem,
        scratch_shapes=[
            three, three, three, three, one, one, three, three,
            pltpu.VMEM((4 * ROWS, stars), jnp.bfloat16),
            pltpu.VMEM((window // BLOCK, CAP, ROWS, LANES), jnp.float32),
            pltpu.VMEM((SUBS, window // BLOCK, CAP, 6, ROWS, LANES), jnp.float32),
            itile, ilanded, tile, landed, tile, groups, sums, sums, tile, landed, tile, landed,
            pltpu.VMEM((2, 14, HALO), jnp.float32), pltpu.VMEM((2, 14, HALO), jnp.float32),
            pltpu.SMEM((ACT,), jnp.int32), pltpu.SMEM((ACT,), jnp.int32), pltpu.SMEM((ACT,), jnp.int32),
            pltpu.VMEM((ACT, 16), jnp.int32),
            dma((6,)), dma((4,)), dma((2,)), dma((2,)), dma((4,)), dma((4,)),
            dma, dma((len(PAIRS),)), dma, dma,
        ],
        compiler_params=pltpu.CompilerParams(collective_id=0, has_side_effects=True),
    )(
        positions,
        velocities,
        accelerations,
        jerk_terms,
        masses[None],
        elapsed[None],
        active_idx,
        owners,
        counts,
        block_lists,
    )
    state, fields, taylor = pl.pallas_call(
        cut,
        out_shape=(
            jax.ShapeDtypeStruct((ACT, 6), jnp.float32),
            jax.ShapeDtypeStruct((ACT, 12), jnp.float32),
            jax.ShapeDtypeStruct((ACT, 6), jnp.float32),
        ),
        in_specs=[vmem],
        out_specs=(vmem, vmem, vmem),
    )(pltpu.with_memory_space_constraint(result, pltpu.VMEM))
    return state.T, fields.T, taylor.T


def solution(mesh):
    in_specs = (
        P(None, ("src", "tgt")),
        P(None, ("src", "tgt")),
        P(None, ("src", "tgt")),
        P(None, ("src", "tgt")),
        P(("src", "tgt")),
        P(("src", "tgt")),
        P(("src", "tgt")),
        P(("src", "tgt")),
        P(("src", "tgt")),
        P(("src", "tgt"), None),
    )
    out_specs = (P(None, ("src", "tgt")), P(None, ("src", "tgt")), P(None, ("src", "tgt")))
    return jax.shard_map(shards, mesh=mesh, in_specs=in_specs, out_specs=out_specs, check_vma=False)
```

```python
import jax
import jax.numpy as jnp
from jax import lax
from jax.experimental import pallas as pl
from jax.experimental.pallas import tpu as pltpu
from jax.sharding import PartitionSpec as P

LANES = 128
ROWS = 8
BLOCK = 128
HALO = 4 * BLOCK
SUBS = 2
CAP = 2
ACT = 4
SRC = 8
TGT = 16
SOFTENING = 0.0001
PIECES = 4
UNROLL = 8
MESH = pl.DeviceIdType.MESH
ORDERS = (
    ((0, 0), (1, 0), (2, 0), (3, 0), (2, 1), (3, 1), (1, 1), (0, 1)),
    ((0, 1), (2, 1), (3, 1), (2, 0), (3, 0), (1, 1), (1, 0), (0, 0)),
)
CODE_TABLES = [sum(code * 4**at for at, (code, dz) in enumerate(order)) for order in ORDERS]
DZ_TABLES = [sum(dz * 2**at for at, (code, dz) in enumerate(order)) for order in ORDERS]
PAIRS = ORDERS[1]


def predict(position, velocity, acceleration, jerk_now, interval):
    new_position = [
        x + interval * (v + interval * (0.5 * a + interval * j / 6.0))
        for x, v, a, j in zip(position, velocity, acceleration, jerk_now)
    ]
    new_velocity = [
        v + interval * (a + 0.5 * interval * j)
        for v, a, j in zip(velocity, acceleration, jerk_now)
    ]
    return new_position, new_velocity


def correct(position, velocity, old_pull, old_change, new_pull, new_change, interval):
    new_position, new_velocity, snaps, crackles = [], [], [], []
    for x, v, a0, j0, a1, j1 in zip(
        position, velocity, old_pull, old_change, new_pull, new_change
    ):
        jump = a0 - a1
        snap = -6.0 * jump - interval * (4.0 * j0 + 2.0 * j1)
        crackle = 12.0 * jump + 6.0 * interval * (j0 + j1)
        new_position.append(x + interval * interval * (snap / 24.0 + crackle / 120.0))
        new_velocity.append(v + interval * (snap / 6.0 + crackle / 24.0))
        snaps.append(snap)
        crackles.append(crackle)
    return new_position, new_velocity, snaps, crackles


def pair_sums(sums, target, source, mass):
    u = [source[k] - target[k] for k in range(3)]
    e = [source[3 + k] - target[3 + k] for k in range(3)]
    distance = u[0] * u[0] + u[1] * u[1] + (u[2] * u[2] + SOFTENING)
    inverse = lax.rsqrt(distance)
    square = inverse * inverse
    weight = (mass * inverse) * square
    radial = (u[0] * e[0] + u[1] * e[1] + u[2] * e[2]) * square
    pull = [weight * u[k] for k in range(3)]
    return (
        [sums[k] + pull[k] for k in range(3)]
        + [sums[3 + k] + weight * e[k] for k in range(3)]
        + [sums[6 + k] + radial * pull[k] for k in range(3)]
    )


def total_of(sums):
    six = sums[0:3] + [sums[3 + k] - 3.0 * sums[6 + k] for k in range(3)]
    return [
        jnp.broadcast_to(jnp.sum(part, axis=1, keepdims=True), (ROWS, LANES)) for part in six
    ]


def lane_of(tile, lane):
    return jnp.broadcast_to(tile[:, lane : lane + 1], (ROWS, LANES))


def wide_row(ref, row, block, many):
    lanes = pl.ds(pl.multiple_of(block * LANES, LANES), LANES)
    return jnp.broadcast_to(ref[row : row + 1, lanes], (many * ACT * ROWS, LANES))


def row_of(ref, row, block):
    lanes = pl.ds(pl.multiple_of(block * LANES, LANES), LANES)
    return jnp.broadcast_to(ref[row : row + 1, lanes], (ROWS, LANES))


def kernel(
    pos, vel, acc, jrk, mas, ela, idx, own, cnt, lists,
    o_all,
    wpos, wvel, wacc, wjrk, wmas, wela, ppos, pvel, feat, mw, moved,
    s1b, s1r, s2b, s2r, s3b, s3r, s4b, s4r, s5b, s5r, s6b, s6r,
    hsend, hland, idx_here, own_here, cnt_here, lists_here,
    load_sem, number_sem, halo_send, halo_recv, src_send, src_recv, tgt_send, tgt_recv, sum_send, sum_recv,
):
    stars = pos.shape[1]
    blocks = stars // BLOCK
    window_blocks = wpos.shape[1] // BLOCK
    me = lax.axis_index("src")
    my_group = lax.axis_index("tgt")
    my_x, my_z, my_core = my_group // 4, (my_group // 2) % 2, my_group % 2

    def src_peer(step):
        return {"src": lax.rem(me + step, SRC)}

    def tgt_peer(code, dz, dc):
        x = lax.rem(my_x + code * (1 + 2 * lax.rem(my_x, 2)), 4)
        z, core = lax.rem(my_z + dz, 2), lax.rem(my_core + dc, 2)
        return {"tgt": x * 4 + z * 2 + core}

    def tile_rows(at):
        return pl.ds(pl.multiple_of(at * ROWS, ROWS), ROWS)

    lane = lax.broadcasted_iota(jnp.int32, (ROWS, LANES), 1)
    sub = lax.broadcasted_iota(jnp.int32, (ROWS, LANES), 0)
    zero = jnp.zeros((ROWS, LANES), jnp.float32)

    barrier = pltpu.get_barrier_semaphore()
    for step in (4, 3, 5, 2, 6, 1, 7):
        pl.semaphore_signal(barrier, inc=1, device_id=src_peer(step), device_id_type=MESH)
    for code, dz in PAIRS:
        for dc in (1, 0):
            if code or dz or dc:
                pl.semaphore_signal(
                    barrier, inc=1, device_id=tgt_peer(code, dz, dc), device_id_type=MESH
                )

    numbered = ((idx, idx_here), (own, own_here), (cnt, cnt_here), (lists, lists_here))
    number_loads = [
        pltpu.make_async_copy(hbm, here, number_sem.at[at])
        for at, (hbm, here) in enumerate(numbered)
    ]
    for load in number_loads:
        load.start()

    arrays = ((pos, wpos), (vel, wvel), (acc, wacc), (jrk, wjrk), (mas, wmas), (ela, wela))
    loads = [
        pltpu.make_async_copy(hbm, win.at[:, HALO : HALO + stars], load_sem.at[at])
        for at, (hbm, win) in enumerate(arrays)
    ]
    for load in loads:
        load.start()
    for load in number_loads:
        load.wait()

    tile = jnp.zeros((ROWS, LANES), jnp.int32)
    for place in range(ACT):
        for at, ref in enumerate((idx_here, own_here, cnt_here)):
            tile = jnp.where((sub == place) & (lane == 16 + at), ref[place], tile)
    s1b[...] = tile
    s1b[0:ACT, 0:16] = lists_here[...]

    pl.semaphore_wait(barrier, SRC + TGT - 2)

    def share(stage, sent, landed):
        for step in (4, 3, 5, 2, 6, 1, 7):
            pltpu.make_async_remote_copy(
                src_ref=sent,
                dst_ref=landed.at[tile_rows(me), :],
                send_sem=src_send.at[stage],
                recv_sem=src_recv.at[stage],
                device_id=src_peer(step),
                device_id_type=MESH,
            ).start()
        return stage, landed

    def wait_bytes(ref, semaphore):
        pltpu.make_async_copy(ref, ref, semaphore).wait()

    def wait_sent(shared):
        stage, landed = shared
        wait_bytes(landed.at[0 : (SRC - 1) * ROWS], src_send.at[stage])

    def wait_landed(shared):
        stage, landed = shared
        wait_bytes(landed.at[0 : (SRC - 1) * ROWS], src_recv.at[stage])

    first = share(0, s1b, s1r)
    s1r[tile_rows(me), :] = s1b[...]

    for load in loads:
        load.wait()

    up = pltpu.make_async_remote_copy(
        src_ref=hsend.at[0],
        dst_ref=hland.at[0],
        send_sem=halo_send.at[0],
        recv_sem=halo_recv.at[0],
        device_id={"src": lax.rem(me + 1, SRC)},
        device_id_type=MESH,
    )
    down = pltpu.make_async_remote_copy(
        src_ref=hsend.at[1],
        dst_ref=hland.at[1],
        send_sem=halo_send.at[1],
        recv_sem=halo_recv.at[1],
        device_id={"src": lax.rem(me + SRC - 1, SRC)},
        device_id_type=MESH,
    )
    row = 0
    for hbm, win in arrays:
        height = win.shape[0]
        hsend[0, row : row + height] = win[:, stars : stars + HALO]
        hsend[1, row : row + height] = win[:, HALO : 2 * HALO]
        row += height

    @pl.when(me < SRC - 1)
    def _():
        up.start()

    @pl.when(me > 0)
    def _():
        down.start()

    @pl.when(me == 0)
    def _():
        hland[0] = jnp.zeros(hland.shape[1:], jnp.float32)

    @pl.when(me == SRC - 1)
    def _():
        hland[1] = jnp.zeros(hland.shape[1:], jnp.float32)

    chunk = 4 * LANES

    def predict_chunk(at, carry):
        there = pl.ds(pl.multiple_of(at * chunk, LANES), chunk)
        (place,), (speed,) = predict(
            [wpos[:, there]], [wvel[:, there]], [wacc[:, there]], [wjrk[:, there]], wela[:, there]
        )
        ppos[:, there] = place
        pvel[:, there] = speed
        return carry

    lax.fori_loop(1, 1 + stars // chunk, predict_chunk, 0)

    def feature_chunk(at, carry):
        there = pl.ds(pl.multiple_of(HALO + at * chunk, LANES), chunk)
        wide = lax.broadcasted_iota(jnp.int32, (ROWS, chunk), 0)
        mass = jnp.broadcast_to(wmas[:, there], (ROWS, chunk))
        rest = jnp.where(wide == 6, mass, 0.0)
        for k in range(3):
            x = jnp.broadcast_to(ppos[k : k + 1, there], (ROWS, chunk))
            v = jnp.broadcast_to(pvel[k : k + 1, there], (ROWS, chunk))
            rest = jnp.where(wide == k, mass * x, jnp.where(wide == 3 + k, mass * v, rest))
        parts = []
        for part in range(3):
            parts.append(rest.astype(jnp.bfloat16).astype(jnp.float32))
            rest = rest - parts[-1]
        parts.append(jnp.zeros((ROWS, chunk), jnp.float32))
        here = pl.ds(pl.multiple_of(at * chunk, LANES), chunk)
        feat[:, here] = jnp.concatenate(parts, 0).astype(jnp.bfloat16)
        return carry

    lax.fori_loop(0, stars // chunk, feature_chunk, 0)

    wait_landed(first)

    numbers = [s1r[pl.ds(place, SRC, stride=ROWS), :] for place in range(ACT)]
    chosen = [[], []]
    before = jnp.zeros((ROWS, LANES), jnp.int32)
    for place in range(ACT):
        mine = lane_of(numbers[place], 17) == me
        for c in range(CAP):
            chosen[c].append(mine & (before == c))
        before = before + jnp.where(mine, 1, 0)

    def pick(c, values, empty):
        result = empty
        for place in range(ACT):
            result = jnp.where(chosen[c][place], values[place], result)
        return result

    izero = jnp.zeros((ROWS, LANES), jnp.int32)
    detail = [pick(c, numbers, izero) for c in range(CAP)]
    first_star = (me * TGT + my_group) * stars
    offset = [lane_of(detail[c], 16) - first_star for c in range(CAP)]
    count = [lane_of(detail[c], 18) for c in range(CAP)]

    def extract(refs):
        wide = sum(ref.shape[0] for ref in refs)

        def step(block, found):
            rows = [
                row_of(ref, row, block + HALO // BLOCK) for ref in refs for row in range(ref.shape[0])
            ]
            out = []
            for c in range(CAP):
                here = lane + block * BLOCK == offset[c]
                out.append([jnp.where(here, row, old) for row, old in zip(rows, found[c])])
            return out

        found = lax.fori_loop(0, blocks, step, [[zero] * wide for _ in range(CAP)], unroll=2)
        return [
            [
                jnp.broadcast_to(jnp.sum(part, axis=1, keepdims=True), (ROWS, LANES))
                for part in found[c]
            ]
            for c in range(CAP)
        ]

    start = extract((ppos, pvel))

    def spread(values, width):
        slots = []
        for c in range(CAP):
            slot = zero
            for k, value in enumerate(values[c]):
                slot = jnp.where(lax.rem(lane, width) == k, value, slot)
            slots.append(slot)
        result = zero
        for place in range(ACT):
            there = lane // width == place
            for c in range(CAP):
                result = jnp.where(there & chosen[c][place], slots[c], result)
        return result

    s2b[...] = spread(start, 8)
    second = share(1, s2b, s2r)
    s2r[tile_rows(me), :] = s2b[...]

    wait_sent(first)
    raw = extract((wpos, wvel, wacc, wjrk, wela))

    def mask_block(block, carry):
        mass = row_of(wmas, 0, block)
        for c in range(CAP):
            listed = jnp.where((detail[c] == block) & (lane < count[c]), 1.0, 0.0)
            member = jnp.broadcast_to(jnp.sum(listed, axis=1, keepdims=True), (ROWS, LANES))
            itself = lane + block * BLOCK == offset[c] + HALO
            mw[block, c] = jnp.where(itself, 0.0, member * mass)
        return carry

    @pl.when(me > 0)
    def _():
        up.wait_recv()

    @pl.when(me < SRC - 1)
    def _():
        down.wait_recv()

    row = 0
    for hbm, win in arrays:
        height = win.shape[0]
        win[:, 0:HALO] = hland[0, row : row + height]
        win[:, HALO + stars :] = hland[1, row : row + height]
        row += height

    lax.fori_loop(0, window_blocks, mask_block, 0, unroll=4)

    wait_landed(second)

    def gathered(ref):
        total = ref[0:ROWS, :]
        for at in range(1, SRC):
            total = total + ref[at * ROWS : (at + 1) * ROWS, :]
        return total

    group_targets = gathered(s2r)
    s3b[...] = group_targets
    s3r[0] = group_targets
    for code, dz in PAIRS:
        for dc in (1, 0):
            if code or dz or dc:
                pltpu.make_async_remote_copy(
                    src_ref=s3b,
                    dst_ref=s3r.at[code * 4 + dz * 2 + dc],
                    send_sem=tgt_send,
                    recv_sem=tgt_recv.at[code * 2 + dz],
                    device_id=tgt_peer(code, dz, dc),
                    device_id_type=MESH,
                ).start()

    def advance_block(block, carry):
        x = [row_of(wpos, k, block) for k in range(3)]
        v = [row_of(wvel, k, block) for k in range(3)]
        a = [row_of(wacc, k, block) for k in range(3)]
        half = [0.5 * row for row in a]
        j = [row_of(wjrk, k, block) for k in range(3)]
        sixth_j = [row / 6.0 for row in j]
        half_j = [0.5 * row for row in j]
        since = row_of(wela, 0, block)
        for number in range(SUBS):
            for c in range(CAP):
                d = since + (0.25 * (number + 1)) * raw[c][12]
                for k in range(3):
                    moved[number, block, c, k] = x[k] + d * (
                        v[k] + d * (half[k] + d * sixth_j[k])
                    )
                    moved[number, block, c, 3 + k] = v[k] + d * (a[k] + d * half_j[k])
        return carry

    lax.fori_loop(0, window_blocks, advance_block, 0)

    def near_field(targets, number):
        def step(block, sums):
            if number is None:
                source = [row_of(ref, k, block) for ref in (ppos, pvel) for k in range(3)]
                sources = [source] * CAP
            else:
                sources = [[moved[number, block, c, k] for k in range(6)] for c in range(CAP)]
            return [pair_sums(sums[c], targets[c], sources[c], mw[block, c]) for c in range(CAP)]

        sums = lax.fori_loop(0, window_blocks, step, [[zero] * 9 for _ in range(CAP)], unroll=8)
        return [total_of(sums[c]) for c in range(CAP)]

    predict_chunk(0, 0)
    predict_chunk(window_blocks * LANES // chunk - 1, 0)
    inner = near_field(start, None)

    def field(tiles):
        many = len(tiles)
        aims = [
            jnp.concatenate(
                [lane_of(tile, place * 8 + k) for tile in tiles for place in range(ACT)], 0
            )
            for k in range(6)
        ]

        def halves(value):
            high = value.astype(jnp.bfloat16)
            return high, (value - high.astype(jnp.float32)).astype(jnp.bfloat16)

        def step(at, sums):
            columns = []
            for piece in range(PIECES):
                block = at * PIECES + piece
                rows = [wide_row(ppos, k, block + HALO // BLOCK, many) for k in range(3)]
                rows += [wide_row(pvel, k, block + HALO // BLOCK, many) for k in range(3)]
                u = [rows[k] - aims[k] for k in range(3)]
                e = [rows[3 + k] - aims[3 + k] for k in range(3)]
                inverse = lax.rsqrt(u[0] * u[0] + u[1] * u[1] + (u[2] * u[2] + SOFTENING))
                square = inverse * inverse
                weight = inverse * square
                radial = weight * ((u[0] * e[0] + u[1] * e[1] + u[2] * e[2]) * square)
                columns.append(jnp.concatenate(halves(weight) + halves(radial), 0))
            left = jnp.concatenate(columns, 1)
            right = feat[:, pl.ds(pl.multiple_of(at * PIECES * LANES, LANES), PIECES * LANES)]
            return sums + lax.dot_general(
                left, right, (((1,), (1,)), ((), ())), preferred_element_type=jnp.float32
            )

        sums = lax.fori_loop(
            0,
            blocks // PIECES,
            step,
            jnp.zeros((4 * many * ACT * ROWS, 4 * ROWS), jnp.float32),
            unroll=UNROLL,
        )
        blank = jnp.zeros((4 * many * ACT * ROWS, LANES - 4 * ROWS), jnp.float32)
        sums = jnp.concatenate([sums, blank], 1)
        results = []
        for at in range(many):
            for array in range(2):
                tile = zero
                for place in range(ACT):
                    row = ((2 * array * many + at) * ACT + place) * ROWS
                    both = sums[row : row + ROWS] + sums[row + many * ACT * ROWS :][0:ROWS]
                    tile = tile + (pltpu.roll(both, 32 * place, 1) if place else both)
                results.append(tile)
        return results

    def send_sum(at, code, dz, dc):
        pltpu.make_async_remote_copy(
            src_ref=s4b.at[at],
            dst_ref=s4r.at[at],
            send_sem=sum_send,
            recv_sem=sum_recv,
            device_id=tgt_peer(code, dz, dc),
            device_id_type=MESH,
        ).start()

    def group_pair(pair, tables):
        code, dz = lax.rem(tables[0], 4), lax.rem(tables[1], 2)
        other = code + dz > 0
        places = [code * 4 + dz * 2 + dc for dc in (0, 1)]

        @pl.when(other)
        def _():
            wait_bytes(s3r.at[pl.ds(0, 2)], tgt_recv.at[code * 2 + dz])

        @pl.when(jnp.logical_not(other))
        def _():
            wait_bytes(s3r.at[0], tgt_recv.at[code * 2 + dz])

        results = field([s3r[place] for place in places])
        for dc in (1, 0):
            for array in range(2):
                s4b[places[dc], array] = results[2 * dc + array]
        send_sum(places[1], code, dz, 1)

        @pl.when(other)
        def _():
            send_sum(places[0], code, dz, 0)

        @pl.when(jnp.logical_not(other))
        def _():
            for array in range(2):
                s4r[0, array] = results[array]

        return [lax.div(tables[0], 4), lax.div(tables[1], 2)]

    tables = [low + my_z * (high - low) for low, high in (CODE_TABLES, DZ_TABLES)]
    lax.fori_loop(0, len(PAIRS), group_pair, tables)

    aim = group_targets
    for place in range(1, ACT):
        aim = jnp.where(lane // 32 == place, pltpu.roll(group_targets, 24 * place, 1), aim)
    wait_bytes(s4r.at[pl.ds(0, TGT - 1)], sum_recv)
    sides = []
    for array in range(2):
        both = s4r[0, array]
        for at in range(1, TGT):
            both = both + s4r[at, array]
        both = both + pltpu.roll(both, LANES - 8, 1) + pltpu.roll(both, LANES - 16, 1)
        ones = lane_of(both, 6)
        for place in range(1, ACT):
            ones = jnp.where(lane // 32 == place, lane_of(both, 32 * place + 6), ones)
        sides.append(both - aim * ones)
    group_sum = jnp.where(
        lax.rem(lane, 32) < 3, sides[0], sides[0] - 3.0 * pltpu.roll(sides[1], 3, 1)
    )

    s5b[...] = group_sum
    fifth = share(2, s5b, s5r)
    s5r[tile_rows(me), :] = group_sum
    wait_sent(second)
    wait_bytes(s3r.at[pl.ds(0, TGT - 1)], tgt_send)
    wait_bytes(s4r.at[pl.ds(0, TGT - 1)], sum_send)

    @pl.when(me < SRC - 1)
    def _():
        up.wait_send()

    @pl.when(me > 0)
    def _():
        down.wait_send()

    wait_sent(fifth)
    wait_landed(fifth)
    summed = gathered(s5r)
    lanes_of = [[lane_of(summed, place * 32 + k) for place in range(ACT)] for k in range(6)]

    totals = [[pick(c, lanes_of[k], zero) for k in range(6)] for c in range(CAP)]
    states = []
    for c in range(CAP):
        interval = raw[c][12]
        old_pull, old_change = raw[c][6:9], raw[c][9:12]
        regular = [totals[c][k] - inner[c][k] for k in range(6)]
        x, v, snap, crackle = correct(
            start[c][0:3],
            start[c][3:6],
            old_pull,
            old_change,
            totals[c][0:3],
            totals[c][3:6],
            interval,
        )
        states.append((x, v, totals[c][0:3], totals[c][3:6], 0.25 * interval, regular, snap + crackle))
    for number in range(SUBS):
        advance = [states[c][4] * (number + 1) for c in range(CAP)]
        guesses = [predict(*states[c][0:5]) for c in range(CAP)]
        inner = near_field([x + v for x, v in guesses], number)
        after = []
        for c in range(CAP):
            x, v, pull, change, substep, regular, rest = states[c]
            new_pull = [
                regular[k] + advance[c] * regular[3 + k] + inner[c][k] for k in range(3)
            ]
            new_change = [regular[3 + k] + inner[c][3 + k] for k in range(3)]
            x, v, unused, ignored = correct(
                guesses[c][0], guesses[c][1], pull, change, new_pull, new_change, substep
            )
            after.append((x, v, new_pull, new_change, substep, regular, rest))
        states = after

    results = [
        states[c][0] + states[c][1] + states[c][5] + inner[c] + states[c][6] for c in range(CAP)
    ]
    s6b[...] = spread(results, 32)
    sixth = share(3, s6b, s6r)
    s6r[tile_rows(me), :] = s6b[...]
    wait_landed(sixth)
    mine = jnp.sum(s6r[pl.ds(me, SRC, stride=ROWS), :], axis=0, keepdims=True)
    mine = jnp.broadcast_to(mine, (ROWS, LANES))
    shifted = mine
    for place in range(1, ACT):
        shifted = jnp.where(sub == place, pltpu.roll(mine, LANES - 32 * place, 1), shifted)
    o_all[...] = shifted[0:ACT, :]

    wait_sent(sixth)


def cut(result, state, fields, taylor):
    state[...] = result[:, 0:6]
    fields[...] = result[:, 6:18]
    taylor[...] = result[:, 18:24]


def shards(
    positions,
    velocities,
    accelerations,
    jerk_terms,
    masses,
    elapsed,
    active_idx,
    owners,
    counts,
    block_lists,
):
    stars = positions.shape[1]
    window = stars + 2 * HALO
    hbm = pl.BlockSpec(memory_space=pl.ANY)
    vmem = pl.BlockSpec(memory_space=pltpu.VMEM)
    tile = pltpu.VMEM((ROWS, LANES), jnp.float32)
    landed = pltpu.VMEM((SRC * ROWS, LANES), jnp.float32)
    groups = pltpu.VMEM((TGT, ROWS, LANES), jnp.float32)
    sums = pltpu.VMEM((TGT, 2, ROWS, LANES), jnp.float32)
    itile = pltpu.VMEM((ROWS, LANES), jnp.int32)
    ilanded = pltpu.VMEM((SRC * ROWS, LANES), jnp.int32)
    three = pltpu.VMEM((3, window), jnp.float32)
    one = pltpu.VMEM((1, window), jnp.float32)
    dma = pltpu.SemaphoreType.DMA
    result = pl.pallas_call(
        kernel,
        out_shape=pltpu.VMEM((ACT, LANES), jnp.float32),
        in_specs=[hbm] * 10,
        out_specs=vmem,
        scratch_shapes=[
            three, three, three, three, one, one, three, three,
            pltpu.VMEM((4 * ROWS, stars), jnp.bfloat16),
            pltpu.VMEM((window // BLOCK, CAP, ROWS, LANES), jnp.float32),
            pltpu.VMEM((SUBS, window // BLOCK, CAP, 6, ROWS, LANES), jnp.float32),
            itile, ilanded, tile, landed, tile, groups, sums, sums, tile, landed, tile, landed,
            pltpu.VMEM((2, 14, HALO), jnp.float32), pltpu.VMEM((2, 14, HALO), jnp.float32),
            pltpu.SMEM((ACT,), jnp.int32), pltpu.SMEM((ACT,), jnp.int32), pltpu.SMEM((ACT,), jnp.int32),
            pltpu.VMEM((ACT, 16), jnp.int32),
            dma((6,)), dma((4,)), dma((2,)), dma((2,)), dma((4,)), dma((4,)),
            dma, dma((len(PAIRS),)), dma, dma,
        ],
        compiler_params=pltpu.CompilerParams(collective_id=0, has_side_effects=True),
    )(
        positions,
        velocities,
        accelerations,
        jerk_terms,
        masses[None],
        elapsed[None],
        active_idx,
        owners,
        counts,
        block_lists,
    )
    state, fields, taylor = pl.pallas_call(
        cut,
        out_shape=(
            jax.ShapeDtypeStruct((ACT, 6), jnp.float32),
            jax.ShapeDtypeStruct((ACT, 12), jnp.float32),
            jax.ShapeDtypeStruct((ACT, 6), jnp.float32),
        ),
        in_specs=[vmem],
        out_specs=(vmem, vmem, vmem),
    )(pltpu.with_memory_space_constraint(result, pltpu.VMEM))
    return state.T, fields.T, taylor.T


def solution(mesh):
    in_specs = (
        P(None, ("src", "tgt")),
        P(None, ("src", "tgt")),
        P(None, ("src", "tgt")),
        P(None, ("src", "tgt")),
        P(("src", "tgt")),
        P(("src", "tgt")),
        P(("src", "tgt")),
        P(("src", "tgt")),
        P(("src", "tgt")),
        P(("src", "tgt"), None),
    )
    out_specs = (P(None, ("src", "tgt")), P(None, ("src", "tgt")), P(None, ("src", "tgt")))
    return jax.shard_map(shards, mesh=mesh, in_specs=in_specs, out_specs=out_specs, check_vma=False)
```

```python
import jax
import jax.numpy as jnp
from jax import lax
from jax.experimental import pallas as pl
from jax.experimental.pallas import tpu as pltpu
from jax.sharding import PartitionSpec as P

LANES = 128
ROWS = 8
BLOCK = 128
HALO = 4 * BLOCK
SUBS = 2
CAP = 2
ACT = 4
SRC = 8
TGT = 16
SOFTENING = 0.0001
PIECES = 4
UNROLL = 8
MESH = pl.DeviceIdType.MESH
ORDERS = (
    ((0, 0), (1, 0), (2, 0), (3, 0), (2, 1), (3, 1), (1, 1), (0, 1)),
    ((0, 1), (1, 1), (2, 1), (3, 1), (2, 0), (3, 0), (1, 0), (0, 0)),
)
CODE_TABLES = [sum(code * 4**at for at, (code, dz) in enumerate(order)) for order in ORDERS]
DZ_TABLES = [sum(dz * 2**at for at, (code, dz) in enumerate(order)) for order in ORDERS]
PAIRS = ORDERS[1]


def predict(position, velocity, acceleration, jerk_now, interval):
    new_position = [
        x + interval * (v + interval * (0.5 * a + interval * j / 6.0))
        for x, v, a, j in zip(position, velocity, acceleration, jerk_now)
    ]
    new_velocity = [
        v + interval * (a + 0.5 * interval * j)
        for v, a, j in zip(velocity, acceleration, jerk_now)
    ]
    return new_position, new_velocity


def correct(position, velocity, old_pull, old_change, new_pull, new_change, interval):
    new_position, new_velocity, snaps, crackles = [], [], [], []
    for x, v, a0, j0, a1, j1 in zip(
        position, velocity, old_pull, old_change, new_pull, new_change
    ):
        jump = a0 - a1
        snap = -6.0 * jump - interval * (4.0 * j0 + 2.0 * j1)
        crackle = 12.0 * jump + 6.0 * interval * (j0 + j1)
        new_position.append(x + interval * interval * (snap / 24.0 + crackle / 120.0))
        new_velocity.append(v + interval * (snap / 6.0 + crackle / 24.0))
        snaps.append(snap)
        crackles.append(crackle)
    return new_position, new_velocity, snaps, crackles


def pair_sums(sums, target, source, mass):
    u = [source[k] - target[k] for k in range(3)]
    e = [source[3 + k] - target[3 + k] for k in range(3)]
    distance = u[0] * u[0] + u[1] * u[1] + (u[2] * u[2] + SOFTENING)
    inverse = lax.rsqrt(distance)
    square = inverse * inverse
    weight = (mass * inverse) * square
    radial = (u[0] * e[0] + u[1] * e[1] + u[2] * e[2]) * square
    pull = [weight * u[k] for k in range(3)]
    return (
        [sums[k] + pull[k] for k in range(3)]
        + [sums[3 + k] + weight * e[k] for k in range(3)]
        + [sums[6 + k] + radial * pull[k] for k in range(3)]
    )


def total_of(sums):
    six = sums[0:3] + [sums[3 + k] - 3.0 * sums[6 + k] for k in range(3)]
    return [
        jnp.broadcast_to(jnp.sum(part, axis=1, keepdims=True), (ROWS, LANES)) for part in six
    ]


def lane_of(tile, lane):
    return jnp.broadcast_to(tile[:, lane : lane + 1], (ROWS, LANES))


def wide_row(ref, row, block, many):
    lanes = pl.ds(pl.multiple_of(block * LANES, LANES), LANES)
    return jnp.broadcast_to(ref[row : row + 1, lanes], (many * ACT * ROWS, LANES))


def row_of(ref, row, block):
    lanes = pl.ds(pl.multiple_of(block * LANES, LANES), LANES)
    return jnp.broadcast_to(ref[row : row + 1, lanes], (ROWS, LANES))


def kernel(
    pos, vel, acc, jrk, mas, ela, idx, own, cnt, lists,
    o_all,
    wpos, wvel, wacc, wjrk, wmas, wela, ppos, pvel, feat, mw, moved,
    s1b, s1r, s2b, s2r, s3b, s3r, s4b, s4r, s5b, s5r, s6b, s6r,
    hsend, hland, idx_here, own_here, cnt_here, lists_here,
    load_sem, number_sem, halo_send, halo_recv, src_send, src_recv, tgt_send, tgt_recv, sum_send, sum_recv,
):
    stars = pos.shape[1]
    blocks = stars // BLOCK
    window_blocks = wpos.shape[1] // BLOCK
    me = lax.axis_index("src")
    my_group = lax.axis_index("tgt")
    my_x, my_z, my_core = my_group // 4, (my_group // 2) % 2, my_group % 2

    def src_peer(step):
        return {"src": lax.rem(me + step, SRC)}

    def tgt_peer(code, dz, dc):
        x = lax.rem(my_x + code * (1 + 2 * lax.rem(my_x, 2)), 4)
        z, core = lax.rem(my_z + dz, 2), lax.rem(my_core + dc, 2)
        return {"tgt": x * 4 + z * 2 + core}

    def tile_rows(at):
        return pl.ds(pl.multiple_of(at * ROWS, ROWS), ROWS)

    lane = lax.broadcasted_iota(jnp.int32, (ROWS, LANES), 1)
    sub = lax.broadcasted_iota(jnp.int32, (ROWS, LANES), 0)
    zero = jnp.zeros((ROWS, LANES), jnp.float32)

    barrier = pltpu.get_barrier_semaphore()
    for step in (4, 3, 5, 2, 6, 1, 7):
        pl.semaphore_signal(barrier, inc=1, device_id=src_peer(step), device_id_type=MESH)
    for code, dz in PAIRS:
        for dc in (1, 0):
            if code or dz or dc:
                pl.semaphore_signal(
                    barrier, inc=1, device_id=tgt_peer(code, dz, dc), device_id_type=MESH
                )

    numbered = ((idx, idx_here), (own, own_here), (cnt, cnt_here), (lists, lists_here))
    number_loads = [
        pltpu.make_async_copy(hbm, here, number_sem.at[at])
        for at, (hbm, here) in enumerate(numbered)
    ]
    for load in number_loads:
        load.start()

    arrays = ((pos, wpos), (vel, wvel), (acc, wacc), (jrk, wjrk), (mas, wmas), (ela, wela))
    loads = [
        pltpu.make_async_copy(hbm, win.at[:, HALO : HALO + stars], load_sem.at[at])
        for at, (hbm, win) in enumerate(arrays)
    ]
    for load in loads:
        load.start()
    for load in number_loads:
        load.wait()

    tile = jnp.zeros((ROWS, LANES), jnp.int32)
    for place in range(ACT):
        for at, ref in enumerate((idx_here, own_here, cnt_here)):
            tile = jnp.where((sub == place) & (lane == 16 + at), ref[place], tile)
    s1b[...] = tile
    s1b[0:ACT, 0:16] = lists_here[...]

    pl.semaphore_wait(barrier, SRC + TGT - 2)

    def share(stage, sent, landed):
        for step in (4, 3, 5, 2, 6, 1, 7):
            pltpu.make_async_remote_copy(
                src_ref=sent,
                dst_ref=landed.at[tile_rows(me), :],
                send_sem=src_send.at[stage],
                recv_sem=src_recv.at[stage],
                device_id=src_peer(step),
                device_id_type=MESH,
            ).start()
        return stage, landed

    def wait_bytes(ref, semaphore):
        pltpu.make_async_copy(ref, ref, semaphore).wait()

    def wait_sent(shared):
        stage, landed = shared
        wait_bytes(landed.at[0 : (SRC - 1) * ROWS], src_send.at[stage])

    def wait_landed(shared):
        stage, landed = shared
        wait_bytes(landed.at[0 : (SRC - 1) * ROWS], src_recv.at[stage])

    first = share(0, s1b, s1r)
    s1r[tile_rows(me), :] = s1b[...]

    for load in loads:
        load.wait()

    up = pltpu.make_async_remote_copy(
        src_ref=hsend.at[0],
        dst_ref=hland.at[0],
        send_sem=halo_send.at[0],
        recv_sem=halo_recv.at[0],
        device_id={"src": lax.rem(me + 1, SRC)},
        device_id_type=MESH,
    )
    down = pltpu.make_async_remote_copy(
        src_ref=hsend.at[1],
        dst_ref=hland.at[1],
        send_sem=halo_send.at[1],
        recv_sem=halo_recv.at[1],
        device_id={"src": lax.rem(me + SRC - 1, SRC)},
        device_id_type=MESH,
    )
    row = 0
    for hbm, win in arrays:
        height = win.shape[0]
        hsend[0, row : row + height] = win[:, stars : stars + HALO]
        hsend[1, row : row + height] = win[:, HALO : 2 * HALO]
        row += height

    @pl.when(me < SRC - 1)
    def _():
        up.start()

    @pl.when(me > 0)
    def _():
        down.start()

    @pl.when(me == 0)
    def _():
        hland[0] = jnp.zeros(hland.shape[1:], jnp.float32)

    @pl.when(me == SRC - 1)
    def _():
        hland[1] = jnp.zeros(hland.shape[1:], jnp.float32)

    chunk = 4 * LANES

    def predict_chunk(at, carry):
        there = pl.ds(pl.multiple_of(at * chunk, LANES), chunk)
        (place,), (speed,) = predict(
            [wpos[:, there]], [wvel[:, there]], [wacc[:, there]], [wjrk[:, there]], wela[:, there]
        )
        ppos[:, there] = place
        pvel[:, there] = speed
        return carry

    lax.fori_loop(1, 1 + stars // chunk, predict_chunk, 0)

    def feature_chunk(at, carry):
        there = pl.ds(pl.multiple_of(HALO + at * chunk, LANES), chunk)
        wide = lax.broadcasted_iota(jnp.int32, (ROWS, chunk), 0)
        mass = jnp.broadcast_to(wmas[:, there], (ROWS, chunk))
        rest = jnp.where(wide == 6, mass, 0.0)
        for k in range(3):
            x = jnp.broadcast_to(ppos[k : k + 1, there], (ROWS, chunk))
            v = jnp.broadcast_to(pvel[k : k + 1, there], (ROWS, chunk))
            rest = jnp.where(wide == k, mass * x, jnp.where(wide == 3 + k, mass * v, rest))
        parts = []
        for part in range(3):
            parts.append(rest.astype(jnp.bfloat16).astype(jnp.float32))
            rest = rest - parts[-1]
        parts.append(jnp.zeros((ROWS, chunk), jnp.float32))
        here = pl.ds(pl.multiple_of(at * chunk, LANES), chunk)
        feat[:, here] = jnp.concatenate(parts, 0).astype(jnp.bfloat16)
        return carry

    lax.fori_loop(0, stars // chunk, feature_chunk, 0)

    wait_landed(first)

    numbers = [s1r[pl.ds(place, SRC, stride=ROWS), :] for place in range(ACT)]
    chosen = [[], []]
    before = jnp.zeros((ROWS, LANES), jnp.int32)
    for place in range(ACT):
        mine = lane_of(numbers[place], 17) == me
        for c in range(CAP):
            chosen[c].append(mine & (before == c))
        before = before + jnp.where(mine, 1, 0)

    def pick(c, values, empty):
        result = empty
        for place in range(ACT):
            result = jnp.where(chosen[c][place], values[place], result)
        return result

    izero = jnp.zeros((ROWS, LANES), jnp.int32)
    detail = [pick(c, numbers, izero) for c in range(CAP)]
    first_star = (me * TGT + my_group) * stars
    offset = [lane_of(detail[c], 16) - first_star for c in range(CAP)]
    count = [lane_of(detail[c], 18) for c in range(CAP)]

    def extract(refs):
        wide = sum(ref.shape[0] for ref in refs)

        def step(block, found):
            rows = [
                row_of(ref, row, block + HALO // BLOCK) for ref in refs for row in range(ref.shape[0])
            ]
            out = []
            for c in range(CAP):
                here = lane + block * BLOCK == offset[c]
                out.append([jnp.where(here, row, old) for row, old in zip(rows, found[c])])
            return out

        found = lax.fori_loop(0, blocks, step, [[zero] * wide for _ in range(CAP)], unroll=8)
        return [
            [
                jnp.broadcast_to(jnp.sum(part, axis=1, keepdims=True), (ROWS, LANES))
                for part in found[c]
            ]
            for c in range(CAP)
        ]

    start = extract((ppos, pvel))

    def spread(values, width):
        slots = []
        for c in range(CAP):
            slot = zero
            for k, value in enumerate(values[c]):
                slot = jnp.where(lax.rem(lane, width) == k, value, slot)
            slots.append(slot)
        result = zero
        for place in range(ACT):
            there = lane // width == place
            for c in range(CAP):
                result = jnp.where(there & chosen[c][place], slots[c], result)
        return result

    s2b[...] = spread(start, 8)
    second = share(1, s2b, s2r)
    s2r[tile_rows(me), :] = s2b[...]

    wait_sent(first)
    raw = extract((wpos, wvel, wacc, wjrk, wela))

    def mask_block(block, carry):
        mass = row_of(wmas, 0, block)
        for c in range(CAP):
            listed = jnp.where((detail[c] == block) & (lane < count[c]), 1.0, 0.0)
            member = jnp.broadcast_to(jnp.sum(listed, axis=1, keepdims=True), (ROWS, LANES))
            itself = lane + block * BLOCK == offset[c] + HALO
            mw[block, c] = jnp.where(itself, 0.0, member * mass)
        return carry

    @pl.when(me > 0)
    def _():
        up.wait_recv()

    @pl.when(me < SRC - 1)
    def _():
        down.wait_recv()

    row = 0
    for hbm, win in arrays:
        height = win.shape[0]
        win[:, 0:HALO] = hland[0, row : row + height]
        win[:, HALO + stars :] = hland[1, row : row + height]
        row += height

    lax.fori_loop(0, window_blocks, mask_block, 0, unroll=4)

    def advance_block(block, carry):
        x = [row_of(wpos, k, block) for k in range(3)]
        v = [row_of(wvel, k, block) for k in range(3)]
        a = [row_of(wacc, k, block) for k in range(3)]
        half = [0.5 * row for row in a]
        j = [row_of(wjrk, k, block) for k in range(3)]
        sixth_j = [row / 6.0 for row in j]
        half_j = [0.5 * row for row in j]
        since = row_of(wela, 0, block)
        for number in range(SUBS):
            for c in range(CAP):
                d = since + (0.25 * (number + 1)) * raw[c][12]
                for k in range(3):
                    moved[number, block, c, k] = x[k] + d * (
                        v[k] + d * (half[k] + d * sixth_j[k])
                    )
                    moved[number, block, c, 3 + k] = v[k] + d * (a[k] + d * half_j[k])
        return carry

    lax.fori_loop(0, window_blocks, advance_block, 0)

    def near_field(targets, number):
        def step(block, sums):
            if number is None:
                source = [row_of(ref, k, block) for ref in (ppos, pvel) for k in range(3)]
                sources = [source] * CAP
            else:
                sources = [[moved[number, block, c, k] for k in range(6)] for c in range(CAP)]
            return [pair_sums(sums[c], targets[c], sources[c], mw[block, c]) for c in range(CAP)]

        sums = lax.fori_loop(0, window_blocks, step, [[zero] * 9 for _ in range(CAP)], unroll=8)
        return [total_of(sums[c]) for c in range(CAP)]

    predict_chunk(0, 0)
    predict_chunk(window_blocks * LANES // chunk - 1, 0)
    inner = near_field(start, None)

    wait_landed(second)

    def gathered(ref):
        total = ref[0:ROWS, :]
        for at in range(1, SRC):
            total = total + ref[at * ROWS : (at + 1) * ROWS, :]
        return total

    group_targets = gathered(s2r)
    s3b[...] = group_targets
    s3r[0] = group_targets
    for code, dz in PAIRS:
        for dc in (1, 0):
            if code or dz or dc:
                pltpu.make_async_remote_copy(
                    src_ref=s3b,
                    dst_ref=s3r.at[code * 4 + dz * 2 + dc],
                    send_sem=tgt_send,
                    recv_sem=tgt_recv.at[code * 2 + dz],
                    device_id=tgt_peer(code, dz, dc),
                    device_id_type=MESH,
                ).start()

    def field(tiles):
        many = len(tiles)
        aims = [
            jnp.concatenate(
                [lane_of(tile, place * 8 + k) for tile in tiles for place in range(ACT)], 0
            )
            for k in range(6)
        ]

        def halves(value):
            high = value.astype(jnp.bfloat16)
            return high, (value - high.astype(jnp.float32)).astype(jnp.bfloat16)

        def step(at, sums):
            columns = []
            for piece in range(PIECES):
                block = at * PIECES + piece
                rows = [wide_row(ppos, k, block + HALO // BLOCK, many) for k in range(3)]
                rows += [wide_row(pvel, k, block + HALO // BLOCK, many) for k in range(3)]
                u = [rows[k] - aims[k] for k in range(3)]
                e = [rows[3 + k] - aims[3 + k] for k in range(3)]
                inverse = lax.rsqrt(u[0] * u[0] + u[1] * u[1] + (u[2] * u[2] + SOFTENING))
                square = inverse * inverse
                weight = inverse * square
                radial = weight * ((u[0] * e[0] + u[1] * e[1] + u[2] * e[2]) * square)
                columns.append(jnp.concatenate(halves(weight) + halves(radial), 0))
            left = jnp.concatenate(columns, 1)
            right = feat[:, pl.ds(pl.multiple_of(at * PIECES * LANES, LANES), PIECES * LANES)]
            return sums + lax.dot_general(
                left, right, (((1,), (1,)), ((), ())), preferred_element_type=jnp.float32
            )

        sums = lax.fori_loop(
            0,
            blocks // PIECES,
            step,
            jnp.zeros((4 * many * ACT * ROWS, 4 * ROWS), jnp.float32),
            unroll=UNROLL,
        )
        blank = jnp.zeros((4 * many * ACT * ROWS, LANES - 4 * ROWS), jnp.float32)
        sums = jnp.concatenate([sums, blank], 1)
        results = []
        for at in range(many):
            for array in range(2):
                tile = zero
                for place in range(ACT):
                    row = ((2 * array * many + at) * ACT + place) * ROWS
                    both = sums[row : row + ROWS] + sums[row + many * ACT * ROWS :][0:ROWS]
                    tile = tile + (pltpu.roll(both, 32 * place, 1) if place else both)
                results.append(tile)
        return results

    def send_sum(at, code, dz, dc):
        pltpu.make_async_remote_copy(
            src_ref=s4b.at[at],
            dst_ref=s4r.at[at],
            send_sem=sum_send,
            recv_sem=sum_recv,
            device_id=tgt_peer(code, dz, dc),
            device_id_type=MESH,
        ).start()

    def group_pair(pair, tables):
        code, dz = lax.rem(tables[0], 4), lax.rem(tables[1], 2)
        other = code + dz > 0
        places = [code * 4 + dz * 2 + dc for dc in (0, 1)]

        @pl.when(other)
        def _():
            wait_bytes(s3r.at[pl.ds(0, 2)], tgt_recv.at[code * 2 + dz])

        @pl.when(jnp.logical_not(other))
        def _():
            wait_bytes(s3r.at[0], tgt_recv.at[code * 2 + dz])

        results = field([s3r[place] for place in places])
        for dc in (1, 0):
            for array in range(2):
                s4b[places[dc], array] = results[2 * dc + array]
        send_sum(places[1], code, dz, 1)

        @pl.when(other)
        def _():
            send_sum(places[0], code, dz, 0)

        @pl.when(jnp.logical_not(other))
        def _():
            for array in range(2):
                s4r[0, array] = results[array]

        return [lax.div(tables[0], 4), lax.div(tables[1], 2)]

    tables = [low + my_z * (high - low) for low, high in (CODE_TABLES, DZ_TABLES)]
    lax.fori_loop(0, len(PAIRS), group_pair, tables)

    aim = group_targets
    for place in range(1, ACT):
        aim = jnp.where(lane // 32 == place, pltpu.roll(group_targets, 24 * place, 1), aim)
    wait_bytes(s4r.at[pl.ds(0, TGT - 1)], sum_recv)
    sides = []
    for array in range(2):
        both = s4r[0, array]
        for at in range(1, TGT):
            both = both + s4r[at, array]
        both = both + pltpu.roll(both, LANES - 8, 1) + pltpu.roll(both, LANES - 16, 1)
        ones = lane_of(both, 6)
        for place in range(1, ACT):
            ones = jnp.where(lane // 32 == place, lane_of(both, 32 * place + 6), ones)
        sides.append(both - aim * ones)
    group_sum = jnp.where(
        lax.rem(lane, 32) < 3, sides[0], sides[0] - 3.0 * pltpu.roll(sides[1], 3, 1)
    )

    s5b[...] = group_sum
    fifth = share(2, s5b, s5r)
    s5r[tile_rows(me), :] = group_sum
    wait_sent(second)
    wait_bytes(s3r.at[pl.ds(0, TGT - 1)], tgt_send)
    wait_bytes(s4r.at[pl.ds(0, TGT - 1)], sum_send)

    @pl.when(me < SRC - 1)
    def _():
        up.wait_send()

    @pl.when(me > 0)
    def _():
        down.wait_send()

    wait_sent(fifth)
    wait_landed(fifth)
    summed = gathered(s5r)
    lanes_of = [[lane_of(summed, place * 32 + k) for place in range(ACT)] for k in range(6)]

    totals = [[pick(c, lanes_of[k], zero) for k in range(6)] for c in range(CAP)]
    states = []
    for c in range(CAP):
        interval = raw[c][12]
        old_pull, old_change = raw[c][6:9], raw[c][9:12]
        regular = [totals[c][k] - inner[c][k] for k in range(6)]
        x, v, snap, crackle = correct(
            start[c][0:3],
            start[c][3:6],
            old_pull,
            old_change,
            totals[c][0:3],
            totals[c][3:6],
            interval,
        )
        states.append((x, v, totals[c][0:3], totals[c][3:6], 0.25 * interval, regular, snap + crackle))
    for number in range(SUBS):
        advance = [states[c][4] * (number + 1) for c in range(CAP)]
        guesses = [predict(*states[c][0:5]) for c in range(CAP)]
        inner = near_field([x + v for x, v in guesses], number)
        after = []
        for c in range(CAP):
            x, v, pull, change, substep, regular, rest = states[c]
            new_pull = [
                regular[k] + advance[c] * regular[3 + k] + inner[c][k] for k in range(3)
            ]
            new_change = [regular[3 + k] + inner[c][3 + k] for k in range(3)]
            x, v, unused, ignored = correct(
                guesses[c][0], guesses[c][1], pull, change, new_pull, new_change, substep
            )
            after.append((x, v, new_pull, new_change, substep, regular, rest))
        states = after

    results = [
        states[c][0] + states[c][1] + states[c][5] + inner[c] + states[c][6] for c in range(CAP)
    ]
    s6b[...] = spread(results, 32)
    sixth = share(3, s6b, s6r)
    s6r[tile_rows(me), :] = s6b[...]
    wait_landed(sixth)
    mine = jnp.sum(s6r[pl.ds(me, SRC, stride=ROWS), :], axis=0, keepdims=True)
    mine = jnp.broadcast_to(mine, (ROWS, LANES))
    shifted = mine
    for place in range(1, ACT):
        shifted = jnp.where(sub == place, pltpu.roll(mine, LANES - 32 * place, 1), shifted)
    o_all[...] = shifted[0:ACT, :]

    wait_sent(sixth)


def cut(result, state, fields, taylor):
    state[...] = result[:, 0:6]
    fields[...] = result[:, 6:18]
    taylor[...] = result[:, 18:24]


def shards(
    positions,
    velocities,
    accelerations,
    jerk_terms,
    masses,
    elapsed,
    active_idx,
    owners,
    counts,
    block_lists,
):
    stars = positions.shape[1]
    window = stars + 2 * HALO
    hbm = pl.BlockSpec(memory_space=pl.ANY)
    vmem = pl.BlockSpec(memory_space=pltpu.VMEM)
    tile = pltpu.VMEM((ROWS, LANES), jnp.float32)
    landed = pltpu.VMEM((SRC * ROWS, LANES), jnp.float32)
    groups = pltpu.VMEM((TGT, ROWS, LANES), jnp.float32)
    sums = pltpu.VMEM((TGT, 2, ROWS, LANES), jnp.float32)
    itile = pltpu.VMEM((ROWS, LANES), jnp.int32)
    ilanded = pltpu.VMEM((SRC * ROWS, LANES), jnp.int32)
    three = pltpu.VMEM((3, window), jnp.float32)
    one = pltpu.VMEM((1, window), jnp.float32)
    dma = pltpu.SemaphoreType.DMA
    result = pl.pallas_call(
        kernel,
        out_shape=pltpu.VMEM((ACT, LANES), jnp.float32),
        in_specs=[hbm] * 10,
        out_specs=vmem,
        scratch_shapes=[
            three, three, three, three, one, one, three, three,
            pltpu.VMEM((4 * ROWS, stars), jnp.bfloat16),
            pltpu.VMEM((window // BLOCK, CAP, ROWS, LANES), jnp.float32),
            pltpu.VMEM((SUBS, window // BLOCK, CAP, 6, ROWS, LANES), jnp.float32),
            itile, ilanded, tile, landed, tile, groups, sums, sums, tile, landed, tile, landed,
            pltpu.VMEM((2, 14, HALO), jnp.float32), pltpu.VMEM((2, 14, HALO), jnp.float32),
            pltpu.SMEM((ACT,), jnp.int32), pltpu.SMEM((ACT,), jnp.int32), pltpu.SMEM((ACT,), jnp.int32),
            pltpu.VMEM((ACT, 16), jnp.int32),
            dma((6,)), dma((4,)), dma((2,)), dma((2,)), dma((4,)), dma((4,)),
            dma, dma((len(PAIRS),)), dma, dma,
        ],
        compiler_params=pltpu.CompilerParams(collective_id=0, has_side_effects=True),
    )(
        positions,
        velocities,
        accelerations,
        jerk_terms,
        masses[None],
        elapsed[None],
        active_idx,
        owners,
        counts,
        block_lists,
    )
    state, fields, taylor = pl.pallas_call(
        cut,
        out_shape=(
            jax.ShapeDtypeStruct((ACT, 6), jnp.float32),
            jax.ShapeDtypeStruct((ACT, 12), jnp.float32),
            jax.ShapeDtypeStruct((ACT, 6), jnp.float32),
        ),
        in_specs=[vmem],
        out_specs=(vmem, vmem, vmem),
    )(pltpu.with_memory_space_constraint(result, pltpu.VMEM))
    return state.T, fields.T, taylor.T


def solution(mesh):
    in_specs = (
        P(None, ("src", "tgt")),
        P(None, ("src", "tgt")),
        P(None, ("src", "tgt")),
        P(None, ("src", "tgt")),
        P(("src", "tgt")),
        P(("src", "tgt")),
        P(("src", "tgt")),
        P(("src", "tgt")),
        P(("src", "tgt")),
        P(("src", "tgt"), None),
    )
    out_specs = (P(None, ("src", "tgt")), P(None, ("src", "tgt")), P(None, ("src", "tgt")))
    return jax.shard_map(shards, mesh=mesh, in_specs=in_specs, out_specs=out_specs, check_vma=False)
```

```python
import jax
import jax.numpy as jnp
from jax import lax
from jax.experimental import pallas as pl
from jax.experimental.pallas import tpu as pltpu
from jax.sharding import PartitionSpec as P

LANES = 128
ROWS = 8
BLOCK = 128
HALO = 4 * BLOCK
SUBS = 2
CAP = 2
ACT = 4
SRC = 8
TGT = 16
SOFTENING = 0.0001
PIECES = 4
UNROLL = 8
MESH = pl.DeviceIdType.MESH
ORDERS = (
    ((0, 0), (1, 0), (2, 0), (3, 0), (2, 1), (3, 1), (1, 1), (0, 1)),
    ((0, 1), (1, 1), (2, 1), (3, 1), (2, 0), (3, 0), (1, 0), (0, 0)),
)
CODE_TABLES = [sum(code * 4**at for at, (code, dz) in enumerate(order)) for order in ORDERS]
DZ_TABLES = [sum(dz * 2**at for at, (code, dz) in enumerate(order)) for order in ORDERS]
PAIRS = ORDERS[1]


def predict(position, velocity, acceleration, jerk_now, interval):
    new_position = [
        x + interval * (v + interval * (0.5 * a + interval * j / 6.0))
        for x, v, a, j in zip(position, velocity, acceleration, jerk_now)
    ]
    new_velocity = [
        v + interval * (a + 0.5 * interval * j)
        for v, a, j in zip(velocity, acceleration, jerk_now)
    ]
    return new_position, new_velocity


def correct(position, velocity, old_pull, old_change, new_pull, new_change, interval):
    new_position, new_velocity, snaps, crackles = [], [], [], []
    for x, v, a0, j0, a1, j1 in zip(
        position, velocity, old_pull, old_change, new_pull, new_change
    ):
        jump = a0 - a1
        snap = -6.0 * jump - interval * (4.0 * j0 + 2.0 * j1)
        crackle = 12.0 * jump + 6.0 * interval * (j0 + j1)
        new_position.append(x + interval * interval * (snap / 24.0 + crackle / 120.0))
        new_velocity.append(v + interval * (snap / 6.0 + crackle / 24.0))
        snaps.append(snap)
        crackles.append(crackle)
    return new_position, new_velocity, snaps, crackles


def pair_sums(sums, target, source, mass):
    u = [source[k] - target[k] for k in range(3)]
    e = [source[3 + k] - target[3 + k] for k in range(3)]
    distance = u[0] * u[0] + u[1] * u[1] + (u[2] * u[2] + SOFTENING)
    inverse = lax.rsqrt(distance)
    square = inverse * inverse
    weight = (mass * inverse) * square
    radial = (u[0] * e[0] + u[1] * e[1] + u[2] * e[2]) * square
    pull = [weight * u[k] for k in range(3)]
    return (
        [sums[k] + pull[k] for k in range(3)]
        + [sums[3 + k] + weight * e[k] for k in range(3)]
        + [sums[6 + k] + radial * pull[k] for k in range(3)]
    )


def total_of(sums):
    six = sums[0:3] + [sums[3 + k] - 3.0 * sums[6 + k] for k in range(3)]
    return [
        jnp.broadcast_to(jnp.sum(part, axis=1, keepdims=True), (ROWS, LANES)) for part in six
    ]


def lane_of(tile, lane):
    return jnp.broadcast_to(tile[:, lane : lane + 1], (ROWS, LANES))


def wide_row(ref, row, block, many):
    lanes = pl.ds(pl.multiple_of(block * LANES, LANES), LANES)
    return jnp.broadcast_to(ref[row : row + 1, lanes], (many * ACT * ROWS, LANES))


def row_of(ref, row, block):
    lanes = pl.ds(pl.multiple_of(block * LANES, LANES), LANES)
    return jnp.broadcast_to(ref[row : row + 1, lanes], (ROWS, LANES))


def kernel(
    pos, vel, acc, jrk, mas, ela, idx, own, cnt, lists,
    o_all,
    wpos, wvel, wacc, wjrk, wmas, wela, ppos, pvel, feat, mw, moved,
    s1b, s1r, s2b, s2r, s3b, s3r, s4b, s4r, s5b, s5r, s6b, s6r,
    hsend, hland, idx_here, own_here, cnt_here, lists_here,
    load_sem, number_sem, halo_send, halo_recv, src_send, src_recv, tgt_send, tgt_recv, sum_send, sum_recv,
):
    stars = pos.shape[1]
    blocks = stars // BLOCK
    window_blocks = wpos.shape[1] // BLOCK
    me = lax.axis_index("src")
    my_group = lax.axis_index("tgt")
    my_x, my_z, my_core = my_group // 4, (my_group // 2) % 2, my_group % 2

    def src_peer(step):
        return {"src": lax.rem(me + step, SRC)}

    def tgt_peer(code, dz, dc):
        x = lax.rem(my_x + code * (1 + 2 * lax.rem(my_x, 2)), 4)
        z, core = lax.rem(my_z + dz, 2), lax.rem(my_core + dc, 2)
        return {"tgt": x * 4 + z * 2 + core}

    def tile_rows(at):
        return pl.ds(pl.multiple_of(at * ROWS, ROWS), ROWS)

    lane = lax.broadcasted_iota(jnp.int32, (ROWS, LANES), 1)
    sub = lax.broadcasted_iota(jnp.int32, (ROWS, LANES), 0)
    zero = jnp.zeros((ROWS, LANES), jnp.float32)

    barrier = pltpu.get_barrier_semaphore()
    for step in (4, 3, 5, 2, 6, 1, 7):
        pl.semaphore_signal(barrier, inc=1, device_id=src_peer(step), device_id_type=MESH)
    for code, dz in PAIRS:
        for dc in (1, 0):
            if code or dz or dc:
                pl.semaphore_signal(
                    barrier, inc=1, device_id=tgt_peer(code, dz, dc), device_id_type=MESH
                )

    numbered = ((idx, idx_here), (own, own_here), (cnt, cnt_here), (lists, lists_here))
    number_loads = [
        pltpu.make_async_copy(hbm, here, number_sem.at[at])
        for at, (hbm, here) in enumerate(numbered)
    ]
    for load in number_loads:
        load.start()

    arrays = ((pos, wpos), (vel, wvel), (acc, wacc), (jrk, wjrk), (mas, wmas), (ela, wela))
    loads = [
        pltpu.make_async_copy(hbm, win.at[:, HALO : HALO + stars], load_sem.at[at])
        for at, (hbm, win) in enumerate(arrays)
    ]
    for load in loads:
        load.start()
    for load in number_loads:
        load.wait()

    tile = jnp.zeros((ROWS, LANES), jnp.int32)
    for place in range(ACT):
        for at, ref in enumerate((idx_here, own_here, cnt_here)):
            tile = jnp.where((sub == place) & (lane == 16 + at), ref[place], tile)
    s1b[...] = tile
    s1b[0:ACT, 0:16] = lists_here[...]

    pl.semaphore_wait(barrier, SRC + TGT - 2)

    def share(stage, sent, landed):
        for step in (4, 3, 5, 2, 6, 1, 7):
            pltpu.make_async_remote_copy(
                src_ref=sent,
                dst_ref=landed.at[tile_rows(me), :],
                send_sem=src_send.at[stage],
                recv_sem=src_recv.at[stage],
                device_id=src_peer(step),
                device_id_type=MESH,
            ).start()
        return stage, landed

    def wait_bytes(ref, semaphore):
        pltpu.make_async_copy(ref, ref, semaphore).wait()

    def wait_sent(shared):
        stage, landed = shared
        wait_bytes(landed.at[0 : (SRC - 1) * ROWS], src_send.at[stage])

    def wait_landed(shared):
        stage, landed = shared
        wait_bytes(landed.at[0 : (SRC - 1) * ROWS], src_recv.at[stage])

    first = share(0, s1b, s1r)
    s1r[tile_rows(me), :] = s1b[...]

    for load in loads:
        load.wait()

    up = pltpu.make_async_remote_copy(
        src_ref=hsend.at[0],
        dst_ref=hland.at[0],
        send_sem=halo_send.at[0],
        recv_sem=halo_recv.at[0],
        device_id={"src": lax.rem(me + 1, SRC)},
        device_id_type=MESH,
    )
    down = pltpu.make_async_remote_copy(
        src_ref=hsend.at[1],
        dst_ref=hland.at[1],
        send_sem=halo_send.at[1],
        recv_sem=halo_recv.at[1],
        device_id={"src": lax.rem(me + SRC - 1, SRC)},
        device_id_type=MESH,
    )
    row = 0
    for hbm, win in arrays:
        height = win.shape[0]
        hsend[0, row : row + height] = win[:, stars : stars + HALO]
        hsend[1, row : row + height] = win[:, HALO : 2 * HALO]
        row += height

    @pl.when(me < SRC - 1)
    def _():
        up.start()

    @pl.when(me > 0)
    def _():
        down.start()

    @pl.when(me == 0)
    def _():
        hland[0] = jnp.zeros(hland.shape[1:], jnp.float32)

    @pl.when(me == SRC - 1)
    def _():
        hland[1] = jnp.zeros(hland.shape[1:], jnp.float32)

    chunk = 4 * LANES

    def predict_chunk(at, carry):
        there = pl.ds(pl.multiple_of(at * chunk, LANES), chunk)
        (place,), (speed,) = predict(
            [wpos[:, there]], [wvel[:, there]], [wacc[:, there]], [wjrk[:, there]], wela[:, there]
        )
        ppos[:, there] = place
        pvel[:, there] = speed
        return carry

    lax.fori_loop(1, 1 + stars // chunk, predict_chunk, 0)

    def feature_chunk(at, carry):
        there = pl.ds(pl.multiple_of(HALO + at * chunk, LANES), chunk)
        wide = lax.broadcasted_iota(jnp.int32, (ROWS, chunk), 0)
        mass = jnp.broadcast_to(wmas[:, there], (ROWS, chunk))
        rest = jnp.where(wide == 6, mass, 0.0)
        for k in range(3):
            x = jnp.broadcast_to(ppos[k : k + 1, there], (ROWS, chunk))
            v = jnp.broadcast_to(pvel[k : k + 1, there], (ROWS, chunk))
            rest = jnp.where(wide == k, mass * x, jnp.where(wide == 3 + k, mass * v, rest))
        parts = []
        for part in range(3):
            parts.append(rest.astype(jnp.bfloat16).astype(jnp.float32))
            rest = rest - parts[-1]
        parts.append(jnp.zeros((ROWS, chunk), jnp.float32))
        here = pl.ds(pl.multiple_of(at * chunk, LANES), chunk)
        feat[:, here] = jnp.concatenate(parts, 0).astype(jnp.bfloat16)
        return carry

    lax.fori_loop(0, stars // chunk, feature_chunk, 0)

    wait_landed(first)

    numbers = [s1r[pl.ds(place, SRC, stride=ROWS), :] for place in range(ACT)]
    chosen = [[], []]
    before = jnp.zeros((ROWS, LANES), jnp.int32)
    for place in range(ACT):
        mine = lane_of(numbers[place], 17) == me
        for c in range(CAP):
            chosen[c].append(mine & (before == c))
        before = before + jnp.where(mine, 1, 0)

    def pick(c, values, empty):
        result = empty
        for place in range(ACT):
            result = jnp.where(chosen[c][place], values[place], result)
        return result

    izero = jnp.zeros((ROWS, LANES), jnp.int32)
    detail = [pick(c, numbers, izero) for c in range(CAP)]
    first_star = (me * TGT + my_group) * stars
    offset = [lane_of(detail[c], 16) - first_star for c in range(CAP)]
    count = [lane_of(detail[c], 18) for c in range(CAP)]

    def extract(refs):
        wide = sum(ref.shape[0] for ref in refs)

        def step(block, found):
            rows = [
                row_of(ref, row, block + HALO // BLOCK) for ref in refs for row in range(ref.shape[0])
            ]
            out = []
            for c in range(CAP):
                here = lane + block * BLOCK == offset[c]
                out.append([jnp.where(here, row, old) for row, old in zip(rows, found[c])])
            return out

        found = lax.fori_loop(0, blocks, step, [[zero] * wide for _ in range(CAP)], unroll=8)
        return [
            [
                jnp.broadcast_to(jnp.sum(part, axis=1, keepdims=True), (ROWS, LANES))
                for part in found[c]
            ]
            for c in range(CAP)
        ]

    start = extract((ppos, pvel))

    def spread(values, width):
        slots = []
        for c in range(CAP):
            slot = zero
            for k, value in enumerate(values[c]):
                slot = jnp.where(lax.rem(lane, width) == k, value, slot)
            slots.append(slot)
        result = zero
        for place in range(ACT):
            there = lane // width == place
            for c in range(CAP):
                result = jnp.where(there & chosen[c][place], slots[c], result)
        return result

    s2b[...] = spread(start, 8)
    second = share(1, s2b, s2r)
    s2r[tile_rows(me), :] = s2b[...]

    wait_sent(first)
    raw = extract((wpos, wvel, wacc, wjrk, wela))

    def mask_block(block, carry):
        mass = row_of(wmas, 0, block)
        for c in range(CAP):
            listed = jnp.where((detail[c] == block) & (lane < count[c]), 1.0, 0.0)
            member = jnp.broadcast_to(jnp.sum(listed, axis=1, keepdims=True), (ROWS, LANES))
            itself = lane + block * BLOCK == offset[c] + HALO
            mw[block, c] = jnp.where(itself, 0.0, member * mass)
        return carry

    @pl.when(me > 0)
    def _():
        up.wait_recv()

    @pl.when(me < SRC - 1)
    def _():
        down.wait_recv()

    row = 0
    for hbm, win in arrays:
        height = win.shape[0]
        win[:, 0:HALO] = hland[0, row : row + height]
        win[:, HALO + stars :] = hland[1, row : row + height]
        row += height

    lax.fori_loop(0, window_blocks, mask_block, 0, unroll=4)

    def advance_block(block, carry):
        x = [row_of(wpos, k, block) for k in range(3)]
        v = [row_of(wvel, k, block) for k in range(3)]
        a = [row_of(wacc, k, block) for k in range(3)]
        half = [0.5 * row for row in a]
        j = [row_of(wjrk, k, block) for k in range(3)]
        sixth_j = [row / 6.0 for row in j]
        half_j = [0.5 * row for row in j]
        since = row_of(wela, 0, block)
        for number in range(SUBS):
            for c in range(CAP):
                d = since + (0.25 * (number + 1)) * raw[c][12]
                for k in range(3):
                    moved[number, block, c, k] = x[k] + d * (
                        v[k] + d * (half[k] + d * sixth_j[k])
                    )
                    moved[number, block, c, 3 + k] = v[k] + d * (a[k] + d * half_j[k])
        return carry

    lax.fori_loop(0, window_blocks, advance_block, 0)

    def near_field(targets, number):
        def step(block, sums):
            if number is None:
                source = [row_of(ref, k, block) for ref in (ppos, pvel) for k in range(3)]
                sources = [source] * CAP
            else:
                sources = [[moved[number, block, c, k] for k in range(6)] for c in range(CAP)]
            return [pair_sums(sums[c], targets[c], sources[c], mw[block, c]) for c in range(CAP)]

        sums = lax.fori_loop(0, window_blocks, step, [[zero] * 9 for _ in range(CAP)], unroll=True)
        return [total_of(sums[c]) for c in range(CAP)]

    predict_chunk(0, 0)
    predict_chunk(window_blocks * LANES // chunk - 1, 0)
    inner = near_field(start, None)

    wait_landed(second)

    def gathered(ref):
        total = ref[0:ROWS, :]
        for at in range(1, SRC):
            total = total + ref[at * ROWS : (at + 1) * ROWS, :]
        return total

    group_targets = gathered(s2r)
    s3b[...] = group_targets
    s3r[0] = group_targets
    for code, dz in PAIRS:
        for dc in (1, 0):
            if code or dz or dc:
                pltpu.make_async_remote_copy(
                    src_ref=s3b,
                    dst_ref=s3r.at[code * 4 + dz * 2 + dc],
                    send_sem=tgt_send,
                    recv_sem=tgt_recv.at[code * 2 + dz],
                    device_id=tgt_peer(code, dz, dc),
                    device_id_type=MESH,
                ).start()

    def field(tiles):
        many = len(tiles)
        aims = [
            jnp.concatenate(
                [lane_of(tile, place * 8 + k) for tile in tiles for place in range(ACT)], 0
            )
            for k in range(6)
        ]

        def halves(value):
            high = value.astype(jnp.bfloat16)
            return high, (value - high.astype(jnp.float32)).astype(jnp.bfloat16)

        def step(at, sums):
            columns = []
            for piece in range(PIECES):
                block = at * PIECES + piece
                rows = [wide_row(ppos, k, block + HALO // BLOCK, many) for k in range(3)]
                rows += [wide_row(pvel, k, block + HALO // BLOCK, many) for k in range(3)]
                u = [rows[k] - aims[k] for k in range(3)]
                e = [rows[3 + k] - aims[3 + k] for k in range(3)]
                inverse = lax.rsqrt(u[0] * u[0] + u[1] * u[1] + (u[2] * u[2] + SOFTENING))
                square = inverse * inverse
                weight = inverse * square
                radial = weight * ((u[0] * e[0] + u[1] * e[1] + u[2] * e[2]) * square)
                columns.append(jnp.concatenate(halves(weight) + halves(radial), 0))
            left = jnp.concatenate(columns, 1)
            right = feat[:, pl.ds(pl.multiple_of(at * PIECES * LANES, LANES), PIECES * LANES)]
            return sums + lax.dot_general(
                left, right, (((1,), (1,)), ((), ())), preferred_element_type=jnp.float32
            )

        sums = lax.fori_loop(
            0,
            blocks // PIECES,
            step,
            jnp.zeros((4 * many * ACT * ROWS, 4 * ROWS), jnp.float32),
            unroll=UNROLL,
        )
        blank = jnp.zeros((4 * many * ACT * ROWS, LANES - 4 * ROWS), jnp.float32)
        sums = jnp.concatenate([sums, blank], 1)
        results = []
        for at in range(many):
            for array in range(2):
                tile = zero
                for place in range(ACT):
                    row = ((2 * array * many + at) * ACT + place) * ROWS
                    both = sums[row : row + ROWS] + sums[row + many * ACT * ROWS :][0:ROWS]
                    tile = tile + (pltpu.roll(both, 32 * place, 1) if place else both)
                results.append(tile)
        return results

    def send_sum(at, code, dz, dc):
        pltpu.make_async_remote_copy(
            src_ref=s4b.at[at],
            dst_ref=s4r.at[at],
            send_sem=sum_send,
            recv_sem=sum_recv,
            device_id=tgt_peer(code, dz, dc),
            device_id_type=MESH,
        ).start()

    def group_pair(pair, tables):
        code, dz = lax.rem(tables[0], 4), lax.rem(tables[1], 2)
        other = code + dz > 0
        places = [code * 4 + dz * 2 + dc for dc in (0, 1)]

        @pl.when(other)
        def _():
            wait_bytes(s3r.at[pl.ds(0, 2)], tgt_recv.at[code * 2 + dz])

        @pl.when(jnp.logical_not(other))
        def _():
            wait_bytes(s3r.at[0], tgt_recv.at[code * 2 + dz])

        results = field([s3r[place] for place in places])
        for dc in (1, 0):
            for array in range(2):
                s4b[places[dc], array] = results[2 * dc + array]
        send_sum(places[1], code, dz, 1)

        @pl.when(other)
        def _():
            send_sum(places[0], code, dz, 0)

        @pl.when(jnp.logical_not(other))
        def _():
            for array in range(2):
                s4r[0, array] = results[array]

        return [lax.div(tables[0], 4), lax.div(tables[1], 2)]

    tables = [low + my_z * (high - low) for low, high in (CODE_TABLES, DZ_TABLES)]
    lax.fori_loop(0, len(PAIRS), group_pair, tables)

    aim = group_targets
    for place in range(1, ACT):
        aim = jnp.where(lane // 32 == place, pltpu.roll(group_targets, 24 * place, 1), aim)
    wait_bytes(s4r.at[pl.ds(0, TGT - 1)], sum_recv)
    sides = []
    for array in range(2):
        both = s4r[0, array]
        for at in range(1, TGT):
            both = both + s4r[at, array]
        both = both + pltpu.roll(both, LANES - 8, 1) + pltpu.roll(both, LANES - 16, 1)
        ones = lane_of(both, 6)
        for place in range(1, ACT):
            ones = jnp.where(lane // 32 == place, lane_of(both, 32 * place + 6), ones)
        sides.append(both - aim * ones)
    group_sum = jnp.where(
        lax.rem(lane, 32) < 3, sides[0], sides[0] - 3.0 * pltpu.roll(sides[1], 3, 1)
    )

    s5b[...] = group_sum
    fifth = share(2, s5b, s5r)
    s5r[tile_rows(me), :] = group_sum
    wait_sent(second)
    wait_bytes(s3r.at[pl.ds(0, TGT - 1)], tgt_send)
    wait_bytes(s4r.at[pl.ds(0, TGT - 1)], sum_send)

    @pl.when(me < SRC - 1)
    def _():
        up.wait_send()

    @pl.when(me > 0)
    def _():
        down.wait_send()

    wait_sent(fifth)
    wait_landed(fifth)
    summed = gathered(s5r)
    lanes_of = [[lane_of(summed, place * 32 + k) for place in range(ACT)] for k in range(6)]

    totals = [[pick(c, lanes_of[k], zero) for k in range(6)] for c in range(CAP)]
    states = []
    for c in range(CAP):
        interval = raw[c][12]
        old_pull, old_change = raw[c][6:9], raw[c][9:12]
        regular = [totals[c][k] - inner[c][k] for k in range(6)]
        x, v, snap, crackle = correct(
            start[c][0:3],
            start[c][3:6],
            old_pull,
            old_change,
            totals[c][0:3],
            totals[c][3:6],
            interval,
        )
        states.append((x, v, totals[c][0:3], totals[c][3:6], 0.25 * interval, regular, snap + crackle))
    for number in range(SUBS):
        advance = [states[c][4] * (number + 1) for c in range(CAP)]
        guesses = [predict(*states[c][0:5]) for c in range(CAP)]
        inner = near_field([x + v for x, v in guesses], number)
        after = []
        for c in range(CAP):
            x, v, pull, change, substep, regular, rest = states[c]
            new_pull = [
                regular[k] + advance[c] * regular[3 + k] + inner[c][k] for k in range(3)
            ]
            new_change = [regular[3 + k] + inner[c][3 + k] for k in range(3)]
            x, v, unused, ignored = correct(
                guesses[c][0], guesses[c][1], pull, change, new_pull, new_change, substep
            )
            after.append((x, v, new_pull, new_change, substep, regular, rest))
        states = after

    results = [
        states[c][0] + states[c][1] + states[c][5] + inner[c] + states[c][6] for c in range(CAP)
    ]
    s6b[...] = spread(results, 32)
    sixth = share(3, s6b, s6r)
    s6r[tile_rows(me), :] = s6b[...]
    wait_landed(sixth)
    mine = jnp.sum(s6r[pl.ds(me, SRC, stride=ROWS), :], axis=0, keepdims=True)
    mine = jnp.broadcast_to(mine, (ROWS, LANES))
    shifted = mine
    for place in range(1, ACT):
        shifted = jnp.where(sub == place, pltpu.roll(mine, LANES - 32 * place, 1), shifted)
    o_all[...] = shifted[0:ACT, :]

    wait_sent(sixth)


def cut(result, state, fields, taylor):
    state[...] = result[:, 0:6]
    fields[...] = result[:, 6:18]
    taylor[...] = result[:, 18:24]


def shards(
    positions,
    velocities,
    accelerations,
    jerk_terms,
    masses,
    elapsed,
    active_idx,
    owners,
    counts,
    block_lists,
):
    stars = positions.shape[1]
    window = stars + 2 * HALO
    hbm = pl.BlockSpec(memory_space=pl.ANY)
    vmem = pl.BlockSpec(memory_space=pltpu.VMEM)
    tile = pltpu.VMEM((ROWS, LANES), jnp.float32)
    landed = pltpu.VMEM((SRC * ROWS, LANES), jnp.float32)
    groups = pltpu.VMEM((TGT, ROWS, LANES), jnp.float32)
    sums = pltpu.VMEM((TGT, 2, ROWS, LANES), jnp.float32)
    itile = pltpu.VMEM((ROWS, LANES), jnp.int32)
    ilanded = pltpu.VMEM((SRC * ROWS, LANES), jnp.int32)
    three = pltpu.VMEM((3, window), jnp.float32)
    one = pltpu.VMEM((1, window), jnp.float32)
    dma = pltpu.SemaphoreType.DMA
    result = pl.pallas_call(
        kernel,
        out_shape=pltpu.VMEM((ACT, LANES), jnp.float32),
        in_specs=[hbm] * 10,
        out_specs=vmem,
        scratch_shapes=[
            three, three, three, three, one, one, three, three,
            pltpu.VMEM((4 * ROWS, stars), jnp.bfloat16),
            pltpu.VMEM((window // BLOCK, CAP, ROWS, LANES), jnp.float32),
            pltpu.VMEM((SUBS, window // BLOCK, CAP, 6, ROWS, LANES), jnp.float32),
            itile, ilanded, tile, landed, tile, groups, sums, sums, tile, landed, tile, landed,
            pltpu.VMEM((2, 14, HALO), jnp.float32), pltpu.VMEM((2, 14, HALO), jnp.float32),
            pltpu.SMEM((ACT,), jnp.int32), pltpu.SMEM((ACT,), jnp.int32), pltpu.SMEM((ACT,), jnp.int32),
            pltpu.VMEM((ACT, 16), jnp.int32),
            dma((6,)), dma((4,)), dma((2,)), dma((2,)), dma((4,)), dma((4,)),
            dma, dma((len(PAIRS),)), dma, dma,
        ],
        compiler_params=pltpu.CompilerParams(collective_id=0, has_side_effects=True),
    )(
        positions,
        velocities,
        accelerations,
        jerk_terms,
        masses[None],
        elapsed[None],
        active_idx,
        owners,
        counts,
        block_lists,
    )
    state, fields, taylor = pl.pallas_call(
        cut,
        out_shape=(
            jax.ShapeDtypeStruct((ACT, 6), jnp.float32),
            jax.ShapeDtypeStruct((ACT, 12), jnp.float32),
            jax.ShapeDtypeStruct((ACT, 6), jnp.float32),
        ),
        in_specs=[vmem],
        out_specs=(vmem, vmem, vmem),
    )(pltpu.with_memory_space_constraint(result, pltpu.VMEM))
    return state.T, fields.T, taylor.T


def solution(mesh):
    in_specs = (
        P(None, ("src", "tgt")),
        P(None, ("src", "tgt")),
        P(None, ("src", "tgt")),
        P(None, ("src", "tgt")),
        P(("src", "tgt")),
        P(("src", "tgt")),
        P(("src", "tgt")),
        P(("src", "tgt")),
        P(("src", "tgt")),
        P(("src", "tgt"), None),
    )
    out_specs = (P(None, ("src", "tgt")), P(None, ("src", "tgt")), P(None, ("src", "tgt")))
    return jax.shard_map(shards, mesh=mesh, in_specs=in_specs, out_specs=out_specs, check_vma=False)
```

```python
import jax
import jax.numpy as jnp
from jax import lax
from jax.experimental import pallas as pl
from jax.experimental.pallas import tpu as pltpu
from jax.sharding import PartitionSpec as P

LANES = 128
ROWS = 8
BLOCK = 128
HALO = 4 * BLOCK
SUBS = 2
CAP = 2
ACT = 4
SRC = 8
TGT = 16
SOFTENING = 0.0001
PIECES = 4
UNROLL = 8
MESH = pl.DeviceIdType.MESH
ORDERS = (
    ((0, 0), (1, 0), (2, 0), (3, 0), (2, 1), (3, 1), (1, 1), (0, 1)),
    ((0, 1), (1, 1), (3, 1), (2, 1), (3, 0), (2, 0), (1, 0), (0, 0)),
)
CODE_TABLES = [sum(code * 4**at for at, (code, dz) in enumerate(order)) for order in ORDERS]
DZ_TABLES = [sum(dz * 2**at for at, (code, dz) in enumerate(order)) for order in ORDERS]
PAIRS = ORDERS[1]


def predict(position, velocity, acceleration, jerk_now, interval):
    new_position = [
        x + interval * (v + interval * (0.5 * a + interval * j / 6.0))
        for x, v, a, j in zip(position, velocity, acceleration, jerk_now)
    ]
    new_velocity = [
        v + interval * (a + 0.5 * interval * j)
        for v, a, j in zip(velocity, acceleration, jerk_now)
    ]
    return new_position, new_velocity


def correct(position, velocity, old_pull, old_change, new_pull, new_change, interval):
    new_position, new_velocity, snaps, crackles = [], [], [], []
    for x, v, a0, j0, a1, j1 in zip(
        position, velocity, old_pull, old_change, new_pull, new_change
    ):
        jump = a0 - a1
        snap = -6.0 * jump - interval * (4.0 * j0 + 2.0 * j1)
        crackle = 12.0 * jump + 6.0 * interval * (j0 + j1)
        new_position.append(x + interval * interval * (snap / 24.0 + crackle / 120.0))
        new_velocity.append(v + interval * (snap / 6.0 + crackle / 24.0))
        snaps.append(snap)
        crackles.append(crackle)
    return new_position, new_velocity, snaps, crackles


def pair_sums(sums, target, source, mass):
    u = [source[k] - target[k] for k in range(3)]
    e = [source[3 + k] - target[3 + k] for k in range(3)]
    distance = u[0] * u[0] + u[1] * u[1] + (u[2] * u[2] + SOFTENING)
    inverse = lax.rsqrt(distance)
    square = inverse * inverse
    weight = (mass * inverse) * square
    radial = (u[0] * e[0] + u[1] * e[1] + u[2] * e[2]) * square
    pull = [weight * u[k] for k in range(3)]
    return (
        [sums[k] + pull[k] for k in range(3)]
        + [sums[3 + k] + weight * e[k] for k in range(3)]
        + [sums[6 + k] + radial * pull[k] for k in range(3)]
    )


def total_of(sums):
    six = sums[0:3] + [sums[3 + k] - 3.0 * sums[6 + k] for k in range(3)]
    return [
        jnp.broadcast_to(jnp.sum(part, axis=1, keepdims=True), (ROWS, LANES)) for part in six
    ]


def lane_of(tile, lane):
    return jnp.broadcast_to(tile[:, lane : lane + 1], (ROWS, LANES))


def wide_row(ref, row, block, many):
    lanes = pl.ds(pl.multiple_of(block * LANES, LANES), LANES)
    return jnp.broadcast_to(ref[row : row + 1, lanes], (many * ACT * ROWS, LANES))


def row_of(ref, row, block):
    lanes = pl.ds(pl.multiple_of(block * LANES, LANES), LANES)
    return jnp.broadcast_to(ref[row : row + 1, lanes], (ROWS, LANES))


def kernel(
    pos, vel, acc, jrk, mas, ela, idx, own, cnt, lists,
    o_all,
    wpos, wvel, wacc, wjrk, wmas, wela, ppos, pvel, feat, mw, moved,
    s1b, s1r, s2b, s2r, s3b, s3r, s4b, s4r, s5b, s5r, s6b, s6r,
    hsend, hland, idx_here, own_here, cnt_here, lists_here,
    load_sem, number_sem, halo_send, halo_recv, src_send, src_recv, tgt_send, tgt_recv, sum_send, sum_recv,
):
    stars = pos.shape[1]
    blocks = stars // BLOCK
    window_blocks = wpos.shape[1] // BLOCK
    me = lax.axis_index("src")
    my_group = lax.axis_index("tgt")
    my_x, my_z, my_core = my_group // 4, (my_group // 2) % 2, my_group % 2

    def src_peer(step):
        return {"src": lax.rem(me + step, SRC)}

    def tgt_peer(code, dz, dc):
        x = lax.rem(my_x + code * (1 + 2 * lax.rem(my_x, 2)), 4)
        z, core = lax.rem(my_z + dz, 2), lax.rem(my_core + dc, 2)
        return {"tgt": x * 4 + z * 2 + core}

    def tile_rows(at):
        return pl.ds(pl.multiple_of(at * ROWS, ROWS), ROWS)

    lane = lax.broadcasted_iota(jnp.int32, (ROWS, LANES), 1)
    sub = lax.broadcasted_iota(jnp.int32, (ROWS, LANES), 0)
    zero = jnp.zeros((ROWS, LANES), jnp.float32)

    barrier = pltpu.get_barrier_semaphore()
    for step in (4, 3, 5, 2, 6, 1, 7):
        pl.semaphore_signal(barrier, inc=1, device_id=src_peer(step), device_id_type=MESH)
    for code, dz in PAIRS:
        for dc in (1, 0):
            if code or dz or dc:
                pl.semaphore_signal(
                    barrier, inc=1, device_id=tgt_peer(code, dz, dc), device_id_type=MESH
                )

    numbered = ((idx, idx_here), (own, own_here), (cnt, cnt_here), (lists, lists_here))
    number_loads = [
        pltpu.make_async_copy(hbm, here, number_sem.at[at])
        for at, (hbm, here) in enumerate(numbered)
    ]
    for load in number_loads:
        load.start()

    arrays = ((pos, wpos), (vel, wvel), (acc, wacc), (jrk, wjrk), (mas, wmas), (ela, wela))
    loads = [
        pltpu.make_async_copy(hbm, win.at[:, HALO : HALO + stars], load_sem.at[at])
        for at, (hbm, win) in enumerate(arrays)
    ]
    for load in loads:
        load.start()
    for load in number_loads:
        load.wait()

    tile = jnp.zeros((ROWS, LANES), jnp.int32)
    for place in range(ACT):
        for at, ref in enumerate((idx_here, own_here, cnt_here)):
            tile = jnp.where((sub == place) & (lane == 16 + at), ref[place], tile)
    s1b[...] = tile
    s1b[0:ACT, 0:16] = lists_here[...]

    pl.semaphore_wait(barrier, SRC + TGT - 2)

    def share(stage, sent, landed):
        for step in (4, 3, 5, 2, 6, 1, 7):
            pltpu.make_async_remote_copy(
                src_ref=sent,
                dst_ref=landed.at[tile_rows(me), :],
                send_sem=src_send.at[stage],
                recv_sem=src_recv.at[stage],
                device_id=src_peer(step),
                device_id_type=MESH,
            ).start()
        return stage, landed

    def wait_bytes(ref, semaphore):
        pltpu.make_async_copy(ref, ref, semaphore).wait()

    def wait_sent(shared):
        stage, landed = shared
        wait_bytes(landed.at[0 : (SRC - 1) * ROWS], src_send.at[stage])

    def wait_landed(shared):
        stage, landed = shared
        wait_bytes(landed.at[0 : (SRC - 1) * ROWS], src_recv.at[stage])

    first = share(0, s1b, s1r)
    s1r[tile_rows(me), :] = s1b[...]

    for load in loads:
        load.wait()

    up = pltpu.make_async_remote_copy(
        src_ref=hsend.at[0],
        dst_ref=hland.at[0],
        send_sem=halo_send.at[0],
        recv_sem=halo_recv.at[0],
        device_id={"src": lax.rem(me + 1, SRC)},
        device_id_type=MESH,
    )
    down = pltpu.make_async_remote_copy(
        src_ref=hsend.at[1],
        dst_ref=hland.at[1],
        send_sem=halo_send.at[1],
        recv_sem=halo_recv.at[1],
        device_id={"src": lax.rem(me + SRC - 1, SRC)},
        device_id_type=MESH,
    )
    row = 0
    for hbm, win in arrays:
        height = win.shape[0]
        hsend[0, row : row + height] = win[:, stars : stars + HALO]
        hsend[1, row : row + height] = win[:, HALO : 2 * HALO]
        row += height

    @pl.when(me < SRC - 1)
    def _():
        up.start()

    @pl.when(me > 0)
    def _():
        down.start()

    @pl.when(me == 0)
    def _():
        hland[0] = jnp.zeros(hland.shape[1:], jnp.float32)

    @pl.when(me == SRC - 1)
    def _():
        hland[1] = jnp.zeros(hland.shape[1:], jnp.float32)

    chunk = 4 * LANES

    def predict_chunk(at, carry):
        there = pl.ds(pl.multiple_of(at * chunk, LANES), chunk)
        (place,), (speed,) = predict(
            [wpos[:, there]], [wvel[:, there]], [wacc[:, there]], [wjrk[:, there]], wela[:, there]
        )
        ppos[:, there] = place
        pvel[:, there] = speed
        return carry

    lax.fori_loop(1, 1 + stars // chunk, predict_chunk, 0)

    def feature_chunk(at, carry):
        there = pl.ds(pl.multiple_of(HALO + at * chunk, LANES), chunk)
        wide = lax.broadcasted_iota(jnp.int32, (ROWS, chunk), 0)
        mass = jnp.broadcast_to(wmas[:, there], (ROWS, chunk))
        rest = jnp.where(wide == 6, mass, 0.0)
        for k in range(3):
            x = jnp.broadcast_to(ppos[k : k + 1, there], (ROWS, chunk))
            v = jnp.broadcast_to(pvel[k : k + 1, there], (ROWS, chunk))
            rest = jnp.where(wide == k, mass * x, jnp.where(wide == 3 + k, mass * v, rest))
        parts = []
        for part in range(3):
            parts.append(rest.astype(jnp.bfloat16).astype(jnp.float32))
            rest = rest - parts[-1]
        parts.append(jnp.zeros((ROWS, chunk), jnp.float32))
        here = pl.ds(pl.multiple_of(at * chunk, LANES), chunk)
        feat[:, here] = jnp.concatenate(parts, 0).astype(jnp.bfloat16)
        return carry

    lax.fori_loop(0, stars // chunk, feature_chunk, 0)

    wait_landed(first)

    numbers = [s1r[pl.ds(place, SRC, stride=ROWS), :] for place in range(ACT)]
    chosen = [[], []]
    before = jnp.zeros((ROWS, LANES), jnp.int32)
    for place in range(ACT):
        mine = lane_of(numbers[place], 17) == me
        for c in range(CAP):
            chosen[c].append(mine & (before == c))
        before = before + jnp.where(mine, 1, 0)

    def pick(c, values, empty):
        result = empty
        for place in range(ACT):
            result = jnp.where(chosen[c][place], values[place], result)
        return result

    izero = jnp.zeros((ROWS, LANES), jnp.int32)
    detail = [pick(c, numbers, izero) for c in range(CAP)]
    first_star = (me * TGT + my_group) * stars
    offset = [lane_of(detail[c], 16) - first_star for c in range(CAP)]
    count = [lane_of(detail[c], 18) for c in range(CAP)]

    def extract(refs):
        wide = sum(ref.shape[0] for ref in refs)

        def step(block, found):
            rows = [
                row_of(ref, row, block + HALO // BLOCK) for ref in refs for row in range(ref.shape[0])
            ]
            out = []
            for c in range(CAP):
                here = lane + block * BLOCK == offset[c]
                out.append([jnp.where(here, row, old) for row, old in zip(rows, found[c])])
            return out

        found = lax.fori_loop(0, blocks, step, [[zero] * wide for _ in range(CAP)], unroll=8)
        return [
            [
                jnp.broadcast_to(jnp.sum(part, axis=1, keepdims=True), (ROWS, LANES))
                for part in found[c]
            ]
            for c in range(CAP)
        ]

    start = extract((ppos, pvel))

    def spread(values, width):
        slots = []
        for c in range(CAP):
            slot = zero
            for k, value in enumerate(values[c]):
                slot = jnp.where(lax.rem(lane, width) == k, value, slot)
            slots.append(slot)
        result = zero
        for place in range(ACT):
            there = lane // width == place
            for c in range(CAP):
                result = jnp.where(there & chosen[c][place], slots[c], result)
        return result

    s2b[...] = spread(start, 8)
    second = share(1, s2b, s2r)
    s2r[tile_rows(me), :] = s2b[...]

    wait_sent(first)
    raw = extract((wpos, wvel, wacc, wjrk, wela))

    def mask_block(block, carry):
        mass = row_of(wmas, 0, block)
        for c in range(CAP):
            listed = jnp.where((detail[c] == block) & (lane < count[c]), 1.0, 0.0)
            member = jnp.broadcast_to(jnp.sum(listed, axis=1, keepdims=True), (ROWS, LANES))
            itself = lane + block * BLOCK == offset[c] + HALO
            mw[block, c] = jnp.where(itself, 0.0, member * mass)
        return carry

    @pl.when(me > 0)
    def _():
        up.wait_recv()

    @pl.when(me < SRC - 1)
    def _():
        down.wait_recv()

    row = 0
    for hbm, win in arrays:
        height = win.shape[0]
        win[:, 0:HALO] = hland[0, row : row + height]
        win[:, HALO + stars :] = hland[1, row : row + height]
        row += height

    lax.fori_loop(0, window_blocks, mask_block, 0, unroll=4)

    def advance_block(block, carry):
        x = [row_of(wpos, k, block) for k in range(3)]
        v = [row_of(wvel, k, block) for k in range(3)]
        a = [row_of(wacc, k, block) for k in range(3)]
        half = [0.5 * row for row in a]
        j = [row_of(wjrk, k, block) for k in range(3)]
        sixth_j = [row / 6.0 for row in j]
        half_j = [0.5 * row for row in j]
        since = row_of(wela, 0, block)
        for number in range(SUBS):
            for c in range(CAP):
                d = since + (0.25 * (number + 1)) * raw[c][12]
                for k in range(3):
                    moved[number, block, c, k] = x[k] + d * (
                        v[k] + d * (half[k] + d * sixth_j[k])
                    )
                    moved[number, block, c, 3 + k] = v[k] + d * (a[k] + d * half_j[k])
        return carry

    lax.fori_loop(0, window_blocks, advance_block, 0)

    def near_field(targets, number):
        def step(block, sums):
            if number is None:
                source = [row_of(ref, k, block) for ref in (ppos, pvel) for k in range(3)]
                sources = [source] * CAP
            else:
                sources = [[moved[number, block, c, k] for k in range(6)] for c in range(CAP)]
            return [pair_sums(sums[c], targets[c], sources[c], mw[block, c]) for c in range(CAP)]

        sums = lax.fori_loop(0, window_blocks, step, [[zero] * 9 for _ in range(CAP)], unroll=True)
        return [total_of(sums[c]) for c in range(CAP)]

    predict_chunk(0, 0)
    predict_chunk(window_blocks * LANES // chunk - 1, 0)
    inner = near_field(start, None)

    wait_landed(second)

    def gathered(ref):
        total = ref[0:ROWS, :]
        for at in range(1, SRC):
            total = total + ref[at * ROWS : (at + 1) * ROWS, :]
        return total

    group_targets = gathered(s2r)
    s3b[...] = group_targets
    s3r[0] = group_targets
    for code, dz in PAIRS:
        for dc in (1, 0):
            if code or dz or dc:
                pltpu.make_async_remote_copy(
                    src_ref=s3b,
                    dst_ref=s3r.at[code * 4 + dz * 2 + dc],
                    send_sem=tgt_send,
                    recv_sem=tgt_recv.at[code * 2 + dz],
                    device_id=tgt_peer(code, dz, dc),
                    device_id_type=MESH,
                ).start()

    def field(tiles):
        many = len(tiles)
        aims = [
            jnp.concatenate(
                [lane_of(tile, place * 8 + k) for tile in tiles for place in range(ACT)], 0
            )
            for k in range(6)
        ]

        def halves(value):
            high = value.astype(jnp.bfloat16)
            return high, (value - high.astype(jnp.float32)).astype(jnp.bfloat16)

        def step(at, sums):
            columns = []
            for piece in range(PIECES):
                block = at * PIECES + piece
                rows = [wide_row(ppos, k, block + HALO // BLOCK, many) for k in range(3)]
                rows += [wide_row(pvel, k, block + HALO // BLOCK, many) for k in range(3)]
                u = [rows[k] - aims[k] for k in range(3)]
                e = [rows[3 + k] - aims[3 + k] for k in range(3)]
                inverse = lax.rsqrt(u[0] * u[0] + u[1] * u[1] + (u[2] * u[2] + SOFTENING))
                square = inverse * inverse
                weight = inverse * square
                radial = weight * ((u[0] * e[0] + u[1] * e[1] + u[2] * e[2]) * square)
                columns.append(jnp.concatenate(halves(weight) + halves(radial), 0))
            left = jnp.concatenate(columns, 1)
            right = feat[:, pl.ds(pl.multiple_of(at * PIECES * LANES, LANES), PIECES * LANES)]
            return sums + lax.dot_general(
                left, right, (((1,), (1,)), ((), ())), preferred_element_type=jnp.float32
            )

        sums = lax.fori_loop(
            0,
            blocks // PIECES,
            step,
            jnp.zeros((4 * many * ACT * ROWS, 4 * ROWS), jnp.float32),
            unroll=UNROLL,
        )
        blank = jnp.zeros((4 * many * ACT * ROWS, LANES - 4 * ROWS), jnp.float32)
        sums = jnp.concatenate([sums, blank], 1)
        results = []
        for at in range(many):
            for array in range(2):
                tile = zero
                for place in range(ACT):
                    row = ((2 * array * many + at) * ACT + place) * ROWS
                    both = sums[row : row + ROWS] + sums[row + many * ACT * ROWS :][0:ROWS]
                    tile = tile + (pltpu.roll(both, 32 * place, 1) if place else both)
                results.append(tile)
        return results

    def send_sum(at, code, dz, dc):
        pltpu.make_async_remote_copy(
            src_ref=s4b.at[at],
            dst_ref=s4r.at[at],
            send_sem=sum_send,
            recv_sem=sum_recv,
            device_id=tgt_peer(code, dz, dc),
            device_id_type=MESH,
        ).start()

    def group_pair(pair, tables):
        code, dz = lax.rem(tables[0], 4), lax.rem(tables[1], 2)
        other = code + dz > 0
        places = [code * 4 + dz * 2 + dc for dc in (0, 1)]

        @pl.when(other)
        def _():
            wait_bytes(s3r.at[pl.ds(0, 2)], tgt_recv.at[code * 2 + dz])

        @pl.when(jnp.logical_not(other))
        def _():
            wait_bytes(s3r.at[0], tgt_recv.at[code * 2 + dz])

        results = field([s3r[place] for place in places])
        for dc in (1, 0):
            for array in range(2):
                s4b[places[dc], array] = results[2 * dc + array]
        send_sum(places[1], code, dz, 1)

        @pl.when(other)
        def _():
            send_sum(places[0], code, dz, 0)

        @pl.when(jnp.logical_not(other))
        def _():
            for array in range(2):
                s4r[0, array] = results[array]

        return [lax.div(tables[0], 4), lax.div(tables[1], 2)]

    tables = [low + my_z * (high - low) for low, high in (CODE_TABLES, DZ_TABLES)]
    lax.fori_loop(0, len(PAIRS), group_pair, tables)

    aim = group_targets
    for place in range(1, ACT):
        aim = jnp.where(lane // 32 == place, pltpu.roll(group_targets, 24 * place, 1), aim)
    wait_bytes(s4r.at[pl.ds(0, TGT - 1)], sum_recv)
    sides = []
    for array in range(2):
        both = s4r[0, array]
        for at in range(1, TGT):
            both = both + s4r[at, array]
        both = both + pltpu.roll(both, LANES - 8, 1) + pltpu.roll(both, LANES - 16, 1)
        ones = lane_of(both, 6)
        for place in range(1, ACT):
            ones = jnp.where(lane // 32 == place, lane_of(both, 32 * place + 6), ones)
        sides.append(both - aim * ones)
    group_sum = jnp.where(
        lax.rem(lane, 32) < 3, sides[0], sides[0] - 3.0 * pltpu.roll(sides[1], 3, 1)
    )

    s5b[...] = group_sum
    fifth = share(2, s5b, s5r)
    s5r[tile_rows(me), :] = group_sum
    wait_sent(second)
    wait_bytes(s3r.at[pl.ds(0, TGT - 1)], tgt_send)
    wait_bytes(s4r.at[pl.ds(0, TGT - 1)], sum_send)

    @pl.when(me < SRC - 1)
    def _():
        up.wait_send()

    @pl.when(me > 0)
    def _():
        down.wait_send()

    wait_sent(fifth)
    wait_landed(fifth)
    summed = gathered(s5r)
    lanes_of = [[lane_of(summed, place * 32 + k) for place in range(ACT)] for k in range(6)]

    totals = [[pick(c, lanes_of[k], zero) for k in range(6)] for c in range(CAP)]
    states = []
    for c in range(CAP):
        interval = raw[c][12]
        old_pull, old_change = raw[c][6:9], raw[c][9:12]
        regular = [totals[c][k] - inner[c][k] for k in range(6)]
        x, v, snap, crackle = correct(
            start[c][0:3],
            start[c][3:6],
            old_pull,
            old_change,
            totals[c][0:3],
            totals[c][3:6],
            interval,
        )
        states.append((x, v, totals[c][0:3], totals[c][3:6], 0.25 * interval, regular, snap + crackle))
    for number in range(SUBS):
        advance = [states[c][4] * (number + 1) for c in range(CAP)]
        guesses = [predict(*states[c][0:5]) for c in range(CAP)]
        inner = near_field([x + v for x, v in guesses], number)
        after = []
        for c in range(CAP):
            x, v, pull, change, substep, regular, rest = states[c]
            new_pull = [
                regular[k] + advance[c] * regular[3 + k] + inner[c][k] for k in range(3)
            ]
            new_change = [regular[3 + k] + inner[c][3 + k] for k in range(3)]
            x, v, unused, ignored = correct(
                guesses[c][0], guesses[c][1], pull, change, new_pull, new_change, substep
            )
            after.append((x, v, new_pull, new_change, substep, regular, rest))
        states = after

    results = [
        states[c][0] + states[c][1] + states[c][5] + inner[c] + states[c][6] for c in range(CAP)
    ]
    s6b[...] = spread(results, 32)
    sixth = share(3, s6b, s6r)
    s6r[tile_rows(me), :] = s6b[...]
    wait_landed(sixth)
    mine = jnp.sum(s6r[pl.ds(me, SRC, stride=ROWS), :], axis=0, keepdims=True)
    mine = jnp.broadcast_to(mine, (ROWS, LANES))
    shifted = mine
    for place in range(1, ACT):
        shifted = jnp.where(sub == place, pltpu.roll(mine, LANES - 32 * place, 1), shifted)
    o_all[...] = shifted[0:ACT, :]

    wait_sent(sixth)


def cut(result, state, fields, taylor):
    state[...] = result[:, 0:6]
    fields[...] = result[:, 6:18]
    taylor[...] = result[:, 18:24]


def shards(
    positions,
    velocities,
    accelerations,
    jerk_terms,
    masses,
    elapsed,
    active_idx,
    owners,
    counts,
    block_lists,
):
    stars = positions.shape[1]
    window = stars + 2 * HALO
    hbm = pl.BlockSpec(memory_space=pl.ANY)
    vmem = pl.BlockSpec(memory_space=pltpu.VMEM)
    tile = pltpu.VMEM((ROWS, LANES), jnp.float32)
    landed = pltpu.VMEM((SRC * ROWS, LANES), jnp.float32)
    groups = pltpu.VMEM((TGT, ROWS, LANES), jnp.float32)
    sums = pltpu.VMEM((TGT, 2, ROWS, LANES), jnp.float32)
    itile = pltpu.VMEM((ROWS, LANES), jnp.int32)
    ilanded = pltpu.VMEM((SRC * ROWS, LANES), jnp.int32)
    three = pltpu.VMEM((3, window), jnp.float32)
    one = pltpu.VMEM((1, window), jnp.float32)
    dma = pltpu.SemaphoreType.DMA
    result = pl.pallas_call(
        kernel,
        out_shape=pltpu.VMEM((ACT, LANES), jnp.float32),
        in_specs=[hbm] * 10,
        out_specs=vmem,
        scratch_shapes=[
            three, three, three, three, one, one, three, three,
            pltpu.VMEM((4 * ROWS, stars), jnp.bfloat16),
            pltpu.VMEM((window // BLOCK, CAP, ROWS, LANES), jnp.float32),
            pltpu.VMEM((SUBS, window // BLOCK, CAP, 6, ROWS, LANES), jnp.float32),
            itile, ilanded, tile, landed, tile, groups, sums, sums, tile, landed, tile, landed,
            pltpu.VMEM((2, 14, HALO), jnp.float32), pltpu.VMEM((2, 14, HALO), jnp.float32),
            pltpu.SMEM((ACT,), jnp.int32), pltpu.SMEM((ACT,), jnp.int32), pltpu.SMEM((ACT,), jnp.int32),
            pltpu.VMEM((ACT, 16), jnp.int32),
            dma((6,)), dma((4,)), dma((2,)), dma((2,)), dma((4,)), dma((4,)),
            dma, dma((len(PAIRS),)), dma, dma,
        ],
        compiler_params=pltpu.CompilerParams(collective_id=0, has_side_effects=True),
    )(
        positions,
        velocities,
        accelerations,
        jerk_terms,
        masses[None],
        elapsed[None],
        active_idx,
        owners,
        counts,
        block_lists,
    )
    state, fields, taylor = pl.pallas_call(
        cut,
        out_shape=(
            jax.ShapeDtypeStruct((ACT, 6), jnp.float32),
            jax.ShapeDtypeStruct((ACT, 12), jnp.float32),
            jax.ShapeDtypeStruct((ACT, 6), jnp.float32),
        ),
        in_specs=[vmem],
        out_specs=(vmem, vmem, vmem),
    )(pltpu.with_memory_space_constraint(result, pltpu.VMEM))
    return state.T, fields.T, taylor.T


def solution(mesh):
    in_specs = (
        P(None, ("src", "tgt")),
        P(None, ("src", "tgt")),
        P(None, ("src", "tgt")),
        P(None, ("src", "tgt")),
        P(("src", "tgt")),
        P(("src", "tgt")),
        P(("src", "tgt")),
        P(("src", "tgt")),
        P(("src", "tgt")),
        P(("src", "tgt"), None),
    )
    out_specs = (P(None, ("src", "tgt")), P(None, ("src", "tgt")), P(None, ("src", "tgt")))
    return jax.shard_map(shards, mesh=mesh, in_specs=in_specs, out_specs=out_specs, check_vma=False)
```
